32 devices in a mesh: shards: 2 (over y), context: 4 (over x, core), tensor: 4 (over z).
Axes of the slice: x: 2, y: 2, z: 4, core: 2. Of those that a mesh axis runs over, the one named last changes fastest.
Arguments:
- tokens: bfloat16 [10240, 768], P(('shards', 'context')), may hold values from -6 to 6
- parents: int32 [2, 13], P('shards'), may hold values from -1 to 4, as said below
- norm1_gain: float32 [768], replicated, may hold values from 0.5 to 1.5
- norm1_bias: float32 [768], replicated, may hold values from -1.25 to 1.25
- in_weight: bfloat16 [768, 3, 768], P('shards', None, 'tensor'), may hold values from -0.21875 to 0.21875
- in_bias: float32 [3, 768], P(None, 'tensor'), may hold values from -1.25 to 1.25
- conv_weight: float32 [3, 3, 768], P(None, None, 'tensor'), may hold values from -3.5 to 3.5
- conv_bias: float32 [3, 768], P(None, 'tensor'), may hold values from -1.25 to 1.25
- filt_in: float32 [33, 64], replicated, may hold values from -1 to 1
- filt_bias1: float32 [64], replicated, may hold values from -6 to 6
- filt_mid: float32 [64, 64], replicated, may hold values from -0.75 to 0.75
- filt_bias2: float32 [64], replicated, may hold values from -3 to 3
- sine_freq: float32 [64], replicated, may hold values from 8 to 12
- filt_out: bfloat16 [64, 768], P('shards', 'tensor'), may hold values from -0.09375 to 0.09375
- skip_gain: float32 [768], P('tensor'), may hold values from -6 to 6
- out_weight: bfloat16 [768, 768], P('tensor', 'shards'), may hold values from -0.21875 to 0.21875
- out_bias: float32 [768], replicated, may hold values from -1.25 to 1.25
- norm2_gain: float32 [768], replicated, may hold values from 0.5 to 1.5
- norm2_bias: float32 [768], replicated, may hold values from -1.25 to 1.25
- up_weight: bfloat16 [768, 3072], P('shards', 'tensor'), may hold values from -0.21875 to 0.21875
- up_bias: float32 [3072], P('tensor'), may hold values from -1.25 to 1.25
- down_weight: bfloat16 [3072, 768], P('tensor', 'shards'), may hold values from -0.109375 to 0.109375
- down_bias: float32 [768], replicated, may hold values from -1.25 to 1.25
- cotangent: bfloat16 [10240, 768], P(('shards', 'context')), may hold values from -6 to 6
Outputs:
- layer_out: bfloat16 [10240, 768], P(('shards', 'context', 'tensor'))
- tokens_grad: bfloat16 [10240, 768], P(('shards', 'context', 'tensor'))
- norm1_gain_grad: float32 [768], replicated
- norm1_bias_grad: float32 [768], replicated
- in_weight_grad: float32 [768, 3, 768], P('shards', None, 'tensor')
- in_bias_grad: float32 [3, 768], P(None, 'tensor')
- conv_weight_grad: float32 [3, 3, 768], P(None, None, 'tensor')
- conv_bias_grad: float32 [3, 768], P(None, 'tensor')
- filt_in_grad: float32 [33, 64], replicated
- filt_bias1_grad: float32 [64], replicated
- filt_mid_grad: float32 [64, 64], replicated
- filt_bias2_grad: float32 [64], replicated
- sine_freq_grad: float32 [64], replicated
- filt_out_grad: float32 [64, 768], P('shards', 'tensor')
- skip_grad: float32 [768], P('tensor')
- out_weight_grad: float32 [768, 768], P('tensor', 'shards')
- out_bias_grad: float32 [768], replicated
- norm2_gain_grad: float32 [768], replicated
- norm2_bias_grad: float32 [768], replicated
- up_weight_grad: float32 [768, 3072], P('shards', 'tensor')
- up_bias_grad: float32 [3072], P('tensor')
- down_weight_grad: float32 [3072, 768], P('tensor', 'shards')
- down_bias_grad: float32 [768], replicated
The draws below stay inside these ranges and needn't reach their ends.
Inputs may be any that keep to these rules, and one draw needn't show every extreme that they name: parents[t, 0] = -1 marks the trunk; segments 1 to 4 are branches with parent 0; the other 8 segments are leaves whose parent is one of the branches 1 to 4; every tree has a leaf under branch 4.
All inputs are finite; a program needn't handle non-finite values.
Results may differ from the reference program's by a relative error of at most 0.011.
Values may be sent and summed in bfloat16 or wider, within the bound.
No kernel may reach another device: no remote copies, remote signals or barrier semaphores. Data moves between devices by JAX's collectives and lax.ppermute only.
A program may use at most 384 MiB of HBM per device.

```python
import math
import jax
import jax.numpy as jnp
from jax import lax

D = 768
FF = 3072
FILT = 64
EMB = 33
BLOCK = 256
TRUNK_BLK = 8
BRANCHES = 4
LEAVES = 8
NPATH = 10
PATH = 2560
TREE_TOK = 5120
TREES = 2
TOKENS = 10240


def draw_parents(key, part):
    leaf_key, pick_key = jax.random.split(jax.random.fold_in(key, 17))
    leaf_parents = jax.random.randint(leaf_key, (TREES, LEAVES), 1, BRANCHES + 1)
    chosen = jax.random.randint(pick_key, (TREES, 1), 0, LEAVES)
    leaf_parents = jnp.where(jnp.arange(LEAVES)[None, :] == chosen, BRANCHES, leaf_parents)
    trunk_column = jnp.full((TREES, 1), -1, dtype=jnp.int32)
    branch_columns = jnp.zeros((TREES, BRANCHES), dtype=jnp.int32)
    return jnp.concatenate([trunk_column, branch_columns, leaf_parents.astype(jnp.int32)], axis=1).astype(jnp.int32)


def draw_filt_in(key, part):
    size_key, sign_key = jax.random.split(jax.random.fold_in(key, 29))
    magnitude = jax.random.uniform(size_key, (EMB, FILT), jnp.float32, 0.5, 1.0)
    flips = jax.random.uniform(sign_key, (EMB, FILT), jnp.float32, 0.0, 1.0)
    signs = jnp.where(flips < 0.5, -1.0, 1.0).astype(jnp.float32)
    return (magnitude * signs).astype(jnp.float32)


def steps_of(key, extent, pieces, least, top_value):
    factor_of, own = 1.0, jax.random.fold_in(key, 6)
    for dim, shards_of in pieces:
        draws = jnp.exp(jax.random.uniform(jax.random.fold_in(own, dim), (shards_of,), jnp.float32, least / len(pieces), top_value / len(pieces)))
        factor_of = factor_of * jnp.repeat(draws, extent[dim] // shards_of).reshape([-1 if axis == dim else 1 for axis in range(len(extent))])
    return factor_of


def normal_values(key, shape, deviation, most, cuts=(), kind=jnp.bfloat16):
    array = jax.random.normal(key, shape, jnp.float32) * deviation
    if len(cuts) > 0:
        array = steps_of(key, shape, cuts, -0.22, 0.18) * array
    return jnp.clip(array, min=-most, max=most).astype(kind)


def setup_inputs(seed: int = 0) -> dict:
    key_of = jax.random.split(jax.random.key(seed), 25)
    tokens = normal_values(key_of[0], (TOKENS, D), 1.0, 6.0, ((0, 8),))
    parents = draw_parents(jax.random.fold_in(key_of[24], 71), 0)
    norm1_gain = jnp.clip(1.0 + 0.1 * jax.random.normal(key_of[2], (D,), jnp.float32), 0.5, 1.5)
    norm1_bias = normal_values(key_of[3], (D,), 0.2, 1.25, (), jnp.float32)
    in_weight = normal_values(key_of[4], (D, 3, D), D ** -0.5, 0.21875, ((0, 2), (2, 4)))
    in_bias = normal_values(key_of[5], (3, D), 0.2, 1.25, ((1, 4),), jnp.float32)
    conv_weight = normal_values(key_of[6], (3, 3, D), 0.6, 3.5, ((2, 4),), jnp.float32)
    conv_bias = normal_values(key_of[7], (3, D), 0.2, 1.25, ((1, 4),), jnp.float32)
    filt_in = draw_filt_in(jax.random.fold_in(key_of[24], 71), 0)
    filt_bias1 = normal_values(key_of[9], (FILT,), 1.0, 6.0, (), jnp.float32)
    filt_mid = normal_values(key_of[10], (FILT, FILT), FILT ** -0.5, 0.75, (), jnp.float32)
    filt_bias2 = normal_values(key_of[11], (FILT,), 0.5, 3.0, (), jnp.float32)
    sine_freq = jnp.clip(jax.random.uniform(key_of[12], (FILT,), jnp.float32, 8.0, 12.0), 8.0, 12.0)
    filt_out = normal_values(key_of[13], (FILT, D), (FILT * FILT) ** -0.5, 0.09375, ((0, 2), (1, 4)))
    skip_gain = normal_values(key_of[14], (D,), 1.0, 6.0, ((0, 4),), jnp.float32)
    out_weight = normal_values(key_of[15], (D, D), D ** -0.5, 0.21875, ((0, 4), (1, 2)))
    out_bias = normal_values(key_of[16], (D,), 0.2, 1.25, (), jnp.float32)
    norm2_gain = jnp.clip(1.0 + 0.1 * jax.random.normal(key_of[17], (D,), jnp.float32), 0.5, 1.5)
    norm2_bias = normal_values(key_of[18], (D,), 0.2, 1.25, (), jnp.float32)
    up_weight = normal_values(key_of[19], (D, FF), D ** -0.5, 0.21875, ((0, 2), (1, 4)))
    up_bias = normal_values(key_of[20], (FF,), 0.2, 1.25, ((0, 4),), jnp.float32)
    down_weight = normal_values(key_of[21], (FF, D), FF ** -0.5, 0.109375, ((0, 4), (1, 2)))
    down_bias = normal_values(key_of[22], (D,), 0.2, 1.25, (), jnp.float32)
    cotangent = normal_values(key_of[23], (TOKENS, D), 1.0, 6.0, ((0, 8),))
    return {"tokens": tokens, "parents": parents, "norm1_gain": norm1_gain, "norm1_bias": norm1_bias, "in_weight": in_weight, "in_bias": in_bias, "conv_weight": conv_weight, "conv_bias": conv_bias, "filt_in": filt_in, "filt_bias1": filt_bias1, "filt_mid": filt_mid, "filt_bias2": filt_bias2, "sine_freq": sine_freq, "filt_out": filt_out, "skip_gain": skip_gain, "out_weight": out_weight, "out_bias": out_bias, "norm2_gain": norm2_gain, "norm2_bias": norm2_bias, "up_weight": up_weight, "up_bias": up_bias, "down_weight": down_weight, "down_bias": down_bias, "cotangent": cotangent}


@jax.custom_vjp
def low(v):
    return lax.optimization_barrier(v.astype(jnp.bfloat16)).astype(jnp.float32)

@jax.custom_vjp
def low_back(v):
    return v

def low_keep(v):
    return (low(v), None)

def low_pass(kept, grad):
    return (grad,)

def back_keep(v):
    return (v, None)

def back_low(kept, grad):
    return (low(grad),)
low.defvjp(low_keep, low_pass)
low_back.defvjp(back_keep, back_low)
exact_mode = lax.Precision.HIGHEST

def layer_norm(values, scale_vec, shift_vec):
    average = lax.optimization_barrier(jnp.mean(values, axis=-1, keepdims=True))
    centred = values - average
    variance = lax.optimization_barrier(jnp.mean(centred * centred, axis=-1, keepdims=True))
    return centred * lax.rsqrt(variance + 1e-05) * scale_vec + shift_vec

def block_tables(tree_parents, trunk_blocks, path_blocks):
    block_count = trunk_blocks + tree_parents.shape[0] - 1
    block_index = jnp.arange(block_count, dtype=jnp.int32)
    segment = jnp.where(block_index < trunk_blocks, 0, block_index - trunk_blocks + 1).astype(jnp.int32)
    owner_seg = tree_parents[segment]
    last_block = jnp.where(owner_seg == 0, trunk_blocks - 1, trunk_blocks + owner_seg - 1)
    parent_block = jnp.where(block_index < trunk_blocks, block_index - 1, jnp.where(owner_seg < 0, -1, last_block)).astype(jnp.int32)
    columns = [block_index]
    for level_index in range(path_blocks - 1):
        current = columns[-1]
        columns.append(jnp.where(current >= 0, parent_block[jnp.maximum(current, 0)], -1).astype(jnp.int32))
    return (parent_block, jnp.stack(columns, axis=1))

def filter_taps(filt_in, filt_bias1, filt_mid, filt_bias2, sine_freq, filt_out, first_channel, total_channels):
    positions = jnp.arange(PATH, dtype=jnp.float32)
    band_count = (filt_in.shape[0] - 1) // 2
    ramp_values = positions / (PATH - 1)
    base_angle = 2.0 * math.pi * positions / PATH
    band_freq = 0.0001 + (band_count - 1 - 0.0001) * jnp.arange(band_count, dtype=jnp.float32) / max(band_count - 1, 1)
    phase_grid = base_angle[:, None] * band_freq[None, :]
    embedded = jnp.concatenate([ramp_values[:, None], jnp.cos(phase_grid), -jnp.sin(phase_grid)], axis=1)
    hidden_one = jnp.sin(sine_freq * (jnp.dot(embedded, filt_in, precision=exact_mode) + filt_bias1))
    hidden_two = jnp.sin(sine_freq * (jnp.dot(hidden_one, filt_mid, precision=exact_mode) + filt_bias2))
    raw_taps = jnp.dot(hidden_two, filt_out, precision=exact_mode)
    channel = jnp.arange(filt_out.shape[1], dtype=jnp.float32) + first_channel
    slow_rate = math.log(0.01) / 1.5
    fast_rate = math.log(0.01) / 0.3
    decay_rates = jnp.abs(slow_rate + (fast_rate - slow_rate) * channel / (total_channels - 1))
    return raw_taps * (jnp.exp(-ramp_values[:, None] * decay_rates[None, :]) + 0.05)

def tree_layer(tree_tokens, tree_parents, weights):
    norm1_gain, norm1_bias, in_weight, in_bias, conv_weight, conv_bias, filt_in, filt_bias1, filt_mid, filt_bias2, sine_freq, filt_out, skip_gain, out_weight, out_bias, norm2_gain, norm2_bias, up_weight, up_bias, down_weight, down_bias = weights
    width = tree_tokens.shape[1]
    normed = low(layer_norm(tree_tokens, norm1_gain, norm1_bias))
    projected = jnp.dot(normed, in_weight.reshape(width, 3 * width), precision=exact_mode) + in_bias.reshape(-1)
    projected = low_back(low(projected))
    blocks = projected.reshape(-1, BLOCK, 3 * width)
    parent_block, ancestors = block_tables(tree_parents, TRUNK_BLK, NPATH)
    has_parent = (parent_block >= 0).astype(jnp.float32)
    previous = blocks[jnp.maximum(parent_block, 0), BLOCK - 2:, :] * has_parent[:, None, None]
    extended = jnp.concatenate([previous, blocks], axis=1)
    short_taps = conv_weight.reshape(3, 3 * width)
    short_out = conv_bias.reshape(-1) + short_taps[0] * extended[:, 2:] + short_taps[1] * extended[:, 1:-1] + short_taps[2] * extended[:, :-2]
    gate_out = short_out[:, :, :width]
    gate_in = short_out[:, :, width:2 * width]
    value_part = short_out[:, :, 2 * width:]
    product_in = low(value_part * gate_in)
    taps_long = filter_taps(filt_in, filt_bias1, filt_mid, filt_bias2, sine_freq, filt_out, 0, width)
    spectrum = jnp.fft.rfft(taps_long, n=2 * PATH, axis=0)

    def one_block(block_id):
        chain_ids = ancestors[block_id][::-1]
        present = (chain_ids >= 0).astype(jnp.float32)
        sequence = (product_in[jnp.maximum(chain_ids, 0)] * present[:, None, None]).reshape(PATH, width)
        convolved = jnp.fft.irfft(jnp.fft.rfft(sequence, n=2 * PATH, axis=0) * spectrum, n=2 * PATH, axis=0)
        return convolved[PATH - BLOCK:PATH]
    long_out = lax.map(jax.checkpoint(one_block), jnp.arange(blocks.shape[0], dtype=jnp.int32))
    conv_out = long_out + skip_gain * product_in
    gated_low = low(gate_out * conv_out).reshape(-1, width)
    mixer_out = low_back(jnp.dot(gated_low, out_weight, precision=exact_mode) + out_bias)
    residual = tree_tokens + mixer_out
    normed_two = low(layer_norm(residual, norm2_gain, norm2_bias))
    pre_act = low_back(jnp.dot(normed_two, up_weight, precision=exact_mode) + up_bias)
    activated = low(jax.nn.gelu(pre_act, approximate=True))
    return residual + jnp.dot(activated, down_weight, precision=exact_mode) + down_bias

def reference(tokens, parents, norm1_gain, norm1_bias, in_weight, in_bias, conv_weight, conv_bias, filt_in, filt_bias1, filt_mid, filt_bias2, sine_freq, filt_out, skip_gain, out_weight, out_bias, norm2_gain, norm2_bias, up_weight, up_bias, down_weight, down_bias, cotangent):
    weights = tuple((weight.astype(jnp.float32) for weight in (norm1_gain, norm1_bias, in_weight, in_bias, conv_weight, conv_bias, filt_in, filt_bias1, filt_mid, filt_bias2, sine_freq, filt_out, skip_gain, out_weight, out_bias, norm2_gain, norm2_bias, up_weight, up_bias, down_weight, down_bias)))

    def forward(token_values, *weight_values):
        tree_values = token_values.reshape(-1, TREE_TOK, token_values.shape[1])

        def one_tree(tree_pair):
            return tree_layer(tree_pair[0], tree_pair[1], weight_values)
        outputs = lax.map(jax.checkpoint(one_tree), (tree_values, parents))
        return outputs.reshape(token_values.shape)
    out_values, backward = jax.vjp(forward, tokens.astype(jnp.float32), *weights)
    gradients = backward(cotangent.astype(jnp.float32))
    return (out_values.astype(jnp.bfloat16), gradients[0].astype(jnp.bfloat16), gradients[1], gradients[2], gradients[3], gradients[4], gradients[5], gradients[6], gradients[7], gradients[8], gradients[9], gradients[10], gradients[11], gradients[12], gradients[13], gradients[14], gradients[15], gradients[16], gradients[17], gradients[18], gradients[19], gradients[20], gradients[21])
```

```python
import functools
import math

import jax
import jax.numpy as jnp
import ml_dtypes
import numpy as np
from jax import lax
from jax.experimental import pallas as pl
from jax.experimental.pallas import tpu as pltpu
from jax.sharding import PartitionSpec as P

BLOCK = 256
TRUNK = 8
NPATH = 10
PATH = 2560
BRANCHES = 4
LEAVES = 8
TREE_BLK = 20
WAYS = 4

f32 = jnp.float32
bf16 = jnp.bfloat16
exact_mode = lax.Precision.HIGHEST
GELU_A = math.sqrt(2.0 / math.pi)
GELU_B = 0.044715


def split_np(a):
    hi = a.astype(ml_dtypes.bfloat16)
    lo = (a - hi.astype(np.float64)).astype(ml_dtypes.bfloat16)
    return hi, lo


def dft_tables():
    k = np.arange(BLOCK)[None, :]
    n = np.arange(BLOCK)[:, None]
    ang = np.pi * ((2 * k + 1) * n % 1024) / 512.0
    fwd = np.concatenate([np.cos(ang), -np.sin(ang)], axis=1)
    m = BLOCK + np.arange(BLOCK)[None, :]
    kk = np.arange(BLOCK)[:, None]
    ang2 = np.pi * ((2 * kk + 1) * m % 1024) / 512.0
    inv = np.concatenate([np.cos(ang2), -np.sin(ang2)], axis=0) / 256.0
    return split_np(fwd) + split_np(inv)


def embed_table(bands):
    pos = np.arange(PATH, dtype=np.float64)
    base = 2.0 * np.pi * pos / PATH
    freq = 0.0001 + (bands - 1 - 0.0001) * np.arange(bands) / max(bands - 1, 1)
    phase = freq[:, None] * base[None, :]
    return np.concatenate([pos[None] / (PATH - 1), np.cos(phase), -np.sin(phase)]).astype(np.float32)


def swap(x, axis, k):
    return lax.ppermute(x, axis, [(i, i ^ k) for i in range(WAYS)])


def vmem_specs(n):
    return [pl.BlockSpec(memory_space=pltpu.VMEM) for _ in range(n)]


def smem_spec():
    return pl.BlockSpec(memory_space=pltpu.SMEM)


def call(kernel, outs, n_vmem, scratch=(), limit=48):
    return pl.pallas_call(
        kernel,
        out_shape=[jax.ShapeDtypeStruct(s, d) for s, d in outs],
        in_specs=[smem_spec()] + vmem_specs(n_vmem),
        out_specs=vmem_specs(len(outs)),
        scratch_shapes=list(scratch),
        compiler_params=pltpu.CompilerParams(vmem_limit_bytes=limit << 20),
    )


def nt(a, b):
    return lax.dot_general(a, b, (((1,), (1,)), ((), ())), preferred_element_type=f32)


def nn(a, b):
    return lax.dot_general(a, b, (((1,), (0,)), ((), ())), preferred_element_type=f32)


def tn(a, b):
    return lax.dot_general(a, b, (((0,), (0,)), ((), ())), preferred_element_type=f32)


def two(a):
    hi = a.astype(bf16)
    return hi, (a - hi.astype(f32)).astype(bf16)


def norm_parts(x):
    mu = jnp.mean(x, axis=-1, keepdims=True)
    xc = x - mu
    rs = lax.rsqrt(jnp.mean(xc * xc, axis=-1, keepdims=True) + 1e-05)
    return xc * rs, rs


def norm_back(nh, rs, dnh):
    m1 = jnp.mean(dnh, axis=-1, keepdims=True)
    m2 = jnp.mean(dnh * nh, axis=-1, keepdims=True)
    return rs * (dnh - m1 - nh * m2)


def share_tiles(t):
    return [((0, 1), 2), ((3, 4), 2), ((5, 6), 7), ((8, 9), 7)][t]


def pack_share(tiles, t, ch, store):
    (a, b), c = share_tiles(t)
    store(0, tiles(a))
    store(ch, tiles(b))
    x = tiles(c)
    low = lax.broadcasted_iota(jnp.int32, (ch // 2, 128), 1) < 64
    top, bot = x[: ch // 2], x[ch // 2 :]
    if t % 2 == 0:
        y = jnp.where(low, top, pltpu.roll(bot, 64, 1))
    else:
        y = jnp.where(low, pltpu.roll(top, 64, 1), bot)
    store(2 * ch, y)


def left_rows(piece, ch):
    x = piece[2 * ch :].astype(f32)
    return jnp.concatenate([x, pltpu.roll(x, 64, 1)], axis=0)


def share_offsets(t):
    odd = t % 2
    return (64 * odd, 64 * odd + 128, 256 * (1 - odd))


def proj_kernel(sc, tok, rim, wt, cols, nv, a1o, zo, zro, so, uo, u0, u1, u2, u3, us):
    b = pl.program_id(0)
    c = sc[1]
    gain, shift = nv[0:1], nv[1:2]
    nh, _ = norm_parts(tok[...].astype(f32))
    a1 = (nh * gain + shift).astype(bf16)
    a1o[...] = a1
    nhr, _ = norm_parts(rim[0].astype(f32))
    a1r = (nhr * gain + shift).astype(bf16)
    a1r = jnp.concatenate([a1r, jnp.zeros((14, a1r.shape[1]), bf16)], axis=0)
    has = jnp.where(sc[3 + b] >= 0, 1.0, 0.0)
    cv = cols[...]
    w0, w1, w2, cb, ib = (cv[:, i : i + 1] for i in range(5))
    w = wt[...]
    zb = (nt(w, a1) + ib).astype(bf16)
    zo[0] = zb
    z = zb.astype(f32)
    zr = (nt(w, a1r) + ib).astype(bf16).astype(f32) * has
    zro[0] = zr
    lane = lax.broadcasted_iota(jnp.int32, z.shape, 1)
    far, near = zr[:, 0:1], zr[:, 1:2]
    z1 = jnp.where(lane == 0, near, pltpu.roll(z, 1, 1))
    z2 = jnp.where(lane == 0, far, jnp.where(lane == 1, near, pltpu.roll(z, 2, 1)))
    s = cb + w0 * z + w1 * z1 + w2 * z2
    so[0] = s
    ch = s.shape[0] // 3
    u = (s[2 * ch :] * s[ch : 2 * ch]).astype(bf16)
    uo[0] = u
    us[...] = u
    cs = ch // WAYS
    for k, o in enumerate((u0, u1, u2, u3)):
        o[0] = us[pl.ds(pl.multiple_of((c ^ k) * cs, 16), cs), :]


def leaf_parent(sc, i):
    return TRUNK - 1 + sc[8 + 1 + BRANCHES + i]


def signs():
    lane = lax.broadcasted_iota(jnp.int32, (1, BLOCK), 1)
    return (1 - 2 * (lane % 2)).astype(f32)


def mul(acc, h, w):
    hr, hi = h[:, :BLOCK], h[:, BLOCK:]
    wr, wi = w[:, :BLOCK], w[:, BLOCK:]
    return acc[0] + (hr * wr - hi * wi), acc[1] + (hr * wi + hi * wr)


def mul_conj(acc, h, w):
    hr, hi = h[:, :BLOCK], h[:, BLOCK:]
    wr, wi = w[:, :BLOCK], w[:, BLOCK:]
    return acc[0] + (hr * wr + hi * wi), acc[1] + (hr * wi - hi * wr)


def conv_kernel(sc, u0, u1, u2, u3, taps, fh, fl, gh, gl, wo, ho, y0, y1, y2, y3, un, sp):
    c = sc[1]
    cs = u0.shape[1]
    for k, r in enumerate((u0, u1, u2, u3)):
        un[pl.ds((c ^ k) * 5, 5)] = r[...]
    for d in range(NPATH):
        thi, tlo = two(taps[:, d * BLOCK : (d + 1) * BLOCK])
        ho[d] = nn(thi, fh[...]) + nn(tlo, fh[...]) + nn(thi, fl[...])
    ua = un[...].reshape(TREE_BLK * cs, BLOCK)
    sp[...] = (nn(ua, fh[...]) + nn(ua, fl[...])).reshape(TREE_BLK, cs, 2 * BLOCK)
    sg = signs()

    def window(k, par):
        a = sp[k]
        wr = sg * a[:, BLOCK:]
        wi = -(sg * a[:, :BLOCK])
        if par is not None:
            q = sp[par]
            wr = wr + q[:, :BLOCK]
            wi = wi + q[:, BLOCK:]
        wo[k, :, :BLOCK] = wr
        wo[k, :, BLOCK:] = wi

    window(0, None)

    @pl.loop(1, TRUNK)
    def _(k):
        window(k, k - 1)

    @pl.loop(0, BRANCHES)
    def _(i):
        window(TRUNK + i, TRUNK - 1)

    @pl.loop(0, LEAVES)
    def _(i):
        window(TRUNK + BRANCHES + i, leaf_parent(sc, i))

    zero = jnp.zeros((cs, BLOCK), f32)

    def put(k, acc):
        sp[k, :, :BLOCK] = acc[0]
        sp[k, :, BLOCK:] = acc[1]

    @pl.loop(0, TRUNK)
    def _(q):
        acc = lax.fori_loop(0, q + 1, lambda d, a: mul(a, ho[d], wo[q - d]), (zero, zero))
        put(q, acc)

    common_b = lax.fori_loop(1, 9, lambda d, a: mul(a, ho[d], wo[8 - d]), (zero, zero))

    @pl.loop(TRUNK, TRUNK + BRANCHES)
    def _(k):
        put(k, mul(common_b, ho[0], wo[k]))

    common_l = lax.fori_loop(2, 10, lambda d, a: mul(a, ho[d], wo[9 - d]), (zero, zero))

    @pl.loop(0, LEAVES)
    def _(i):
        k = TRUNK + BRANCHES + i
        put(k, mul(mul(common_l, ho[0], wo[k]), ho[1], wo[leaf_parent(sc, i)]))

    yhi, ylo = two(sp[...].reshape(TREE_BLK * cs, 2 * BLOCK))
    y = nn(yhi, gh[...]) + nn(ylo, gh[...]) + nn(yhi, gl[...])
    un[...] = y.astype(bf16).reshape(TREE_BLK, cs, BLOCK)
    for k, o in enumerate((y0, y1, y2, y3)):
        o[...] = un[pl.ds((c ^ k) * 5, 5)]


def gate_kernel(sc, y0, y1, y2, y3, g0, u, cols, yo, p0, p1, p2, p3, ys, gs, pk):
    c, t = sc[1], sc[2]
    cs = y0.shape[1]
    for k, r in enumerate((y0, y1, y2, y3)):
        for b in range(5):
            ys[b, pl.ds(pl.multiple_of((c ^ k) * cs, 16), cs), :] = r[b]
    skip = cols[:, 5:6][: u.shape[1]]
    for b in range(5):
        y = ys[b]
        yo[b] = y
        gs[b] = g0[b] * (y.astype(f32) + skip * u[b].astype(f32))
    pack_all(t, u.shape[1], lambda j: gs[j // 2, :, (j % 2) * 128 : (j % 2) * 128 + 128], pk, (p0, p1, p2, p3))


def pack_all(t, ch, tiles, pk, outs):
    for s in range(WAYS):

        def store(row, v, s=s):
            pk[s, row : row + v.shape[0]] = v.astype(bf16)

        pack_share(tiles, s, ch, store)
    for k, o in enumerate(outs):
        o[...] = pk[t ^ k]


def unpack_all(t, ch, ins, pk, put):
    for k, r in enumerate(ins):
        pk[t ^ k] = r[...]
    for s in range(WAYS):
        (a, b), _ = share_tiles(s)
        put(a, pk[s, 0:ch].astype(f32))
        put(b, pk[s, ch : 2 * ch].astype(f32))
    low = lax.broadcasted_iota(jnp.int32, (ch // 2, 128), 1) < 64
    for j, (s0, s1) in ((2, (0, 1)), (7, (2, 3))):
        x0 = pk[s0, 2 * ch :].astype(f32)
        x1 = pk[s1, 2 * ch :].astype(f32)
        top = jnp.where(low, x0, pltpu.roll(x1, 64, 1))
        bot = jnp.where(low, pltpu.roll(x0, 64, 1), x1)
        put(j, jnp.concatenate([top, bot], axis=0))


def mix_kernel(sc, p0, p1, p2, p3, ow, tok, vec, r1o, a2o, acc):
    t = sc[2]
    ch = ow.shape[0] // WAYS
    offs = share_offsets(t)
    parts = [None, None, None]
    for k, r in enumerate((p0, p1, p2, p3)):
        w = ow[pl.ds(pl.multiple_of((t ^ k) * ch, 64), ch), :]
        piece = r[...]
        xs = (piece[:ch].astype(f32), piece[ch : 2 * ch].astype(f32), left_rows(piece, ch))
        for i, x in enumerate(xs):
            v = nn(x.T.astype(bf16), w)
            parts[i] = v if parts[i] is None else parts[i] + v
    acc[pl.ds(pl.multiple_of(offs[0], 64), 128), :] = parts[0]
    acc[pl.ds(pl.multiple_of(offs[1], 64), 128), :] = parts[1]
    acc[pl.ds(pl.multiple_of(offs[2], 64), 64), :] = parts[2][:64]
    r1 = tok[...].astype(f32) + (acc[...] + vec[2:3])
    r1o[...] = r1
    nh, _ = norm_parts(r1)
    a2o[...] = (nh * vec[3:4] + vec[4:5]).astype(bf16)


def mlp_kernel(sc, xa, xb, ca, cb, up, down, vec, dpa, dpb, aca, acb, pa, pb):
    bias = vec[5:6]
    for x, ct, dpo, aco, po in ((xa, ca, dpa, aca, pa), (xb, cb, dpb, acb, pb)):
        p = nt(x[...], up[...]) + bias
        d = nt(ct[...], down[...])
        p2 = p * p
        th = jnp.tanh(GELU_A * p * (1.0 + GELU_B * p2))
        half = 0.5 * (1.0 + th)
        aco[...] = (p * half).astype(bf16)
        slope = half + 0.5 * p * (1.0 - th * th) * (GELU_A * (1.0 + 3.0 * GELU_B * p2))
        dp = (d * slope).astype(bf16)
        dpo[...] = dp
        po[...] = nn(dp, up[...]).astype(bf16)


def ffn_kernel(sc, a0, a1, a2, a3, down, f0, f1, f2, f3):
    for a, o in ((a0, f0), (a1, f1), (a2, f2), (a3, f3)):
        o[...] = nn(a[...], down[...]).astype(bf16)


def mlp_grad_kernel(sc, x0, x1, x2, x3, d0, d1, d2, d3, a0, a1, a2, a3, c0, c1, c2, c3, ug, dg, ub):
    acc = None
    for x, d in ((x0, d0), (x1, d1), (x2, d2), (x3, d3)):
        v = tn(d[...], x[...])
        acc = v if acc is None else acc + v
    ug[...] = acc.astype(bf16)
    acc = None
    sums = None
    for a, ct, d in ((a0, c0, d0), (a1, c1, d1), (a2, c2, d2), (a3, c3, d3)):
        v = tn(a[...], ct[...])
        acc = v if acc is None else acc + v
        w = jnp.sum(d[...].astype(f32), axis=0, keepdims=True)
        sums = w if sums is None else sums + w
    dg[...] = acc.astype(bf16)
    ub[...] = sums


def norm2_kernel(sc, own, core, far, r1, cot, vec, ow, dro, dmo, sums, p0, p1, p2, p3, pk):
    t = sc[2]
    dn2 = own[...].astype(f32) + core[...].astype(f32) + far[...].astype(f32)
    nh, rs = norm_parts(r1[...])
    ct = cot[...].astype(f32)
    sums[0:1] = jnp.sum(dn2 * nh, axis=0, keepdims=True)
    sums[1:2] = jnp.sum(dn2, axis=0, keepdims=True)
    dr = ct + norm_back(nh, rs, dn2 * vec[3:4])
    dro[...] = dr
    dm = dr.astype(bf16)
    dmo[...] = dm
    sums[2:3] = jnp.sum(dm.astype(f32), axis=0, keepdims=True)
    sums[3:4] = jnp.sum(ct, axis=0, keepdims=True)
    offs = share_offsets(t)
    ch = ow.shape[0] // WAYS
    da = dmo[pl.ds(pl.multiple_of(offs[0], 64), 128), :]
    db = dmo[pl.ds(pl.multiple_of(offs[1], 64), 128), :]
    dc = dmo[pl.ds(pl.multiple_of(offs[2], 64), 64), :]
    low = lax.broadcasted_iota(jnp.int32, (ch // 2, 128), 1) < 64
    dc2 = jnp.concatenate([dc, dc], axis=0)
    for s in range(WAYS):
        w = ow[s * ch : (s + 1) * ch, :]
        pk[s, 0:ch] = nt(w, da).astype(bf16)
        pk[s, ch : 2 * ch] = nt(w, db).astype(bf16)
        v = nt(w, dc2)
        pk[s, 2 * ch :] = jnp.where(low, v[: ch // 2], v[ch // 2 :]).astype(bf16)
    for k, o in enumerate((p0, p1, p2, p3)):
        o[...] = pk[t ^ k]


def out_grad_kernel(sc, p0, p1, p2, p3, dm, og):
    t = sc[2]
    offs = share_offsets(t)
    ch = og.shape[0] // WAYS
    da = dm[pl.ds(pl.multiple_of(offs[0], 64), 128), :]
    db = dm[pl.ds(pl.multiple_of(offs[1], 64), 128), :]
    dc = dm[pl.ds(pl.multiple_of(offs[2], 64), 64), :]
    for k, r in enumerate((p0, p1, p2, p3)):
        piece = r[...]
        left = left_rows(piece, ch)[:, :64].astype(bf16)
        v = nn(piece[:ch], da) + nn(piece[ch : 2 * ch], db) + nn(left, dc)
        og[pl.ds(pl.multiple_of((t ^ k) * ch, 64), ch), :] = v.astype(bf16)


def ungate_kernel(sc, p0, p1, p2, p3, g0, ys, u, cols, dyo, dgo, so, d0, d1, d2, d3, pk, dg):
    c, t = sc[1], sc[2]
    ch = u.shape[1]
    cs = ch // WAYS

    def put(j, v):
        dg[j // 2, :, (j % 2) * 128 : (j % 2) * 128 + 128] = v

    unpack_all(t, ch, (p0, p1, p2, p3), pk, put)
    skip = cols[:, 5:6][:ch]
    tot = None
    for b in range(5):
        g = dg[b]
        uu = u[b].astype(f32)
        dgo[b] = g * (ys[b].astype(f32) + skip * uu)
        dy = g * g0[b]
        v = jnp.sum(dy * uu, axis=1, keepdims=True)
        tot = v if tot is None else tot + v
        dyo[b] = dy.astype(bf16)
    so[...] = tot
    for k, o in enumerate((d0, d1, d2, d3)):
        for b in range(5):
            o[b] = dyo[b, pl.ds(pl.multiple_of((c ^ k) * cs, 16), cs), :]


def conv_back_kernel(sc, d0, d1, d2, d3, ws, hs, fh, fl, gh, gl, dho, o0, o1, o2, o3, un, dy, dw, dh):
    c = sc[1]
    cs = d0.shape[1]
    for k, r in enumerate((d0, d1, d2, d3)):
        un[pl.ds((c ^ k) * 5, 5)] = r[...]
    da = un[...].reshape(TREE_BLK * cs, BLOCK)
    dy[0:TREE_BLK] = (nt(da, gh[...]) + nt(da, gl[...])).reshape(TREE_BLK, cs, 2 * BLOCK)
    zero = jnp.zeros((cs, BLOCK), f32)
    zz = jnp.zeros((cs, 2 * BLOCK), f32)
    first_leaf = TRUNK + BRANCHES
    sum_b = lax.fori_loop(TRUNK, first_leaf, lambda k, a: a + dy[k], zz)
    sum_l = lax.fori_loop(first_leaf, TREE_BLK, lambda k, a: a + dy[k], zz)
    dy[TREE_BLK] = sum_b
    dy[TREE_BLK + 1] = sum_l
    for i in range(BRANCHES):
        dy[TREE_BLK + 2 + i] = zz

    @pl.loop(0, LEAVES)
    def _(i):
        k = TREE_BLK + 2 + leaf_parent(sc, i) - TRUNK
        dy[k] = dy[k] + dy[first_leaf + i]

    def put(ref, k, acc):
        ref[k, :, :BLOCK] = acc[0]
        ref[k, :, BLOCK:] = acc[1]

    @pl.loop(0, TRUNK)
    def _(j):
        acc = lax.fori_loop(j, TRUNK, lambda q, a: mul_conj(a, hs[q - j], dy[q]), (zero, zero))
        acc = mul_conj(acc, hs[8 - j], dy[TREE_BLK])
        put(dw, j, mul_conj(acc, hs[9 - j], dy[TREE_BLK + 1]))

    @pl.loop(0, BRANCHES)
    def _(i):
        k = TRUNK + i
        acc = mul_conj((zero, zero), hs[0], dy[k])
        put(dw, k, mul_conj(acc, hs[1], dy[TREE_BLK + 2 + i]))

    @pl.loop(first_leaf, TREE_BLK)
    def _(k):
        put(dw, k, mul_conj((zero, zero), hs[0], dy[k]))

    @pl.loop(0, TRUNK)
    def _(d):
        put(dh, d, lax.fori_loop(d, TRUNK, lambda q, a: mul_conj(a, ws[q - d], dy[q]), (zero, zero)))

    put(dh, 8, (zero, zero))
    put(dh, 9, (zero, zero))

    def more(d, k, q):
        acc = (dh[d, :, :BLOCK], dh[d, :, BLOCK:])
        put(dh, d, mul_conj(acc, ws[k], dy[q]))

    @pl.loop(1, 9)
    def _(d):
        more(d, 8 - d, TREE_BLK)

    @pl.loop(2, 10)
    def _(d):
        more(d, 9 - d, TREE_BLK + 1)

    @pl.loop(TRUNK, TREE_BLK)
    def _(k):
        more(0, k, k)

    @pl.loop(0, BRANCHES)
    def _(i):
        more(1, TRUNK + i, TREE_BLK + 2 + i)

    for d in range(NPATH):
        thi, tlo = two(dh[d])
        dho[:, d * BLOCK : (d + 1) * BLOCK] = nt(thi, fh[...]) + nt(tlo, fh[...]) + nt(thi, fl[...])

    sg = signs()

    def own(k):
        w = dw[k]
        return jnp.concatenate([-(sg * w[:, BLOCK:]), sg * w[:, :BLOCK]], axis=1)

    @pl.loop(0, TRUNK - 1)
    def _(k):
        dy[k] = own(k) + dw[k + 1]

    dy[TRUNK - 1] = lax.fori_loop(TRUNK, first_leaf, lambda k, a: a + dw[k], own(TRUNK - 1))

    @pl.loop(TRUNK, TREE_BLK)
    def _(k):
        dy[k] = own(k)

    @pl.loop(0, LEAVES)
    def _(i):
        k = leaf_parent(sc, i)
        dy[k] = dy[k] + dw[first_leaf + i]

    shi, slo = two(dy[0:TREE_BLK].reshape(TREE_BLK * cs, 2 * BLOCK))
    du = nt(shi, fh[...]) + nt(slo, fh[...]) + nt(shi, fl[...])
    un[...] = du.astype(bf16).reshape(TREE_BLK, cs, BLOCK)
    for k, o in enumerate((o0, o1, o2, o3)):
        o[...] = un[pl.ds((c ^ k) * 5, 5)]


def unconv_kernel(sc, u0, u1, u2, u3, dyv, dg0, s, z, zr, cols, dzo, rims, cg, dus, rs):
    b = pl.program_id(0)
    c = sc[1]
    ch = dyv.shape[1]
    cs = ch // WAYS
    for k, r in enumerate((u0, u1, u2, u3)):
        dus[pl.ds(pl.multiple_of((c ^ k) * cs, 16), cs), :] = r[0]
    cv = cols[...]
    w0, w1, w2 = (cv[:, i : i + 1] for i in range(3))
    skip = cv[:ch, 5:6]
    du = dus[...].astype(f32) + skip * dyv[0].astype(f32)
    sv = s[0]
    ds = jnp.concatenate([dg0[0], du * sv[2 * ch :], du * sv[ch : 2 * ch]], axis=0)
    lane = lax.broadcasted_iota(jnp.int32, ds.shape, 1)
    zv = z[0].astype(f32)
    far, near = zr[0][:, 0:1], zr[0][:, 1:2]
    z1 = jnp.where(lane == 0, near, pltpu.roll(zv, 1, 1))
    z2 = jnp.where(lane == 0, far, jnp.where(lane == 1, near, pltpu.roll(zv, 2, 1)))

    def total(v):
        return jnp.sum(v, axis=1, keepdims=True)

    lane8 = lax.broadcasted_iota(jnp.int32, (ds.shape[0], 128), 1)
    packed = jnp.where(
        lane8 == 0,
        total(ds),
        jnp.where(lane8 == 1, total(ds * zv), jnp.where(lane8 == 2, total(ds * z1), jnp.where(lane8 == 3, total(ds * z2), 0.0))),
    )

    @pl.when(b == 0)
    def _():
        cg[...] = packed
        rs[...] = jnp.zeros_like(rs)

    @pl.when(b > 0)
    def _():
        cg[...] = cg[...] + packed

    n1 = jnp.where(lane == BLOCK - 1, 0.0, pltpu.roll(ds, BLOCK - 1, 1))
    n2 = jnp.where(lane >= BLOCK - 2, 0.0, pltpu.roll(ds, BLOCK - 2, 1))
    dzo[0] = w0 * ds + w1 * n1 + w2 * n2
    d0, d1 = ds[:, 0:1], ds[:, 1:2]
    rs[...] = rs[...] + jnp.where(lane8 == 2 * b, w2 * d0, jnp.where(lane8 == 2 * b + 1, w1 * d0 + w2 * d1, 0.0))

    @pl.when(b == 4)
    def _():
        rims[...] = rs[...].T[:16]


def dz_kernel(sc, dzo, r0, r1, r2, r3, pick, dz, p0, p1, p2, p3, ib, rall, rt, pk):
    c, t = sc[1], sc[2]
    rows = dzo.shape[1]
    for k, r in enumerate((r0, r1, r2, r3)):
        rall[pl.ds(pl.multiple_of((c ^ k) * 16, 16), 16), :] = r[...]
    got = lax.dot_general(
        pick[...], rall[...], (((1,), (0,)), ((), ())), precision=exact_mode, preferred_element_type=f32
    )
    rt[...] = got.T
    lane = lax.broadcasted_iota(jnp.int32, (rows, 128), 1)
    tot = None
    for b in range(5):
        add = jnp.where(lane >= 126, pltpu.roll(rt[...], 126 - 2 * b, 1), 0.0)
        lo = dzo[b, :, :128].astype(bf16)
        hi = (dzo[b, :, 128:] + add).astype(bf16)
        dz[b, :, :128] = lo
        dz[b, :, 128:] = hi
        v = jnp.sum(lo.astype(f32) + hi.astype(f32), axis=1, keepdims=True)
        tot = v if tot is None else tot + v
    ib[...] = tot
    pack_all(t, rows, lambda j: dz[j // 2, :, (j % 2) * 128 : (j % 2) * 128 + 128].astype(f32), pk, (p0, p1, p2, p3))


def in_grad_kernel(sc, dz, a1, wt, ib, vec, ig, sums):
    acc = None
    for b in range(5):
        v = nn(dz[b], a1[b * BLOCK : (b + 1) * BLOCK, :])
        acc = v if acc is None else acc + v
    ig[...] = acc
    w = wt[...].astype(f32)
    gsum = jnp.sum(w * acc, axis=0, keepdims=True)
    bsum = jnp.sum(w * ib[...], axis=0, keepdims=True)
    sums[0:1] = (gsum - vec[1:2] * bsum) / vec[0:1]
    sums[1:2] = bsum


def norm1_kernel(sc, p0, p1, p2, p3, wf, tok, dr, vec, out, acc):
    t = sc[2]
    rows = wf.shape[1]
    offs = share_offsets(t)
    parts = [None, None, None]
    for k, r in enumerate((p0, p1, p2, p3)):
        w = wf[t ^ k]
        piece = r[...]
        xs = (piece[:rows].astype(f32), piece[rows : 2 * rows].astype(f32), left_rows(piece, rows))
        for i, x in enumerate(xs):
            v = nn(x.T.astype(bf16), w)
            parts[i] = v if parts[i] is None else parts[i] + v
    acc[pl.ds(pl.multiple_of(offs[0], 64), 128), :] = parts[0]
    acc[pl.ds(pl.multiple_of(offs[1], 64), 128), :] = parts[1]
    acc[pl.ds(pl.multiple_of(offs[2], 64), 64), :] = parts[2][:64]
    nh, rs = norm_parts(tok[...].astype(f32))
    out[...] = (dr[...] + norm_back(nh, rs, acc[...] * vec[0:1])).astype(bf16)


def layer_out_kernel(sc, r1, own, core, far, vec, out):
    ffn = own[...].astype(f32) + core[...].astype(f32) + far[...].astype(f32)
    out[...] = (r1[...] + ffn + vec[6:7]).astype(bf16)


def body(
    shard_count,
    tokens,
    parents,
    norm1_gain,
    norm1_bias,
    in_weight,
    in_bias,
    conv_weight,
    conv_bias,
    filt_in,
    filt_bias1,
    filt_mid,
    filt_bias2,
    sine_freq,
    filt_out,
    skip_gain,
    out_weight,
    out_bias,
    norm2_gain,
    norm2_bias,
    up_weight,
    up_bias,
    down_weight,
    down_bias,
    cotangent,
):
    rows, width = tokens.shape
    ch = skip_gain.shape[0]
    cs = ch // WAYS
    ch3 = 3 * ch
    ffq = up_bias.shape[0]
    ffs = ffq // WAYS
    share = rows // WAYS
    d_part = in_weight.shape[0]
    s_id = lax.axis_index("shards")
    c_id = lax.axis_index("context")
    t_id = lax.axis_index("tensor")
    pair = shard_count == 2

    def gather_shards(x, axis):
        if not pair:
            return lax.all_gather(x, "shards", axis=axis, tiled=True)
        o = lax.ppermute(x, "shards", [(0, 1), (1, 0)])
        lo = jnp.where(s_id == 0, x, o)
        hi = jnp.where(s_id == 0, o, x)
        return jnp.concatenate([lo, hi], axis=axis)

    par = parents[0]
    gb = c_id * 5 + jnp.arange(5, dtype=jnp.int32)
    all_b = jnp.arange(TREE_BLK, dtype=jnp.int32)
    all_par = jnp.concatenate(
        [jnp.arange(-1, TRUNK - 1, dtype=jnp.int32), jnp.full((BRANCHES,), TRUNK - 1, jnp.int32), TRUNK - 1 + par[1 + BRANCHES :]]
    )
    own_par = lax.dynamic_slice_in_dim(all_par, c_id * 5, 5, 0)
    sc = jnp.concatenate([jnp.stack([s_id, c_id, t_id]).astype(jnp.int32), own_par, par]).astype(jnp.int32)

    wt_part = jnp.transpose(in_weight, (1, 2, 0)).reshape(ch3, d_part)
    wt = gather_shards(wt_part, 1)
    rim_tok = lax.all_gather(tokens.reshape(5, BLOCK, width)[:, BLOCK - 2 :, :], "context", axis=0, tiled=True)
    fo = gather_shards(filt_out, 0)
    fo_t = lax.dynamic_slice_in_dim(fo, c_id * cs, cs, 1).astype(f32).T
    up_t = lax.dynamic_slice_in_dim(up_weight, c_id * ffs, ffs, 1).T
    down_c = lax.dynamic_slice_in_dim(down_weight, c_id * ffs, ffs, 0)
    packed = gather_shards(jnp.stack([out_weight, up_t, down_c]), 2)
    ow = lax.all_gather(packed[0], "tensor", axis=0, tiled=True)
    up = lax.all_gather(packed[1], "tensor", axis=0, tiled=True)
    down = lax.all_gather(packed[2], "tensor", axis=0, tiled=True)
    up_b = lax.all_gather(lax.dynamic_slice_in_dim(up_bias, c_id * ffs, ffs, 0), "tensor", axis=0, tiled=True)
    w_full = lax.all_gather(wt, "tensor", axis=0, tiled=False)
    tok_share = lax.dynamic_slice_in_dim(tokens, t_id * share, share, 0)
    cot_share = lax.dynamic_slice_in_dim(cotangent, t_id * share, share, 0)
    cot1 = swap(cot_share, "context", 1)
    cot2 = swap(cot_share, "context", 2)
    cot3 = swap(cot2, "context", 1)

    vec = jnp.stack([norm1_gain, norm1_bias, out_bias, norm2_gain, norm2_bias, up_b, down_bias, down_bias])
    zcol = jnp.zeros((ch3,), f32)
    cols = jnp.stack(
        [
            conv_weight[0].reshape(-1),
            conv_weight[1].reshape(-1),
            conv_weight[2].reshape(-1),
            conv_bias.reshape(-1),
            in_bias.reshape(-1),
            jnp.concatenate([skip_gain, skip_gain, skip_gain]),
            zcol,
            zcol,
        ],
        axis=1,
    )
    fh, fl, gh, gl = (jnp.asarray(a) for a in dft_tables())

    embedded = jnp.asarray(embed_table((filt_in.shape[0] - 1) // 2))
    channel = (t_id * ch + c_id * cs).astype(f32) + jnp.arange(cs, dtype=f32)
    slow, fast = math.log(0.01) / 1.5, math.log(0.01) / 0.3
    rates = jnp.abs(slow + (fast - slow) * channel / (ch * WAYS - 1))
    ramp = jnp.arange(PATH, dtype=f32) / (PATH - 1)

    def make_taps(f_in, b1, f_mid, b2, freq, f_out_t):
        one = jnp.sin(freq[:, None] * (jnp.einsum("ek,el->kl", f_in, embedded, precision=exact_mode) + b1[:, None]))
        mid = jnp.sin(freq[:, None] * (jnp.einsum("jk,jl->kl", f_mid, one, precision=exact_mode) + b2[:, None]))
        raw = jnp.dot(f_out_t, mid, precision=exact_mode)
        return raw * (jnp.exp(-ramp[None, :] * rates[:, None]) + 0.05)

    taps, taps_back = jax.vjp(make_taps, filt_in, filt_bias1, filt_mid, filt_bias2, sine_freq, fo_t)

    nb, B = 5, BLOCK
    a1, z, zr, s, u, u0, u1, u2, u3 = pl.pallas_call(
        proj_kernel,
        grid_spec=pltpu.PrefetchScalarGridSpec(
            num_scalar_prefetch=1,
            grid=(nb,),
            in_specs=[
                pl.BlockSpec((B, width), lambda b, sc: (b, 0)),
                pl.BlockSpec((1, 2, width), lambda b, sc: (jnp.maximum(sc[3 + b], 0), 0, 0)),
                pl.BlockSpec((ch3, width), lambda b, sc: (0, 0)),
                pl.BlockSpec((ch3, 8), lambda b, sc: (0, 0)),
                pl.BlockSpec((8, width), lambda b, sc: (0, 0)),
            ],
            out_specs=[
                pl.BlockSpec((B, width), lambda b, sc: (b, 0)),
                pl.BlockSpec((1, ch3, B), lambda b, sc: (b, 0, 0)),
                pl.BlockSpec((1, ch3, 16), lambda b, sc: (b, 0, 0)),
                pl.BlockSpec((1, ch3, B), lambda b, sc: (b, 0, 0)),
                pl.BlockSpec((1, ch, B), lambda b, sc: (b, 0, 0)),
            ]
            + [pl.BlockSpec((1, cs, B), lambda b, sc: (b, 0, 0))] * 4,
            scratch_shapes=[pltpu.VMEM((ch, B), bf16)],
        ),
        out_shape=[
            jax.ShapeDtypeStruct((rows, width), bf16),
            jax.ShapeDtypeStruct((nb, ch3, B), bf16),
            jax.ShapeDtypeStruct((nb, ch3, 16), f32),
            jax.ShapeDtypeStruct((nb, ch3, B), f32),
            jax.ShapeDtypeStruct((nb, ch, B), bf16),
        ]
        + [jax.ShapeDtypeStruct((nb, cs, B), bf16)] * 4,
        compiler_params=pltpu.CompilerParams(vmem_limit_bytes=48 << 20),
    )(sc, tokens, rim_tok, wt, cols, vec)

    def ctx(p):
        return (p[0], swap(p[1], "context", 1), swap(p[2], "context", 2), swap(p[3], "context", 3))

    def ten(p):
        return (p[0], swap(p[1], "tensor", 1), swap(p[2], "tensor", 2), swap(p[3], "tensor", 3))

    un = ctx((u0, u1, u2, u3))
    spec = ((TREE_BLK, cs, 2 * B), f32)
    piece = ((nb, cs, B), bf16)
    ws, hs, y0, y1, y2, y3 = call(
        conv_kernel,
        [spec, ((NPATH, cs, 2 * B), f32)] + [piece] * 4,
        9,
        [pltpu.VMEM((TREE_BLK, cs, B), bf16), pltpu.VMEM((TREE_BLK, cs, 2 * B), f32)],
    )(sc, *un, taps, fh, fl, gh, gl)
    yn = ctx((y0, y1, y2, y3))

    g0 = s[:, :ch]
    packs = (5 * ch // 2, 128)
    packed_out = [(packs, bf16)] * 4
    ys, *gp = call(
        gate_kernel,
        [((nb, ch, B), bf16)] + packed_out,
        7,
        [pltpu.VMEM((nb, ch, B), bf16), pltpu.VMEM((nb, ch, B), f32), pltpu.VMEM((WAYS,) + packs, bf16)],
    )(sc, *yn, g0, u, cols)
    gn = ten(gp)

    sh = (share, width)
    r1, a2 = call(mix_kernel, [(sh, f32), (sh, bf16)], 7, [pltpu.VMEM(sh, f32)])(sc, *gn, ow, tok_share, vec)

    x1 = swap(a2, "context", 1)
    x2 = swap(a2, "context", 2)
    x3 = swap(x2, "context", 1)
    mlp = call(mlp_kernel, [((share, ffq), bf16)] * 4 + [(sh, bf16)] * 2, 7)
    dp0, dp1, ac0, ac1, n0, n1 = mlp(sc, a2, x1, cot_share, cot1, up, down, vec)
    dp2, dp3, ac2, ac3, n2, n3 = mlp(sc, x2, x3, cot2, cot3, up, down, vec)

    def sum_context(q0, q1, q2, q3):
        a = swap(q1, "context", 1)
        b = swap(q3, "context", 1)
        far = swap((q2.astype(f32) + b.astype(f32)).astype(bf16), "context", 2)
        return q0, a, far

    dn = sum_context(n0, n1, n2, n3)
    dr1, dm, sums2, *dgp = call(
        norm2_kernel, [(sh, f32), (sh, bf16), ((8, width), f32)] + packed_out, 7, [pltpu.VMEM((WAYS,) + packs, bf16)]
    )(sc, *dn, r1, cot_share, vec, ow)
    dgn = ten(dgp)

    f0, f1, f2, f3 = call(ffn_kernel, [(sh, bf16)] * 4, 5)(sc, ac0, ac1, ac2, ac3, down)
    fs = sum_context(f0, f1, f2, f3)
    (layer_out,) = call(layer_out_kernel, [(sh, bf16)], 5)(sc, r1, *fs, vec)

    ug, dgw, ub = call(mlp_grad_kernel, [((ffq, width), bf16)] * 2 + [((1, ffq), f32)], 16)(
        sc, a2, x1, x2, x3, dp0, dp1, dp2, dp3, ac0, ac1, ac2, ac3, cot_share, cot1, cot2, cot3
    )
    (og,) = call(out_grad_kernel, [((WAYS * ch, width), bf16)], 5)(sc, *gn, dm)

    dy, dg0, skip_g, d0, d1, d2, d3 = call(
        ungate_kernel,
        [((nb, ch, B), bf16), ((nb, ch, B), f32), ((ch, 1), f32)] + [piece] * 4,
        8,
        [pltpu.VMEM((WAYS,) + packs, bf16), pltpu.VMEM((nb, ch, B), f32)],
    )(sc, *dgn, g0, ys, u, cols)
    dn_ = ctx((d0, d1, d2, d3))
    dtaps, e0, e1, e2, e3 = call(
        conv_back_kernel,
        [((cs, PATH), f32)] + [piece] * 4,
        10,
        [
            pltpu.VMEM((TREE_BLK, cs, B), bf16),
            pltpu.VMEM((TREE_BLK + 6, cs, 2 * B), f32),
            pltpu.VMEM((TREE_BLK, cs, 2 * B), f32),
            pltpu.VMEM((NPATH, cs, 2 * B), f32),
        ],
    )(sc, *dn_, ws, hs, fh, fl, gh, gl)
    en = ctx((e0, e1, e2, e3))

    blk = lambda *d: pl.BlockSpec((1,) + d, lambda b, sc: (b, 0, 0))
    dzo, rims, cg = pl.pallas_call(
        unconv_kernel,
        grid_spec=pltpu.PrefetchScalarGridSpec(
            num_scalar_prefetch=1,
            grid=(nb,),
            in_specs=[blk(cs, B)] * 4
            + [blk(ch, B), blk(ch, B), blk(ch3, B), blk(ch3, B), blk(ch3, 16), pl.BlockSpec((ch3, 8), lambda b, sc: (0, 0))],
            out_specs=[
                blk(ch3, B),
                pl.BlockSpec((16, ch3), lambda b, sc: (0, 0)),
                pl.BlockSpec((ch3, 128), lambda b, sc: (0, 0)),
            ],
            scratch_shapes=[pltpu.VMEM((ch, B), bf16), pltpu.VMEM((ch3, 128), f32)],
        ),
        out_shape=[
            jax.ShapeDtypeStruct((nb, ch3, B), f32),
            jax.ShapeDtypeStruct((16, ch3), f32),
            jax.ShapeDtypeStruct((ch3, 128), f32),
        ],
        compiler_params=pltpu.CompilerParams(vmem_limit_bytes=48 << 20),
    )(sc, *en, dy, dg0, s, z, zr, cols)
    rn = ctx((rims, rims, rims, rims))
    col = jnp.arange(WAYS * 16, dtype=jnp.int32)
    col_blk = (col // 16) * 5 + (col % 16) // 2
    col_ok = (col % 16) < 10
    col_par = jnp.where(col_ok, all_par[jnp.minimum(col_blk, TREE_BLK - 1)], -2)
    row = jnp.arange(128, dtype=jnp.int32)
    pick = (
        (row[:, None] < 10)
        & (col_par[None, :] == c_id * 5 + row[:, None] // 2)
        & (col[None, :] % 2 == row[:, None] % 2)
    ).astype(f32)
    dpacks = (5 * ch3 // 2, 128)
    dz, q0, q1, q2, q3, ib = call(
        dz_kernel,
        [((nb, ch3, B), bf16)] + [(dpacks, bf16)] * 4 + [((ch3, 1), f32)],
        6,
        [pltpu.VMEM((WAYS * 16, ch3), f32), pltpu.VMEM((ch3, 128), f32), pltpu.VMEM((WAYS,) + dpacks, bf16)],
    )(sc, dzo, *rn, pick)
    qn = ten((q0, q1, q2, q3))
    ig, sums1 = call(in_grad_kernel, [((ch3, width), f32), ((8, width), f32)], 5)(sc, dz, a1, wt, ib, vec)
    (tokens_grad,) = call(norm1_kernel, [(sh, bf16)], 8, [pltpu.VMEM(sh, f32)])(sc, *qn, w_full, tok_share, dr1, vec)

    def half_sum(x, axis):
        if not pair:
            return lax.psum_scatter(x, "shards", scatter_dimension=axis, tiled=True)
        n = x.shape[axis] // 2
        theirs = lax.dynamic_slice_in_dim(x, (1 - s_id) * n, n, axis).astype(bf16)
        mine = lax.dynamic_slice_in_dim(x, s_id * n, n, axis)
        return mine + lax.ppermute(theirs, "shards", [(0, 1), (1, 0)]).astype(f32)

    ih = half_sum(ig, 1)
    ih = ih + swap(ih.astype(bf16), "context", 1).astype(f32)
    ih = ih + swap(ih.astype(bf16), "context", 2).astype(f32)
    in_grad = jnp.transpose(ih.reshape(3, ch, d_part), (2, 0, 1))

    both = jnp.stack([ug, dgw])
    both = lax.psum_scatter(both, "shards", scatter_dimension=2, tiled=True)
    both = lax.psum_scatter(both, "tensor", scatter_dimension=1, tiled=True)
    both = lax.all_gather(both, "context", axis=1, tiled=True).astype(f32)
    up_grad, down_grad = both[0].T, both[1]
    oh = lax.psum_scatter(og, "shards", scatter_dimension=1, tiled=True)
    oh = lax.psum_scatter(oh, "tensor", scatter_dimension=0, tiled=True)
    out_grad = lax.psum(oh.astype(f32), "context")

    f_in_g, b1_g, f_mid_g, b2_g, freq_g, fo_g = taps_back(dtaps)

    def widen(part, place, count):
        whole = jnp.zeros(part.shape[:-1] + (part.shape[-1] * count,), f32)
        return lax.dynamic_update_slice_in_dim(whole, part, place * part.shape[-1], part.ndim - 1)

    def wide_t(part):
        return widen(part, t_id, WAYS)

    conv_sums = cg[:, :4].T.reshape(4, 3, ch)
    ub_rows = ub.reshape(WAYS, 1, ffs)
    ub_wide = lax.dynamic_update_slice(jnp.zeros((WAYS, WAYS, ffs), f32), ub_rows, (0, c_id, 0)).reshape(-1)
    fo_wide = widen(widen(fo_g.T, c_id, WAYS), t_id, WAYS)
    items = [
        sums1[0],
        sums1[1],
        wide_t(ib.reshape(3, ch)),
        wide_t(conv_sums),
        f_in_g,
        b1_g,
        f_mid_g,
        b2_g,
        freq_g,
        wide_t(skip_g.reshape(1, ch)),
        sums2[0],
        sums2[1],
        sums2[2],
        sums2[3],
        ub_wide,
        fo_wide,
    ]
    flat = lax.psum(jnp.concatenate([i.reshape(-1) for i in items]), ("shards", "context", "tensor"))
    got, at = [], 0
    for i in items:
        got.append(flat[at : at + i.size].reshape(i.shape))
        at += i.size

    def narrow(x):
        return lax.dynamic_slice_in_dim(x, t_id * ch, ch, x.ndim - 1)

    conv_all = narrow(got[3])
    fo_own = lax.dynamic_slice_in_dim(narrow(got[15]), s_id * filt_out.shape[0], filt_out.shape[0], 0)
    return (
        layer_out,
        tokens_grad,
        got[0],
        got[1],
        in_grad,
        narrow(got[2]),
        conv_all[1:4],
        conv_all[0],
        got[4],
        got[5],
        got[6],
        got[7],
        got[8],
        fo_own,
        narrow(got[9]).reshape(ch),
        out_grad,
        got[12],
        got[10],
        got[11],
        up_grad,
        lax.dynamic_slice_in_dim(got[14], t_id * ffq, ffq, 0),
        down_grad,
        got[13],
    )


def solution(mesh):
    return jax.shard_map(
        functools.partial(body, mesh.shape["shards"]),
        mesh=mesh,
        in_specs=(
            P(("shards", "context"), None),
            P("shards", None),
            P(),
            P(),
            P("shards", None, "tensor"),
            P(None, "tensor"),
            P(None, None, "tensor"),
            P(None, "tensor"),
            P(),
            P(),
            P(),
            P(),
            P(),
            P("shards", "tensor"),
            P("tensor"),
            P("tensor", "shards"),
            P(),
            P(),
            P(),
            P("shards", "tensor"),
            P("tensor"),
            P("tensor", "shards"),
            P(),
            P(("shards", "context"), None),
        ),
        out_specs=(
            P(("shards", "context", "tensor"), None),
            P(("shards", "context", "tensor"), None),
            P(),
            P(),
            P("shards", None, "tensor"),
            P(None, "tensor"),
            P(None, None, "tensor"),
            P(None, "tensor"),
            P(),
            P(),
            P(),
            P(),
            P(),
            P("shards", "tensor"),
            P("tensor"),
            P("tensor", "shards"),
            P(),
            P(),
            P(),
            P("shards", "tensor"),
            P("tensor"),
            P("tensor", "shards"),
            P(),
        ),
        check_vma=False,
    )
```

```python
import functools
import math

import jax
import jax.numpy as jnp
import ml_dtypes
import numpy as np
from jax import lax
from jax.experimental import pallas as pl
from jax.experimental.pallas import tpu as pltpu
from jax.sharding import PartitionSpec as P

BLOCK = 256
TRUNK = 8
NPATH = 10
PATH = 2560
BRANCHES = 4
LEAVES = 8
TREE_BLK = 20
WAYS = 4

f32 = jnp.float32
bf16 = jnp.bfloat16
exact_mode = lax.Precision.HIGHEST
GELU_A = math.sqrt(2.0 / math.pi)
GELU_B = 0.044715


def split_np(a):
    hi = a.astype(ml_dtypes.bfloat16)
    lo = (a - hi.astype(np.float64)).astype(ml_dtypes.bfloat16)
    return hi, lo


def dft_tables():
    k = np.arange(BLOCK)[None, :]
    n = np.arange(BLOCK)[:, None]
    ang = np.pi * ((2 * k + 1) * n % 1024) / 512.0
    fwd = np.concatenate([np.cos(ang), -np.sin(ang)], axis=1)
    m = BLOCK + np.arange(BLOCK)[None, :]
    kk = np.arange(BLOCK)[:, None]
    ang2 = np.pi * ((2 * kk + 1) * m % 1024) / 512.0
    inv = np.concatenate([np.cos(ang2), -np.sin(ang2)], axis=0) / 256.0
    return split_np(fwd) + split_np(inv)


def embed_table(bands):
    pos = np.arange(PATH, dtype=np.float64)
    base = 2.0 * np.pi * pos / PATH
    freq = 0.0001 + (bands - 1 - 0.0001) * np.arange(bands) / max(bands - 1, 1)
    phase = freq[:, None] * base[None, :]
    return np.concatenate([pos[None] / (PATH - 1), np.cos(phase), -np.sin(phase)]).astype(np.float32)


def swap(x, axis, k):
    return lax.ppermute(x, axis, [(i, i ^ k) for i in range(WAYS)])


def smem_spec():
    return pl.BlockSpec(memory_space=pltpu.SMEM)


def call(kernel, outs, n_in, scratch=(), limit=24):
    def run(sc, *args):
        assert len(args) == n_in
        vm = pl.BlockSpec(memory_space=pltpu.VMEM)
        return pl.pallas_call(
            kernel,
            out_shape=[jax.ShapeDtypeStruct(s, d) for s, d in outs],
            in_specs=[smem_spec()] + [vm] * n_in,
            out_specs=[vm] * len(outs),
            scratch_shapes=list(scratch),
            compiler_params=pltpu.CompilerParams(vmem_limit_bytes=limit << 20),
        )(sc, *args)

    return run


def after(x, *deps):
    return lax.optimization_barrier((x, deps))[0]


def nt(a, b):
    return lax.dot_general(a, b, (((1,), (1,)), ((), ())), preferred_element_type=f32)


def nn(a, b):
    return lax.dot_general(a, b, (((1,), (0,)), ((), ())), preferred_element_type=f32)


def tn(a, b):
    return lax.dot_general(a, b, (((0,), (0,)), ((), ())), preferred_element_type=f32)


def two(a):
    hi = a.astype(bf16)
    return hi, (a - hi.astype(f32)).astype(bf16)


def norm_parts(x):
    mu = jnp.mean(x, axis=-1, keepdims=True)
    xc = x - mu
    rs = lax.rsqrt(jnp.mean(xc * xc, axis=-1, keepdims=True) + 1e-05)
    return xc * rs, rs


def norm_back(nh, rs, dnh):
    m1 = jnp.mean(dnh, axis=-1, keepdims=True)
    m2 = jnp.mean(dnh * nh, axis=-1, keepdims=True)
    return rs * (dnh - m1 - nh * m2)


def share_tiles(t):
    return [((0, 1), 2), ((3, 4), 2), ((5, 6), 7), ((8, 9), 7)][t]


def pack_share(tiles, t, ch, store):
    (a, b), c = share_tiles(t)
    store(0, tiles(a))
    store(ch, tiles(b))
    x = tiles(c)
    low = lax.broadcasted_iota(jnp.int32, (ch // 2, 128), 1) < 64
    top, bot = x[: ch // 2], x[ch // 2 :]
    if t % 2 == 0:
        y = jnp.where(low, top, pltpu.roll(bot, 64, 1))
    else:
        y = jnp.where(low, pltpu.roll(top, 64, 1), bot)
    store(2 * ch, y)


def left_rows(piece, ch):
    x = piece[2 * ch :].astype(f32)
    return jnp.concatenate([x, pltpu.roll(x, 64, 1)], axis=0)


def share_offsets(t):
    odd = t % 2
    return (64 * odd, 64 * odd + 128, 256 * (1 - odd))


def norm1_fwd_kernel(sc, tok, rows, nv, a1o, colo, rt):
    gain, shift = nv[0:1], nv[1:2]
    n = rows.shape[0]
    rt[...] = jnp.zeros_like(rt)
    rt[0:n] = rows[...]
    colo[...] = rt[...].T
    for b in range(5):
        nh, _ = norm_parts(tok[b * BLOCK : (b + 1) * BLOCK, :].astype(f32))
        a1o[b * BLOCK : (b + 1) * BLOCK, :] = (nh * gain + shift).astype(bf16)


def proj_kernel(sc, a1, m0, m1, m2, m3, wt, cols, nv, zo, zro, go, gvo, uo, u0, u1, u2, u3, rim):
    c = sc[1]
    gain, shift = nv[0:1], nv[1:2]
    cv = cols[...]
    w0, w1, w2, cb, ib = (cv[:, i : i + 1] for i in range(5))
    ch = go.shape[1]
    cs = ch // WAYS
    lane = lax.broadcasted_iota(jnp.int32, (3 * ch, 128), 1)
    for k, r in enumerate((m0, m1, m2, m3)):
        rim[pl.ds((c ^ k) * 5, 5)] = r[...]
    rows = [rim[jnp.maximum(sc[3 + b], 0)] for b in range(5)]
    nhr, _ = norm_parts(jnp.concatenate(rows, axis=0).astype(f32))
    a1r = (nhr * gain + shift).astype(bf16)
    a1r = jnp.concatenate([a1r, jnp.zeros((6, a1r.shape[1]), bf16)], axis=0)
    zr = (nt(wt[...], a1r) + ib).astype(bf16).astype(f32)
    lane16 = lax.broadcasted_iota(jnp.int32, zr.shape, 1)
    keep = jnp.zeros(zr.shape, f32)
    for b in range(5):
        keep = jnp.where(lane16 // 2 == b, jnp.where(sc[3 + b] >= 0, 1.0, 0.0), keep)
    zr = zr * keep
    zro[...] = jnp.concatenate([zr, jnp.zeros((zr.shape[0], 112), f32)], axis=1).T[:16]
    for b in range(5):
        zb = (nt(wt[...], a1[b * BLOCK : (b + 1) * BLOCK, :]) + ib).astype(bf16)
        zo[b] = zb
        z = zb.astype(f32)
        far, near = zr[:, 2 * b : 2 * b + 1], zr[:, 2 * b + 1 : 2 * b + 2]
        r1, r2 = pltpu.roll(z, 1, 1), pltpu.roll(z, 2, 1)
        z1 = jnp.concatenate([jnp.where(lane == 0, near, r1[:, :128]), r1[:, 128:]], axis=1)
        z2 = jnp.concatenate(
            [jnp.where(lane == 0, far, jnp.where(lane == 1, near, r2[:, :128])), r2[:, 128:]], axis=1
        )
        sv = cb + w0 * z + w1 * z1 + w2 * z2
        go[b] = sv[:ch]
        gvo[b] = sv[ch:]
        uo[b] = (sv[2 * ch :] * sv[ch : 2 * ch]).astype(bf16)
        for k, o in enumerate((u0, u1, u2, u3)):
            o[b] = uo[b, pl.ds(pl.multiple_of((c ^ k) * cs, 16), cs), :]


def sincos(x):
    n = jnp.floor(x * (2.0 / math.pi) + 0.5)
    r = ((x - n * 1.5703125) - n * 4.837512969970703125e-4) - n * 7.54978995489188216e-8
    r2 = r * r
    sn = r + r * r2 * (-1.6666654611e-1 + r2 * (8.3321608736e-3 - r2 * 1.9515295891e-4))
    cn = 1.0 - 0.5 * r2 + r2 * r2 * (4.166664568298827e-2 + r2 * (-1.388731625493765e-3 + r2 * 2.443315711809948e-5))
    q = n.astype(jnp.int32)
    odd = (q & 1) == 1
    s1, c1 = jnp.where(odd, cn, sn), jnp.where(odd, sn, cn)
    return jnp.where((q & 2) == 2, -s1, s1), jnp.where(((q + 1) & 2) == 2, -c1, c1)


def exact_nn(a, b):
    return lax.dot_general(a, b, (((1,), (0,)), ((), ())), precision=exact_mode, preferred_element_type=f32)


def filter_chunk(d, sl, emb, fit, fmt, fc):
    frv, b1, b2, rate = (fc[:, i : i + 1] for i in range(4))
    p1 = exact_nn(fit[...], emb[:, sl]) + b1
    s1, c1 = sincos(frv * p1)
    p2 = exact_nn(fmt[...], s1) + b2
    s2, c2 = sincos(frv * p2)
    lag = (lax.broadcasted_iota(jnp.int32, (1, BLOCK), 1) + d * BLOCK).astype(f32) / (PATH - 1)
    return p1, s1, c1, p2, s2, c2, lag, rate


def filter_kernel(sc, emb, fit, fmt, fc, fo, taps):
    cs = fo.shape[0]

    for d in range(PATH // BLOCK):
        sl = pl.ds(d * BLOCK, BLOCK)
        _, _, _, _, s2, _, lag, rate = filter_chunk(d, sl, emb, fit, fmt, fc)
        taps[:, sl] = exact_nn(fo[...], s2) * (jnp.exp(-lag * rate[:cs]) + 0.05)


def leaf_parent(sc, i):
    return TRUNK - 1 + sc[8 + 1 + BRANCHES + i]


def signs():
    lane = lax.broadcasted_iota(jnp.int32, (1, BLOCK), 1)
    return (1 - 2 * (lane % 2)).astype(f32)


def mul(acc, h, w):
    hr, hi = h[:, :BLOCK], h[:, BLOCK:]
    wr, wi = w[:, :BLOCK], w[:, BLOCK:]
    return acc[0] + (hr * wr - hi * wi), acc[1] + (hr * wi + hi * wr)


def mul_conj(acc, h, w):
    hr, hi = h[:, :BLOCK], h[:, BLOCK:]
    wr, wi = w[:, :BLOCK], w[:, BLOCK:]
    return acc[0] + (hr * wr + hi * wi), acc[1] + (hr * wi - hi * wr)


def conv_kernel(sc, u0, u1, u2, u3, taps, fh, fl, gh, gl, wo, ho, y0, y1, y2, y3, un, sp):
    c = sc[1]
    cs = u0.shape[1]
    for k, r in enumerate((u0, u1, u2, u3)):
        un[pl.ds((c ^ k) * 5, 5)] = r[...]
    for d in range(NPATH):
        thi, tlo = two(taps[:, d * BLOCK : (d + 1) * BLOCK])
        ho[d] = nn(thi, fh[...]) + nn(tlo, fh[...]) + nn(thi, fl[...])
    ua = un[...].reshape(TREE_BLK * cs, BLOCK)
    sp[...] = (nn(ua, fh[...]) + nn(ua, fl[...])).reshape(TREE_BLK, cs, 2 * BLOCK)
    sg = signs()

    def window(k, par):
        a = sp[k]
        wr = sg * a[:, BLOCK:]
        wi = -(sg * a[:, :BLOCK])
        if par is not None:
            q = sp[par]
            wr = wr + q[:, :BLOCK]
            wi = wi + q[:, BLOCK:]
        wo[k, :, :BLOCK] = wr
        wo[k, :, BLOCK:] = wi

    window(0, None)

    @pl.loop(1, TRUNK)
    def _(k):
        window(k, k - 1)

    @pl.loop(0, BRANCHES)
    def _(i):
        window(TRUNK + i, TRUNK - 1)

    @pl.loop(0, LEAVES)
    def _(i):
        window(TRUNK + BRANCHES + i, leaf_parent(sc, i))

    zero = jnp.zeros((cs, BLOCK), f32)

    def put(k, acc):
        sp[k, :, :BLOCK] = acc[0]
        sp[k, :, BLOCK:] = acc[1]

    @pl.loop(0, TRUNK)
    def _(q):
        acc = lax.fori_loop(0, q + 1, lambda d, a: mul(a, ho[d], wo[q - d]), (zero, zero))
        put(q, acc)

    common_b = lax.fori_loop(1, 9, lambda d, a: mul(a, ho[d], wo[8 - d]), (zero, zero))

    @pl.loop(TRUNK, TRUNK + BRANCHES)
    def _(k):
        put(k, mul(common_b, ho[0], wo[k]))

    common_l = lax.fori_loop(2, 10, lambda d, a: mul(a, ho[d], wo[9 - d]), (zero, zero))

    @pl.loop(0, LEAVES)
    def _(i):
        k = TRUNK + BRANCHES + i
        put(k, mul(mul(common_l, ho[0], wo[k]), ho[1], wo[leaf_parent(sc, i)]))

    yhi, ylo = two(sp[...].reshape(TREE_BLK * cs, 2 * BLOCK))
    y = nn(yhi, gh[...]) + nn(ylo, gh[...]) + nn(yhi, gl[...])
    un[...] = y.astype(bf16).reshape(TREE_BLK, cs, BLOCK)
    for k, o in enumerate((y0, y1, y2, y3)):
        o[...] = un[pl.ds((c ^ k) * 5, 5)]


def gate_kernel(sc, y0, y1, y2, y3, g0, u, cols, yo, p0, p1, p2, p3, ys, gs, pk):
    c, t = sc[1], sc[2]
    cs = y0.shape[1]
    for k, r in enumerate((y0, y1, y2, y3)):
        for b in range(5):
            ys[b, pl.ds(pl.multiple_of((c ^ k) * cs, 16), cs), :] = r[b]
    skip = cols[:, 5:6][: u.shape[1]]
    for b in range(5):
        y = ys[b]
        yo[b] = y
        gs[b] = g0[b] * (y.astype(f32) + skip * u[b].astype(f32))
    pack_all(t, u.shape[1], lambda j: gs[j // 2, :, (j % 2) * 128 : (j % 2) * 128 + 128], pk, (p0, p1, p2, p3))


def pack_all(t, ch, tiles, pk, outs):
    for s in range(WAYS):

        def store(row, v, s=s):
            pk[s, row : row + v.shape[0]] = v.astype(bf16)

        pack_share(tiles, s, ch, store)
    for k, o in enumerate(outs):
        if o is not None:
            o[...] = pk[t ^ k]


def unpack_all(t, ch, ins, pk, put):
    for k, r in enumerate(ins):
        pk[t ^ k] = r[...]
    for s in range(WAYS):
        (a, b), _ = share_tiles(s)
        put(a, pk[s, 0:ch].astype(f32))
        put(b, pk[s, ch : 2 * ch].astype(f32))
    low = lax.broadcasted_iota(jnp.int32, (ch // 2, 128), 1) < 64
    for j, (s0, s1) in ((2, (0, 1)), (7, (2, 3))):
        x0 = pk[s0, 2 * ch :].astype(f32)
        x1 = pk[s1, 2 * ch :].astype(f32)
        top = jnp.where(low, x0, pltpu.roll(x1, 64, 1))
        bot = jnp.where(low, pltpu.roll(x0, 64, 1), x1)
        put(j, jnp.concatenate([top, bot], axis=0))


def sides(sc, half):
    h = sc[0]
    return pl.ds(pl.multiple_of(h * half, 128), half), pl.ds(pl.multiple_of((1 - h) * half, 128), half)


def mix_kernel(sc, p0, p1, p2, p3, owm, owo, tok, vec, r1o, a2o, acc):
    t = sc[2]
    ch, half = owm.shape[0] // WAYS, owm.shape[1]
    mine, other = sides(sc, half)
    offs = share_offsets(t)
    parts = [None, None, None]
    for k, r in enumerate((p0, p1, p2, p3)):
        wm, wo = owm[k * ch : (k + 1) * ch, :], owo[k * ch : (k + 1) * ch, :]
        piece = r[...]
        xs = (piece[:ch].astype(f32), piece[ch : 2 * ch].astype(f32), left_rows(piece, ch))
        for i, x in enumerate(xs):
            xt = x.T.astype(bf16)
            v = (nn(xt, wm), nn(xt, wo))
            parts[i] = v if parts[i] is None else (parts[i][0] + v[0], parts[i][1] + v[1])
    for i, n in ((0, 128), (1, 128), (2, 64)):
        at = pl.ds(pl.multiple_of(offs[i], 64), n)
        acc[at, mine] = parts[i][0][:n]
        acc[at, other] = parts[i][1][:n]
    r1 = tok[...].astype(f32) + (acc[...] + vec[2:3])
    r1o[...] = r1
    nh, _ = norm_parts(r1)
    a2o[...] = (nh * vec[3:4] + vec[4:5]).astype(bf16)


def mlp_kernel(sc, xa, xb, ca, cb, um, uo, dm, do, upb, dpa, dpb, aca, acb, pa, pb):
    mine, other = sides(sc, um.shape[1])
    bias = upb[...]
    for x, ct, dpo, aco, po in ((xa, ca, dpa, aca, pa), (xb, cb, dpb, acb, pb)):
        p = nt(x[:, mine], um[...]) + nt(x[:, other], uo[...]) + bias
        d = nt(ct[:, mine], dm[...]) + nt(ct[:, other], do[...])
        p2 = p * p
        th = jnp.tanh(GELU_A * p * (1.0 + GELU_B * p2))
        half = 0.5 * (1.0 + th)
        aco[...] = (p * half).astype(bf16)
        slope = half + 0.5 * p * (1.0 - th * th) * (GELU_A * (1.0 + 3.0 * GELU_B * p2))
        dp = (d * slope).astype(bf16)
        dpo[...] = dp
        po[:, mine] = nn(dp, um[...]).astype(bf16)
        po[:, other] = nn(dp, uo[...]).astype(bf16)


def put_grad(sc, outs, v, mat):
    n = v.shape[0] // WAYS
    if len(outs) == 1:
        for q in range(WAYS):
            outs[0][q, mat] = v[q * n : (q + 1) * n].astype(bf16)
        return
    m = v.shape[1] // 2
    first = sc[0] == 0
    for q in range(WAYS):
        a, b = v[q * n : (q + 1) * n, :m], v[q * n : (q + 1) * n, m:]
        outs[0][q, mat] = jnp.where(first, a, b).astype(bf16)
        outs[1][q, mat] = jnp.where(first, b, a).astype(bf16)


def ffn_part(sc, a, dm, do, out):
    mine, other = sides(sc, dm.shape[1])
    out[:, mine] = nn(a[...], dm[...]).astype(bf16)
    out[:, other] = nn(a[...], do[...]).astype(bf16)


def mlp_grad_one_kernel(sc, x0, x1, d0, d1, a0, a1, c0, c1, dm, do, out, ub, f0, f1):
    out[0] = (tn(d0[...], x0[...]) + tn(d1[...], x1[...])).astype(bf16)
    out[1] = (tn(a0[...], c0[...]) + tn(a1[...], c1[...])).astype(bf16)
    ub[...] = jnp.sum(d0[...].astype(f32) + d1[...].astype(f32), axis=0, keepdims=True)
    ffn_part(sc, a0, dm, do, f0)
    ffn_part(sc, a1, dm, do, f1)


def mlp_grad_two_kernel(sc, x0, x1, d0, d1, a0, a1, c0, c1, one, ubone, dm, do, *outs):
    *grads, ub, f0, f1 = outs
    put_grad(sc, grads, one[0].astype(f32) + tn(d0[...], x0[...]) + tn(d1[...], x1[...]), 0)
    put_grad(sc, grads, one[1].astype(f32) + tn(a0[...], c0[...]) + tn(a1[...], c1[...]), 1)
    ub[...] = ubone[...] + jnp.sum(d0[...].astype(f32) + d1[...].astype(f32), axis=0, keepdims=True)
    ffn_part(sc, a0, dm, do, f0)
    ffn_part(sc, a1, dm, do, f1)


def norm2_kernel(sc, own, core, far, r1, cot, vec, owm, owo, dro, dmo, sums, p0, p1, p2, p3):
    t = sc[2]
    sums[...] = jnp.zeros_like(sums)
    dn2 = own[...].astype(f32) + core[...].astype(f32) + far[...].astype(f32)
    nh, rs = norm_parts(r1[...])
    ct = cot[...].astype(f32)
    sums[0:1] = jnp.sum(dn2 * nh, axis=0, keepdims=True)
    sums[1:2] = jnp.sum(dn2, axis=0, keepdims=True)
    dr = ct + norm_back(nh, rs, dn2 * vec[3:4])
    dro[...] = dr
    dm = dr.astype(bf16)
    dmo[...] = dm
    sums[2:3] = jnp.sum(dm.astype(f32), axis=0, keepdims=True)
    sums[3:4] = jnp.sum(ct, axis=0, keepdims=True)
    offs = share_offsets(t)
    ch, half = owm.shape[0] // WAYS, owm.shape[1]
    mine, other = sides(sc, half)
    low = lax.broadcasted_iota(jnp.int32, (ch // 2, 128), 1) < 64
    at = [pl.ds(pl.multiple_of(offs[i], 64), n) for i, n in ((0, 128), (1, 128), (2, 64))]
    dms = [(dmo[a, mine], dmo[a, other]) for a in at]
    dms[2] = tuple(jnp.concatenate([v, v], axis=0) for v in dms[2])
    for k, o in enumerate((p0, p1, p2, p3)):
        wm, wo = owm[k * ch : (k + 1) * ch, :], owo[k * ch : (k + 1) * ch, :]
        vs = [nt(wm, a) + nt(wo, b) for a, b in dms]
        o[0:ch] = vs[0].astype(bf16)
        o[ch : 2 * ch] = vs[1].astype(bf16)
        o[2 * ch :] = jnp.where(low, vs[2][: ch // 2], vs[2][ch // 2 :]).astype(bf16)


def out_grad_kernel(sc, p0, p1, p2, p3, dm, *outs):
    t = sc[2]
    offs = share_offsets(t)
    ch = p0.shape[0] * 2 // 5
    da = dm[pl.ds(pl.multiple_of(offs[0], 64), 128), :]
    db = dm[pl.ds(pl.multiple_of(offs[1], 64), 128), :]
    dc = dm[pl.ds(pl.multiple_of(offs[2], 64), 64), :]
    vs = []
    for r in (p0, p1, p2, p3):
        piece = r[...]
        left = left_rows(piece, ch)[:, :64].astype(bf16)
        vs.append(nn(piece[:ch], da) + nn(piece[ch : 2 * ch], db) + nn(left, dc))
    put_grad(sc, outs, jnp.concatenate(vs, axis=0), 0)


def ungate_kernel(sc, p0, p1, p2, p3, g0, ys, u, cols, dyo, dgo, so, d0, d1, d2, d3, pk, dg):
    c, t = sc[1], sc[2]
    ch = u.shape[1]
    cs = ch // WAYS

    def put(j, v):
        dg[j // 2, :, (j % 2) * 128 : (j % 2) * 128 + 128] = v

    unpack_all(t, ch, (p0, p1, p2, p3), pk, put)
    skip = cols[:, 5:6][:ch]
    tot = None
    for b in range(5):
        g = dg[b]
        uu = u[b].astype(f32)
        dgo[b] = g * (ys[b].astype(f32) + skip * uu)
        dy = g * g0[b]
        v = jnp.sum(dy * uu, axis=1, keepdims=True)
        tot = v if tot is None else tot + v
        dyo[b] = dy.astype(bf16)
    so[...] = tot
    for k, o in enumerate((d0, d1, d2, d3)):
        for b in range(5):
            o[b] = dyo[b, pl.ds(pl.multiple_of((c ^ k) * cs, 16), cs), :]


def conv_back_kernel(sc, d0, d1, d2, d3, ws, hs, fh, fl, gh, gl, dho, o0, o1, o2, o3, un, dy, dw, dh):
    c = sc[1]
    cs = d0.shape[1]
    for k, r in enumerate((d0, d1, d2, d3)):
        un[pl.ds((c ^ k) * 5, 5)] = r[...]
    da = un[...].reshape(TREE_BLK * cs, BLOCK)
    dy[0:TREE_BLK] = (nt(da, gh[...]) + nt(da, gl[...])).reshape(TREE_BLK, cs, 2 * BLOCK)
    zero = jnp.zeros((cs, BLOCK), f32)
    zz = jnp.zeros((cs, 2 * BLOCK), f32)
    first_leaf = TRUNK + BRANCHES
    sum_b = lax.fori_loop(TRUNK, first_leaf, lambda k, a: a + dy[k], zz)
    sum_l = lax.fori_loop(first_leaf, TREE_BLK, lambda k, a: a + dy[k], zz)
    dy[TREE_BLK] = sum_b
    dy[TREE_BLK + 1] = sum_l
    for i in range(BRANCHES):
        dy[TREE_BLK + 2 + i] = zz

    @pl.loop(0, LEAVES)
    def _(i):
        k = TREE_BLK + 2 + leaf_parent(sc, i) - TRUNK
        dy[k] = dy[k] + dy[first_leaf + i]


    def put(ref, k, acc):
        ref[k, :, :BLOCK] = acc[0]
        ref[k, :, BLOCK:] = acc[1]

    @pl.loop(0, TRUNK)
    def _(j):
        acc = lax.fori_loop(j, TRUNK, lambda q, a: mul_conj(a, hs[q - j], dy[q]), (zero, zero))
        acc = mul_conj(acc, hs[8 - j], dy[TREE_BLK])
        put(dw, j, mul_conj(acc, hs[9 - j], dy[TREE_BLK + 1]))

    @pl.loop(0, BRANCHES)
    def _(i):
        k = TRUNK + i
        acc = mul_conj((zero, zero), hs[0], dy[k])
        put(dw, k, mul_conj(acc, hs[1], dy[TREE_BLK + 2 + i]))

    @pl.loop(first_leaf, TREE_BLK)
    def _(k):
        put(dw, k, mul_conj((zero, zero), hs[0], dy[k]))


    @pl.loop(0, TRUNK)
    def _(d):
        put(dh, d, lax.fori_loop(d, TRUNK, lambda q, a: mul_conj(a, ws[q - d], dy[q]), (zero, zero)))

    put(dh, 8, (zero, zero))
    put(dh, 9, (zero, zero))

    def more(d, k, q):
        acc = (dh[d, :, :BLOCK], dh[d, :, BLOCK:])
        put(dh, d, mul_conj(acc, ws[k], dy[q]))

    @pl.loop(1, 9)
    def _(d):
        more(d, 8 - d, TREE_BLK)

    @pl.loop(2, 10)
    def _(d):
        more(d, 9 - d, TREE_BLK + 1)

    @pl.loop(TRUNK, TREE_BLK)
    def _(k):
        more(0, k, k)

    @pl.loop(0, BRANCHES)
    def _(i):
        more(1, TRUNK + i, TREE_BLK + 2 + i)

    for d in range(NPATH):
        thi, tlo = two(dh[d])
        dho[:, d * BLOCK : (d + 1) * BLOCK] = nt(thi, fh[...]) + nt(tlo, fh[...]) + nt(thi, fl[...])

    sg = signs()

    def own(k):
        w = dw[k]
        return jnp.concatenate([-(sg * w[:, BLOCK:]), sg * w[:, :BLOCK]], axis=1)

    @pl.loop(0, TRUNK - 1)
    def _(k):
        dy[k] = own(k) + dw[k + 1]

    dy[TRUNK - 1] = lax.fori_loop(TRUNK, first_leaf, lambda k, a: a + dw[k], own(TRUNK - 1))

    @pl.loop(TRUNK, TREE_BLK)
    def _(k):
        dy[k] = own(k)

    @pl.loop(0, LEAVES)
    def _(i):
        k = leaf_parent(sc, i)
        dy[k] = dy[k] + dw[first_leaf + i]

    shi, slo = two(dy[0:TREE_BLK].reshape(TREE_BLK * cs, 2 * BLOCK))
    du = nt(shi, fh[...]) + nt(slo, fh[...]) + nt(shi, fl[...])
    un[...] = du.astype(bf16).reshape(TREE_BLK, cs, BLOCK)
    for k, o in enumerate((o0, o1, o2, o3)):
        o[...] = un[pl.ds((c ^ k) * 5, 5)]


def unconv_kernel(sc, u0, u1, u2, u3, dyv, dg0, gv, z, zr, cols, dzo, rims, cg, dus, rs, acc, zc):
    c = sc[1]
    ch = dyv.shape[1]
    cs = ch // WAYS
    cv = cols[...]
    w0, w1, w2 = (cv[:, i : i + 1] for i in range(3))
    skip = cv[:ch, 5:6]
    lane = lax.broadcasted_iota(jnp.int32, (3 * ch, 128), 1)
    rs[...] = jnp.zeros_like(rs)
    acc[...] = jnp.zeros_like(acc)

    def fold(i, v):
        acc[i] = acc[i] + (v[:, :128] + v[:, 128:])

    zc[...] = jnp.zeros_like(zc)
    zc[0:16] = zr[...]
    zcol = zc[...].T

    for b in range(5):
        for k, r in enumerate((u0, u1, u2, u3)):
            dus[pl.ds(pl.multiple_of((c ^ k) * cs, 16), cs), :] = r[b]
        du = dus[...].astype(f32) + skip * dyv[b].astype(f32)
        sv = gv[b]
        ds = jnp.concatenate([dg0[b], du * sv[ch:], du * sv[:ch]], axis=0)
        zv = z[b].astype(f32)
        far, near = zcol[:, 2 * b : 2 * b + 1], zcol[:, 2 * b + 1 : 2 * b + 2]
        r1, r2 = pltpu.roll(ds, BLOCK - 1, 1), pltpu.roll(ds, BLOCK - 2, 1)
        n1 = jnp.concatenate([r1[:, :128], jnp.where(lane == 127, 0.0, r1[:, 128:])], axis=1)
        n2 = jnp.concatenate([r2[:, :128], jnp.where(lane >= 126, 0.0, r2[:, 128:])], axis=1)
        dzo[b] = w0 * ds + w1 * n1 + w2 * n2
        d0, d1 = ds[:, 0:1], ds[:, 1:2]
        fold(0, ds)
        fold(1, ds * zv)
        fold(2, n1 * zv)
        fold(3, n2 * zv)
        acc[2] = acc[2] + jnp.where(lane == 0, d0 * near, 0.0)
        acc[3] = acc[3] + jnp.where(lane == 0, d0 * far + d1 * near, 0.0)
        rs[...] = rs[...] + jnp.where(lane == 2 * b, w2 * d0, jnp.where(lane == 2 * b + 1, w1 * d0 + w2 * d1, 0.0))

    rims[...] = rs[...].T[:16]
    out = jnp.zeros(lane.shape, f32)
    for i in range(4):
        out = jnp.where(lane == i, jnp.sum(acc[i], axis=1, keepdims=True), out)
    cg[...] = out


def dz_kernel(sc, dzo, r0, r1, r2, r3, pick, dz, p0, p1, p2, p3, ib, rall, rt, pk):
    c, t = sc[1], sc[2]
    rows = dzo.shape[1]
    for k, r in enumerate((r0, r1, r2, r3)):
        rall[pl.ds(pl.multiple_of((c ^ k) * 16, 16), 16), :] = r[...]
    got = lax.dot_general(
        pick[...], rall[...], (((1,), (0,)), ((), ())), precision=exact_mode, preferred_element_type=f32
    )
    rt[...] = got.T
    lane = lax.broadcasted_iota(jnp.int32, (rows, 128), 1)
    tot = None
    for b in range(5):
        add = jnp.where(lane >= 126, pltpu.roll(rt[...], 126 - 2 * b, 1), 0.0)
        lo = dzo[b, :, :128].astype(bf16)
        hi = (dzo[b, :, 128:] + add).astype(bf16)
        dz[b, :, :128] = lo
        dz[b, :, 128:] = hi
        v = jnp.sum(lo.astype(f32) + hi.astype(f32), axis=1, keepdims=True)
        tot = v if tot is None else tot + v
    ib[...] = tot
    pack_all(t, rows, lambda j: dz[j // 2, :, (j % 2) * 128 : (j % 2) * 128 + 128].astype(f32), pk, (p0, p1, p2, p3))


def in_grad_kernel(sc, dz, a1, wt, ib, vec, *outs):
    acc = None
    for b in range(5):
        v = nn(dz[b], a1[b * BLOCK : (b + 1) * BLOCK, :])
        acc = v if acc is None else acc + v
    sums = outs[-1]
    if len(outs) == 2:
        outs[0][...] = acc
    else:
        n = acc.shape[1] // 2
        first = sc[0] == 0
        outs[0][...] = jnp.where(first, acc[:, :n], acc[:, n:])
        outs[1][...] = jnp.where(first, acc[:, n:], acc[:, :n]).astype(bf16)
    w = wt[...].astype(f32)
    gsum = jnp.sum(w * acc, axis=0, keepdims=True)
    bsum = jnp.sum(w * ib[...], axis=0, keepdims=True)
    sums[...] = jnp.zeros_like(sums)
    sums[0:1] = (gsum - vec[1:2] * bsum) / vec[0:1]
    sums[1:2] = bsum


FILT_ROWS = 112


def put_row(out, at, row):
    n = row.shape[1]
    k = -(-n // 128)
    for j in range(k):
        w = min(128, n - 128 * j)
        out[pl.ds(at + j, 1), :w] = row[:, 128 * j : 128 * j + w]
    return k


def pack_kernel(sc, sums1, sums2, ub, filt, fo, cg, ib, skip, out, colt):
    c, t = sc[1], sc[2]
    out[...] = jnp.zeros_like(out)
    for i in range(4):
        put_row(out, 8 * i, sums2[i : i + 1])
    n = ub.shape[1] // WAYS
    for q in range(WAYS):
        put_row(out, 32 + 2 * (WAYS * c + (t ^ q)), ub[0:1, q * n : (q + 1) * n])
    out[64 : 64 + FILT_ROWS, : filt.shape[1]] = filt[...]
    at = 64 + FILT_ROWS
    put_row(out, at, sums1[0:1])
    put_row(out, at + 8, sums1[1:2])
    at += 16
    lane = lax.broadcasted_iota(jnp.int32, cg.shape, 1)
    colt[...] = jnp.where(lane == 4, ib[...], cg[...]).T
    m = cg.shape[0]
    for j in range(-(-m // 128)):
        w = min(128, m - 128 * j)
        out[at : at + 8, :w] = colt[0:8, 128 * j : 128 * j + w]
        at += 8
    ch = skip.shape[0]
    put_row(out, at, jnp.broadcast_to(skip[...], (ch, 128)).T[0:1])
    at += 8
    cs = fo.shape[0]
    out[pl.ds(at + c * cs, cs), : fo.shape[1]] = fo[...]


def filter_back_kernel(sc, dt, emb, fit, fmt, fc, fo, fm, out, fog):
    def three(dot, a, b):
        (ah, al), (bh, bl) = two(a), two(b)
        return dot(ah, bh) + dot(ah, bl) + dot(al, bh)

    n, ne, cs = fm.shape[0], emb.shape[0], fo.shape[0]
    fov, fmv, frv = fo[...], fm[...], fc[:, 0:1]

    def step(d, acc):
        a_fo, a_fm, a_fi, a_b1, a_b2, a_fr = acc
        sl = pl.ds(d * BLOCK, BLOCK)
        q1, one, c1, q2, mid, c2, lag, rate = filter_chunk(d, sl, emb, fit, fmt, fc)
        draw = dt[:, sl] * (jnp.exp(-lag * rate[:cs]) + 0.05)
        a_fo = a_fo + three(nt, draw, mid)
        da2 = three(tn, fov, draw) * c2
        dp2 = da2 * frv
        a_fm = a_fm + three(nt, one, dp2)
        da1 = three(nn, fmv, dp2) * c1
        dp1 = da1 * frv
        a_fi = a_fi + three(nt, emb[:, sl], dp1)
        return a_fo, a_fm, a_fi, a_b1 + dp1, a_b2 + dp2, a_fr + (da2 * q2 + da1 * q1)

    zero = jnp.zeros((n, BLOCK), f32)
    init = (jnp.zeros(fog.shape, f32), jnp.zeros((n, n), f32), jnp.zeros((ne, n), f32), zero, zero, zero)
    acc = init
    for d in range(PATH // BLOCK):
        acc = step(d, acc)
    a_fo, a_fm, a_fi, b1, b2, fg = acc
    fog[...] = a_fo
    out[...] = jnp.zeros_like(out)
    out[0:n] = a_fm
    out[n : n + ne] = a_fi
    cols = [jnp.sum(v, axis=1, keepdims=True) for v in (b1, b2, fg)]
    lane = lax.broadcasted_iota(jnp.int32, (n, 128), 1)
    m = jnp.where(lane == 0, cols[0], jnp.where(lane == 1, cols[1], jnp.where(lane == 2, cols[2], 0.0)))
    out[n + ne : n + ne + 8] = m.T[0:8]


def norm1_kernel(sc, p0, p1, p2, p3, w0, wr, tok, dr, vec, out, acc):
    t = sc[2]
    rows = w0.shape[0]
    offs = share_offsets(t)
    parts = [None, None, None]
    for k, r in enumerate((p0, p1, p2, p3)):
        w = w0[...] if k == 0 else wr[k - 1]
        piece = r[...]
        xs = (piece[:rows].astype(f32), piece[rows : 2 * rows].astype(f32), left_rows(piece, rows))
        for i, x in enumerate(xs):
            v = nn(x.T.astype(bf16), w)
            parts[i] = v if parts[i] is None else parts[i] + v
    acc[pl.ds(pl.multiple_of(offs[0], 64), 128), :] = parts[0]
    acc[pl.ds(pl.multiple_of(offs[1], 64), 128), :] = parts[1]
    acc[pl.ds(pl.multiple_of(offs[2], 64), 64), :] = parts[2][:64]
    nh, rs = norm_parts(tok[...].astype(f32))
    out[...] = (dr[...] + norm_back(nh, rs, acc[...] * vec[0:1])).astype(bf16)


def matrices_kernel(sc, m0, m1, m2, m3, upo, downo, outo, rows):
    c = sc[1]
    n = m0.shape[1]
    for k, m in enumerate((m0, m1, m2, m3)):
        at = pl.ds(pl.multiple_of((c ^ k) * n, 64), n)
        rows[at, :] = m[0].astype(f32)
        downo[at, :] = m[1].astype(f32)
    upo[...] = rows[...].T
    outo[...] = (m0[2].astype(f32) + m1[2].astype(f32)) + (m2[2].astype(f32) + m3[2].astype(f32))


def layer_out_kernel(sc, r1, own, core, far, vec, out):
    ffn = own[...].astype(f32) + core[...].astype(f32) + far[...].astype(f32)
    out[...] = (r1[...] + ffn + vec[6:7]).astype(bf16)


def body(
    shard_count,
    tokens,
    parents,
    norm1_gain,
    norm1_bias,
    in_weight,
    in_bias,
    conv_weight,
    conv_bias,
    filt_in,
    filt_bias1,
    filt_mid,
    filt_bias2,
    sine_freq,
    filt_out,
    skip_gain,
    out_weight,
    out_bias,
    norm2_gain,
    norm2_bias,
    up_weight,
    up_bias,
    down_weight,
    down_bias,
    cotangent,
):
    rows, width = tokens.shape
    ch = skip_gain.shape[0]
    cs = ch // WAYS
    ch3 = 3 * ch
    ffq = up_bias.shape[0]
    ffs = ffq // WAYS
    share = rows // WAYS
    d_part = in_weight.shape[0]
    s_id = lax.axis_index("shards")
    c_id = lax.axis_index("context")
    t_id = lax.axis_index("tensor")
    pair = shard_count == 2

    def gather_shards(x, axis):
        if not pair:
            return lax.all_gather(x, "shards", axis=axis, tiled=True)
        o = lax.ppermute(x, "shards", [(0, 1), (1, 0)])
        lo = jnp.where(s_id == 0, x, o)
        hi = jnp.where(s_id == 0, o, x)
        return jnp.concatenate([lo, hi], axis=axis)

    par = parents[0]
    all_par = jnp.concatenate(
        [jnp.arange(-1, TRUNK - 1, dtype=jnp.int32), jnp.full((BRANCHES,), TRUNK - 1, jnp.int32), TRUNK - 1 + par[1 + BRANCHES :]]
    )
    own_par = lax.dynamic_slice_in_dim(all_par, c_id * 5, 5, 0)
    side = s_id if pair else jnp.zeros_like(s_id)
    sc = jnp.concatenate([jnp.stack([side, c_id, t_id]).astype(jnp.int32), own_par, par]).astype(jnp.int32)

    def swap_y(x):
        return lax.ppermute(x, "shards", [(0, 1), (1, 0)])

    wt_part = jnp.transpose(in_weight, (1, 2, 0)).reshape(ch3, d_part)
    wt = gather_shards(wt_part, 1)
    rim_tok = tokens.reshape(5, BLOCK, width)[:, BLOCK - 2 :, :]
    rims_in = [rim_tok] + [swap(rim_tok, "context", k) for k in (1, 2, 3)]
    up_t = lax.dynamic_slice_in_dim(up_weight, c_id * ffs, ffs, 1).T
    down_c = lax.dynamic_slice_in_dim(down_weight, c_id * ffs, ffs, 0)
    bias_c = lax.dynamic_slice_in_dim(up_bias, c_id * ffs, ffs, 0)
    b_hi, b_mid = two(bias_c)
    b_lo = (bias_c - b_hi.astype(f32) - b_mid.astype(f32)).astype(bf16)
    wide = d_part >= ffs
    if wide:
        b_rows = jnp.stack([b_hi, b_mid, b_lo] + [jnp.zeros_like(b_hi)] * 13)
        b_rows = jnp.concatenate([b_rows, jnp.zeros((16, d_part - ffs), bf16)], axis=1)
        two_mats = jnp.concatenate([out_weight, up_t, b_rows])
    else:
        two_mats = jnp.concatenate([out_weight, up_t])
    parts_a = [two_mats] + [swap(two_mats, "tensor", k) for k in (1, 2, 3)]
    fo = gather_shards(filt_out, 0)
    fo_t = lax.dynamic_slice_in_dim(fo, c_id * cs, cs, 1).astype(f32).T

    vec = jnp.concatenate(
        [norm1_gain, norm1_bias, out_bias, norm2_gain, norm2_bias, down_bias, down_bias, down_bias]
    ).reshape(8, width)
    skip3 = jnp.concatenate([skip_gain, skip_gain, skip_gain])
    flat_rows = [conv_weight.reshape(-1), conv_bias.reshape(-1), in_bias.reshape(-1), skip3, jnp.zeros((2 * ch3,), f32)]
    col_rows = jnp.concatenate(flat_rows).reshape(8, ch3)
    fh, fl, gh, gl = (jnp.asarray(a) for a in dft_tables())

    embedded = embed_table((filt_in.shape[0] - 1) // 2)
    n_in, fw = filt_in.shape
    pad = 40 - n_in
    emb = jnp.asarray(np.concatenate([embedded, np.zeros((pad, PATH), np.float32)]))
    fit = jnp.concatenate([filt_in, jnp.zeros((pad, fw), f32)]).T
    fmt = filt_mid.T
    channel = (t_id * ch + c_id * cs).astype(f32) + jnp.arange(fw, dtype=f32)
    slow, fast = math.log(0.01) / 1.5, math.log(0.01) / 0.3
    rates = jnp.abs(slow + (fast - slow) * channel / (ch * WAYS - 1))
    fc = jnp.stack([sine_freq, filt_bias1, filt_bias2, rates] + [rates] * 4, axis=1)

    nb, B = 5, BLOCK
    piece = ((nb, cs, B), bf16)
    a1, cols = call(
        norm1_fwd_kernel,
        [((rows, width), bf16), ((ch3, 128), f32)],
        3,
        [pltpu.VMEM((128, ch3), f32)],
    )(sc, tokens, col_rows, vec)
    z, zr, g0, gv, u, u0, u1, u2, u3 = call(
        proj_kernel,
        [((nb, ch3, B), bf16), ((16, ch3), f32), ((nb, ch, B), f32), ((nb, 2 * ch, B), f32), ((nb, ch, B), bf16)]
        + [piece] * 4,
        8,
        [pltpu.VMEM((TREE_BLK, 2, width), bf16)],
    )(sc, a1, *rims_in, wt, cols, vec)

    def ctx(p):
        return (p[0], swap(p[1], "context", 1), swap(p[2], "context", 2), swap(p[3], "context", 3))

    def ten(p):
        return (p[0], swap(p[1], "tensor", 1), swap(p[2], "tensor", 2), swap(p[3], "tensor", 3))

    un = ctx((u0, u1, u2, u3))
    (taps,) = call(filter_kernel, [((cs, PATH), f32)], 5)(after(sc, u0), emb, fit, fmt, fc, fo_t)

    def columns(parts, *deps):
        m = jnp.concatenate(parts, axis=0)
        if pair:
            return m, swap_y(after(m, *deps))
        m = lax.all_gather(m, "shards", axis=1, tiled=True)
        return m[:, : width // 2], m[:, width // 2 :]

    down_now = after(down_c, u0)
    parts_b = [down_now] + [swap(down_now, "tensor", k) for k in (1, 2, 3)]
    parts_a = after(tuple(parts_a), u0)
    ow = columns([p[:ch] for p in parts_a])
    up = columns([p[ch : ch + ffs] for p in parts_a], ow[0])
    if wide:
        up_b = jnp.concatenate([p[ch + ffs : ch + ffs + 3, :ffs].astype(f32).sum(0) for p in parts_a]).reshape(1, ffq)
    else:
        up_b = jnp.concatenate([bias_c] + [swap(bias_c, "tensor", k) for k in (1, 2, 3)]).reshape(1, ffq)
    spec = ((TREE_BLK, cs, 2 * B), f32)
    ws, hs, y0, y1, y2, y3 = call(
        conv_kernel,
        [spec, ((NPATH, cs, 2 * B), f32)] + [piece] * 4,
        9,
        [pltpu.VMEM((TREE_BLK, cs, B), bf16), pltpu.VMEM((TREE_BLK, cs, 2 * B), f32)],
    )(sc, *un, taps, fh, fl, gh, gl)
    yn = ctx((y0, y1, y2, y3))
    tok_share = lax.dynamic_slice_in_dim(tokens, t_id * share, share, 0)
    cot_share = lax.dynamic_slice_in_dim(cotangent, t_id * share, share, 0)
    tok_share, cot_share = after((tok_share, cot_share), u0)

    packs = (5 * ch // 2, 128)
    packed_out = [(packs, bf16)] * 4
    ys, *gp = call(
        gate_kernel,
        [((nb, ch, B), bf16)] + packed_out,
        7,
        [pltpu.VMEM((nb, ch, B), bf16), pltpu.VMEM((nb, ch, B), f32), pltpu.VMEM((WAYS,) + packs, bf16)],
    )(sc, *yn, g0, after(u, ow), cols)
    gn = ten(gp)
    cot_share = after(cot_share, ys)
    cot1 = swap(cot_share, "context", 1)
    cot2 = swap(cot_share, "context", 2)
    down = columns(after(tuple(parts_b), ys))

    sh = (share, width)
    r1, a2 = call(mix_kernel, [(sh, f32), (sh, bf16)], 8, [pltpu.VMEM(sh, f32)])(
        sc, *gn, *ow, after(tok_share, up_b, up), vec
    )

    x1 = swap(a2, "context", 1)
    x2 = swap(a2, "context", 2)
    cot3 = swap(after(cot2, a2), "context", 1)
    odd = c_id & 1
    wt_half = after(lax.dynamic_slice_in_dim(wt, odd * (ch3 // 2), ch3 // 2, 0), a2)
    w_got = [swap(wt_half, "tensor", k) for k in (1, 2, 3)]
    mlp = call(mlp_kernel, [((share, ffq), bf16)] * 4 + [(sh, bf16)] * 2, 9)
    dp0, dp1, ac0, ac1, n0, n1 = mlp(sc, a2, x1, cot_share, cot1, *up, *down, up_b)
    one, ub_one, f0, f1 = call(mlp_grad_one_kernel, [((2, ffq, width), bf16), ((1, ffq), f32), (sh, bf16), (sh, bf16)], 10)(
        after(sc, n0), a2, x1, dp0, dp1, ac0, ac1, cot_share, cot1, *down
    )
    x2 = after(x2, one, w_got[0], w_got[2])
    x3 = swap(x2, "context", 1)
    dp2, dp3, ac2, ac3, n2, n3 = mlp(sc, x2, x3, cot2, cot3, *up, *down, up_b)
    one, ub_one, f0, f1 = after((one, ub_one, f0, f1), n2)

    def sum_context(q0, q1, q2, q3):
        a = swap(q1, "context", 1)
        b = swap(q3, "context", 1)
        mid = (q2.astype(f32) + b.astype(f32)).astype(bf16)
        return q0, a, swap(mid, "context", 2)

    dn = sum_context(n0, n1, n2, n3)
    n_grad = 2 if pair else 1
    gcol = width // n_grad
    *mg, ub, f2, f3 = call(
        mlp_grad_two_kernel, [((WAYS, 2, ffs, gcol), bf16)] * n_grad + [((1, ffq), f32), (sh, bf16), (sh, bf16)], 12
    )(after(sc, n2), x2, x3, dp2, dp3, ac2, ac3, cot2, cot3, one, ub_one, *down)
    dn = dn[:2] + (after(dn[2], mg, w_got[1]),)
    dr1, dm, sums2, *dgp = call(norm2_kernel, [(sh, f32), (sh, bf16), ((8, width), f32)] + packed_out, 8)(
        sc, *dn, r1, cot_share, vec, *ow
    )
    mg, f1, f3, w_got = after((mg, f1, f3, w_got), dm)
    w_got = jnp.stack(w_got)
    dgn = ten(dgp)

    og = call(out_grad_kernel, [((WAYS, 1, ch, gcol), bf16)] * n_grad, 5)(sc, *gn, dm)
    fs = sum_context(f0, f1, f2, f3)
    def over_shards(x):
        if pair:
            mine, theirs = x
            return (mine.astype(f32) + swap_y(theirs).astype(f32)).astype(bf16)
        return lax.psum_scatter(x[0].astype(f32), "shards", scatter_dimension=3, tiled=True).astype(bf16)

    def over_tensor(x, *deps):
        got = [swap(x[k], "tensor", k) for k in (1, 2, 3)]
        return x[0], got

    def total(x, got):
        v = x.astype(f32)
        for g in got:
            v = v + g.astype(f32)
        return v.astype(bf16)

    dy, dg0, skip_g, d0, d1, d2, d3 = call(
        ungate_kernel,
        [((nb, ch, B), bf16), ((nb, ch, B), f32), ((ch, 1), f32)] + [piece] * 4,
        8,
        [pltpu.VMEM((WAYS,) + packs, bf16), pltpu.VMEM((nb, ch, B), f32)],
    )(sc, *dgn, g0, ys, u, cols)
    og = after(og, dy)
    fs = after(fs, dy)
    (layer_out,) = call(layer_out_kernel, [(sh, bf16)], 5)(sc, r1, *fs, vec)
    mg_y = over_shards(mg)
    og_y = over_shards(og)
    dn_ = ctx((d0, d1, d2, d3))
    dtaps, e0, e1, e2, e3 = call(
        conv_back_kernel,
        [((cs, PATH), f32)] + [piece] * 4,
        10,
        [
            pltpu.VMEM((TREE_BLK, cs, B), bf16),
            pltpu.VMEM((TREE_BLK + 6, cs, 2 * B), f32),
            pltpu.VMEM((TREE_BLK, cs, 2 * B), f32),
            pltpu.VMEM((NPATH, cs, 2 * B), f32),
        ],
    )(sc, *dn_, ws, hs, fh, fl, gh, gl)
    en = ctx((e0, e1, e2, e3))
    w_other = swap(after(w_got, dy), "context", 1)
    w_rest = jnp.where(odd == 0, jnp.concatenate([w_got, w_other], axis=1), jnp.concatenate([w_other, w_got], axis=1))
    filt, fo_g = call(filter_back_kernel, [((FILT_ROWS, fw), f32), ((cs, fw), f32)], 7)(
        after(sc, en[1]), dtaps, emb, fit, fmt, fc, fo_t, filt_mid
    )
    dzo, rims, cg = call(
        unconv_kernel,
        [((nb, ch3, B), f32), ((16, ch3), f32), ((ch3, 128), f32)],
        10,
        [pltpu.VMEM((ch, B), bf16), pltpu.VMEM((ch3, 128), f32), pltpu.VMEM((4, ch3, 128), f32), pltpu.VMEM((128, ch3), f32)],
    )(sc, en[0], en[1], after(en[2], filt, mg_y), en[3], dy, dg0, gv, z, zr, cols)
    filt, fo_g, w_rest, og_y = after((filt, fo_g, w_rest, og_y), rims)
    mg_own, mg_got = over_tensor(mg_y)
    og_own, og_got = over_tensor(og_y)
    rn = ctx((rims, rims, rims, rims))
    col = jnp.arange(WAYS * 16, dtype=jnp.int32)
    col_blk = (col // 16) * 5 + (col % 16) // 2
    col_ok = (col % 16) < 10
    col_par = jnp.where(col_ok, all_par[jnp.minimum(col_blk, TREE_BLK - 1)], -2)
    row = jnp.arange(128, dtype=jnp.int32)
    pick = (
        (row[:, None] < 10)
        & (col_par[None, :] == c_id * 5 + row[:, None] // 2)
        & (col[None, :] % 2 == row[:, None] % 2)
    ).astype(f32)
    dpacks = (5 * ch3 // 2, 128)
    dz, q0, q1, q2, q3, ib = call(
        dz_kernel,
        [((nb, ch3, B), bf16)] + [(dpacks, bf16)] * 4 + [((ch3, 1), f32)],
        6,
        [pltpu.VMEM((WAYS * 16, ch3), f32), pltpu.VMEM((ch3, 128), f32), pltpu.VMEM((WAYS,) + dpacks, bf16)],
    )(sc, dzo, *rn, pick)
    qn = ten((q0, q1, q2, q3))
    if pair:
        mine, theirs, sums1 = call(
            in_grad_kernel,
            [((ch3, d_part), f32), ((ch3, d_part), bf16), ((8, width), f32)],
            5,
        )(sc, dz, a1, wt, ib, vec)
        ih = mine + swap_y(theirs).astype(f32)
    else:
        ig, sums1 = call(in_grad_kernel, [((ch3, width), f32), ((8, width), f32)], 5)(sc, dz, a1, wt, ib, vec)
        ih = lax.psum_scatter(ig, "shards", scatter_dimension=1, tiled=True)

    (tokens_grad,) = call(norm1_kernel, [(sh, bf16)], 9, [pltpu.VMEM(sh, f32)])(
        sc, *qn, wt, w_rest, tok_share, dr1, vec
    )
    ih = ih + swap(ih.astype(bf16), "context", 1).astype(f32)
    far = after(swap(ih.astype(bf16), "context", 2), tokens_grad)
    in_grad = jnp.transpose((ih + far.astype(f32)).reshape(3, ch, d_part), (2, 0, 1))

    mg_got, og_got = after((mg_got, og_got), qn[1])
    mats = jnp.concatenate([total(mg_own, mg_got), total(og_own, og_got)], axis=0)
    m1, m2 = swap(mats, "context", 1), swap(mats, "context", 2)
    m3 = swap(m2, "context", 1)
    up_grad, down_grad, out_grad = call(
        matrices_kernel,
        [((d_part, ffq), f32), ((ffq, d_part), f32), ((ch, d_part), f32)],
        4,
        [pltpu.VMEM((ffq, d_part), f32)],
    )(after(sc, tokens_grad), mats, m1, m2, m3)

    n_col = 8 * (-(-ch3 // 128))
    n_all = 64 + FILT_ROWS + 16
    (small,) = call(pack_kernel, [((n_all + n_col + 8 + ch, 128), f32)], 8, [pltpu.VMEM((128, ch3), f32)])(
        sc, sums1, sums2, ub, filt, fo_g, cg, ib, skip_g
    )
    small = small + swap(small, "context", 1)
    small = small + swap(small, "context", 2)
    small = small + swap_y(small) if pair else lax.psum(small, "shards")
    late = small[n_all:]
    early = small[:n_all]
    early = early + swap(early, "tensor", 1)
    early = early + after(swap(early, "tensor", 2), tokens_grad)
    first = early[64 + FILT_ROWS :]

    def row(x, at):
        return x[at : at + 8].reshape(-1)[:width]

    hid = early[32:64].reshape(WAYS, WAYS, 256)[:, :, :ffs]
    up_bias_grad = lax.dynamic_index_in_dim(hid, t_id, 1, keepdims=False).reshape(ffq)
    fil = early[64 : 64 + FILT_ROWS, :fw]
    fo_own = lax.dynamic_slice_in_dim(late[8 + n_col :, :fw].T, s_id * filt_out.shape[0], filt_out.shape[0], 0)
    colsum = late[:n_col].reshape(n_col // 8, 8, 128).transpose(1, 0, 2).reshape(8, -1)[:, :ch3]
    skip_sum = late[n_col : 8 + n_col].reshape(-1)[:ch]
    conv_all = colsum.reshape(8, 3, ch)
    return (
        layer_out,
        tokens_grad,
        row(first, 0),
        row(first, 8),
        in_grad,
        conv_all[4],
        conv_all[1:4],
        conv_all[0],
        fil[fw : fw + n_in],
        fil[fw + 40],
        fil[:fw],
        fil[fw + 41],
        fil[fw + 42],
        fo_own,
        skip_sum,
        out_grad,
        row(early, 16),
        row(early, 0),
        row(early, 8),
        up_grad,
        up_bias_grad,
        down_grad,
        row(early, 24),
    )


def solution(mesh):
    return jax.shard_map(
        functools.partial(body, mesh.shape["shards"]),
        mesh=mesh,
        in_specs=(
            P(("shards", "context"), None),
            P("shards", None),
            P(),
            P(),
            P("shards", None, "tensor"),
            P(None, "tensor"),
            P(None, None, "tensor"),
            P(None, "tensor"),
            P(),
            P(),
            P(),
            P(),
            P(),
            P("shards", "tensor"),
            P("tensor"),
            P("tensor", "shards"),
            P(),
            P(),
            P(),
            P("shards", "tensor"),
            P("tensor"),
            P("tensor", "shards"),
            P(),
            P(("shards", "context"), None),
        ),
        out_specs=(
            P(("shards", "context", "tensor"), None),
            P(("shards", "context", "tensor"), None),
            P(),
            P(),
            P("shards", None, "tensor"),
            P(None, "tensor"),
            P(None, None, "tensor"),
            P(None, "tensor"),
            P(),
            P(),
            P(),
            P(),
            P(),
            P("shards", "tensor"),
            P("tensor"),
            P("tensor", "shards"),
            P(),
            P(),
            P(),
            P("shards", "tensor"),
            P("tensor"),
            P("tensor", "shards"),
            P(),
        ),
        check_vma=False,
    )
```

```python
import functools
import math

import jax
import jax.numpy as jnp
import ml_dtypes
import numpy as np
from jax import lax
from jax.experimental import pallas as pl
from jax.experimental.pallas import tpu as pltpu
from jax.sharding import PartitionSpec as P

BLOCK = 256
TRUNK = 8
NPATH = 10
PATH = 2560
BRANCHES = 4
LEAVES = 8
TREE_BLK = 20
WAYS = 4

f32 = jnp.float32
bf16 = jnp.bfloat16
exact_mode = lax.Precision.HIGHEST
GELU_A = math.sqrt(2.0 / math.pi)
GELU_B = 0.044715


def dft_tables():
    k = np.arange(BLOCK)[None, :]
    n = np.arange(BLOCK)[:, None]
    ang = np.pi * ((2 * k + 1) * n % 1024) / 512.0
    fwd = np.concatenate([np.cos(ang), -np.sin(ang)], axis=1)
    m = BLOCK + np.arange(BLOCK)[None, :]
    kk = np.arange(BLOCK)[:, None]
    ang2 = np.pi * ((2 * kk + 1) * m % 1024) / 512.0
    inv = np.concatenate([np.cos(ang2), -np.sin(ang2)], axis=0) / 256.0
    return fwd.astype(ml_dtypes.bfloat16), inv.astype(ml_dtypes.bfloat16)


def swap(x, axis, k):
    return lax.ppermute(x, axis, [(i, i ^ k) for i in range(WAYS)])


def smem_spec():
    return pl.BlockSpec(memory_space=pltpu.SMEM)


def call(kernel, outs, n_in, scratch=(), limit=24):
    def run(sc, *args):
        assert len(args) == n_in
        vm = pl.BlockSpec(memory_space=pltpu.VMEM)
        return pl.pallas_call(
            kernel,
            out_shape=[jax.ShapeDtypeStruct(s, d) for s, d in outs],
            in_specs=[smem_spec()] + [vm] * n_in,
            out_specs=[vm] * len(outs),
            scratch_shapes=list(scratch),
            compiler_params=pltpu.CompilerParams(vmem_limit_bytes=limit << 20),
        )(sc, *args)

    return run


def after(x, *deps):
    return lax.optimization_barrier((x, deps))[0]


def nt(a, b):
    return lax.dot_general(a, b, (((1,), (1,)), ((), ())), preferred_element_type=f32)


def nn(a, b):
    return lax.dot_general(a, b, (((1,), (0,)), ((), ())), preferred_element_type=f32)


def tn(a, b):
    return lax.dot_general(a, b, (((0,), (0,)), ((), ())), preferred_element_type=f32)


def two(a):
    hi = a.astype(bf16)
    return hi, (a - hi.astype(f32)).astype(bf16)


def row(ref):
    return ref[...].reshape(1, ref.shape[0])


def norm_parts(x):
    mu = jnp.mean(x, axis=-1, keepdims=True)
    xc = x - mu
    rs = lax.rsqrt(jnp.mean(xc * xc, axis=-1, keepdims=True) + 1e-05)
    return xc * rs, rs


def norm_back(nh, rs, dnh):
    m1 = jnp.mean(dnh, axis=-1, keepdims=True)
    m2 = jnp.mean(dnh * nh, axis=-1, keepdims=True)
    return rs * (dnh - m1 - nh * m2)


def share_tiles(t):
    return [((0, 1), 2), ((3, 4), 2), ((5, 6), 7), ((8, 9), 7)][t]


def pack_share(tiles, t, ch, store):
    (a, b), c = share_tiles(t)
    store(0, tiles(a))
    store(ch, tiles(b))
    x = tiles(c)
    low = lax.broadcasted_iota(jnp.int32, (ch // 2, 128), 1) < 64
    top, bot = x[: ch // 2], x[ch // 2 :]
    if t % 2 == 0:
        y = jnp.where(low, top, pltpu.roll(bot, 64, 1))
    else:
        y = jnp.where(low, pltpu.roll(top, 64, 1), bot)
    store(2 * ch, y)


def left_rows(piece, ch):
    x = piece[2 * ch :].astype(f32)
    return jnp.concatenate([x, pltpu.roll(x, 64, 1)], axis=0)


def share_offsets(t):
    odd = t % 2
    return (64 * odd, 64 * odd + 128, 256 * (1 - odd))


def norm1_fwd_kernel(sc, tok, cw, cb, ib, sk, g, b, a1o, colo, rt):
    gain, shift = row(g), row(b)
    ch = sk.shape[0]
    rt[...] = jnp.zeros_like(rt)
    for p in range(3):
        at = slice(p * ch, (p + 1) * ch)
        for k in range(3):
            rt[k : k + 1, at] = cw[k, p : p + 1, :]
        rt[3:4, at] = cb[p : p + 1, :]
        rt[4:5, at] = ib[p : p + 1, :]
        rt[5:6, at] = row(sk)
    colo[...] = rt[...].T

    @pl.loop(0, 5)
    def _(i):
        rows = pl.ds(pl.multiple_of(i * BLOCK, BLOCK), BLOCK)
        nh, _ = norm_parts(tok[rows, :].astype(f32))
        a1o[rows, :] = (nh * gain + shift).astype(bf16)


def proj_kernel(sc, a1, m0, m1, m2, m3, wt, cols, g, bb, zo, zro, go, gvo, uo, u0, u1, u2, u3, rim, zs):
    c = sc[1]
    gain, shift = row(g), row(bb)
    cv = cols[...]
    w0, w1, w2, cb, ib = (cv[:, i : i + 1] for i in range(5))
    ch = go.shape[1]
    cs = ch // WAYS
    lane = lax.broadcasted_iota(jnp.int32, (3 * ch, 128), 1)
    for k, r in enumerate((m0, m1, m2, m3)):
        rim[pl.ds((c ^ k) * 5, 5)] = r[...]
    rows = [rim[jnp.maximum(sc[3 + b], 0)] for b in range(5)]
    nhr, _ = norm_parts(jnp.concatenate(rows, axis=0).astype(f32))
    a1r = (nhr * gain + shift).astype(bf16)
    a1r = jnp.concatenate([a1r, jnp.zeros((6, a1r.shape[1]), bf16)], axis=0)
    zr = (nt(wt[...], a1r) + ib).astype(bf16).astype(f32)
    lane16 = lax.broadcasted_iota(jnp.int32, zr.shape, 1)
    keep = jnp.zeros(zr.shape, f32)
    for b in range(5):
        keep = jnp.where(lane16 // 2 == b, jnp.where(sc[3 + b] >= 0, 1.0, 0.0), keep)
    zr = zr * keep
    zro[...] = jnp.concatenate([zr, jnp.zeros((zr.shape[0], 112), f32)], axis=1).T[:16]
    for b in range(5):
        zs[b] = zr[:, 2 * b : 2 * b + 2]

    for b in range(5):
        zb = (nt(wt[...], a1[b * BLOCK : (b + 1) * BLOCK, :]) + ib).astype(bf16)
        zo[b] = zb
        z = zb.astype(f32)
        far, near = zs[b, :, 0:1], zs[b, :, 1:2]
        r1, r2 = pltpu.roll(z, 1, 1), pltpu.roll(z, 2, 1)
        z1 = jnp.concatenate([jnp.where(lane == 0, near, r1[:, :128]), r1[:, 128:]], axis=1)
        z2 = jnp.concatenate(
            [jnp.where(lane == 0, far, jnp.where(lane == 1, near, r2[:, :128])), r2[:, 128:]], axis=1
        )
        sv = cb + w0 * z + w1 * z1 + w2 * z2
        go[b] = sv[:ch]
        gvo[b] = sv[ch:]
        uo[b] = (sv[2 * ch :] * sv[ch : 2 * ch]).astype(bf16)
        for k, o in enumerate((u0, u1, u2, u3)):
            o[b] = uo[b, pl.ds(pl.multiple_of((c ^ k) * cs, 16), cs), :]


def sincos(x):
    n = jnp.floor(x * (2.0 / math.pi) + 0.5)
    r = ((x - n * 1.5703125) - n * 4.837512969970703125e-4) - n * 7.54978995489188216e-8
    r2 = r * r
    sn = r + r * r2 * (-1.6666654611e-1 + r2 * (8.3321608736e-3 - r2 * 1.9515295891e-4))
    cn = 1.0 - 0.5 * r2 + r2 * r2 * (4.166664568298827e-2 + r2 * (-1.388731625493765e-3 + r2 * 2.443315711809948e-5))
    q = n.astype(jnp.int32)
    odd = (q & 1) == 1
    s1, c1 = jnp.where(odd, cn, sn), jnp.where(odd, sn, cn)
    return jnp.where((q & 2) == 2, -s1, s1), jnp.where(((q + 1) & 2) == 2, -c1, c1)


def exact_nn(a, b):
    return lax.dot_general(a, b, (((1,), (0,)), ((), ())), precision=exact_mode, preferred_element_type=f32)


STEP = 5 * BLOCK


def filter_chunk(d, emb, fit, fmt, fc, bands):
    frv, b1, b2, rate = (fc[:, i : i + 1] for i in range(4))
    pos = (lax.broadcasted_iota(jnp.int32, (1, STEP), 1) + d * STEP).astype(f32)
    k = lax.broadcasted_iota(jnp.int32, (bands, 1), 0).astype(f32)
    freq = 0.0001 + (bands - 1 - 0.0001) * k / max(bands - 1, 1)
    sn, cn = sincos(freq * (2.0 * math.pi * pos / PATH))
    emb[...] = jnp.zeros_like(emb)
    emb[0:bands] = cn
    emb[bands : 2 * bands] = -sn
    lag = pos / (PATH - 1)
    emb[2 * bands : 2 * bands + 1] = lag
    e = emb[...]
    p1 = exact_nn(fit[...], e) + b1
    s1, c1 = sincos(frv * p1)
    p2 = exact_nn(fmt[...], s1) + b2
    s2, c2 = sincos(frv * p2)
    return e, p1, s1, c1, p2, s2, c2, lag, rate


def hidden_kernel(bands, sc, fit, fmt, fc, mid, emb):
    @pl.loop(0, PATH // STEP)
    def _(d):
        sl = pl.ds(pl.multiple_of(d * STEP, STEP), STEP)
        mid[:, sl] = filter_chunk(d, emb, fit, fmt, fc, bands)[5]


def taps_kernel(sc, mid, fc, fo, taps):
    cs = fo.shape[0]
    lag = lax.broadcasted_iota(jnp.int32, (1, PATH), 1).astype(f32) / (PATH - 1)
    taps[...] = exact_nn(fo[...], mid[...]) * (jnp.exp(-lag * fc[:cs, 3:4]) + 0.05)


def leaf_parent(sc, i):
    return TRUNK - 1 + sc[8 + 1 + BRANCHES + i]


def signs():
    lane = lax.broadcasted_iota(jnp.int32, (1, BLOCK), 1)
    return (1 - 2 * (lane % 2)).astype(f32)


def mul(acc, h, w):
    hr, hi = h[:, :BLOCK], h[:, BLOCK:]
    wr, wi = w[:, :BLOCK], w[:, BLOCK:]
    return acc[0] + (hr * wr - hi * wi), acc[1] + (hr * wi + hi * wr)


def mul_conj(acc, h, w):
    hr, hi = h[:, :BLOCK], h[:, BLOCK:]
    wr, wi = w[:, :BLOCK], w[:, BLOCK:]
    return acc[0] + (hr * wr + hi * wi), acc[1] + (hr * wi - hi * wr)


def conv_kernel(sc, u0, u1, u2, u3, taps, fh, gh, wo, ho, y0, y1, y2, y3, un, sp):
    c = sc[1]
    cs = u0.shape[1]
    for k, r in enumerate((u0, u1, u2, u3)):
        un[pl.ds((c ^ k) * 5, 5)] = r[...]
    for d in range(NPATH):
        thi, tlo = two(taps[:, d * BLOCK : (d + 1) * BLOCK])
        ho[d] = nn(thi, fh[...]) + nn(tlo, fh[...])
    ua = un[...].reshape(TREE_BLK * cs, BLOCK)
    sp[...] = nn(ua, fh[...]).reshape(TREE_BLK, cs, 2 * BLOCK)
    sg = signs()

    def window(k, par):
        a = sp[k]
        wr = sg * a[:, BLOCK:]
        wi = -(sg * a[:, :BLOCK])
        if par is not None:
            q = sp[par]
            wr = wr + q[:, :BLOCK]
            wi = wi + q[:, BLOCK:]
        wo[k, :, :BLOCK] = wr
        wo[k, :, BLOCK:] = wi

    window(0, None)

    @pl.loop(1, TRUNK)
    def _(k):
        window(k, k - 1)

    @pl.loop(0, BRANCHES)
    def _(i):
        window(TRUNK + i, TRUNK - 1)

    @pl.loop(0, LEAVES)
    def _(i):
        window(TRUNK + BRANCHES + i, leaf_parent(sc, i))

    zero = jnp.zeros((cs, BLOCK), f32)

    def put(k, acc):
        sp[k, :, :BLOCK] = acc[0]
        sp[k, :, BLOCK:] = acc[1]

    @pl.loop(0, TRUNK)
    def _(q):
        acc = lax.fori_loop(0, q + 1, lambda d, a: mul(a, ho[d], wo[q - d]), (zero, zero))
        put(q, acc)

    common_b = lax.fori_loop(1, 9, lambda d, a: mul(a, ho[d], wo[8 - d]), (zero, zero))

    @pl.loop(TRUNK, TRUNK + BRANCHES)
    def _(k):
        put(k, mul(common_b, ho[0], wo[k]))

    common_l = lax.fori_loop(2, 10, lambda d, a: mul(a, ho[d], wo[9 - d]), (zero, zero))

    @pl.loop(0, LEAVES)
    def _(i):
        k = TRUNK + BRANCHES + i
        put(k, mul(mul(common_l, ho[0], wo[k]), ho[1], wo[leaf_parent(sc, i)]))

    yhi, ylo = two(sp[...].reshape(TREE_BLK * cs, 2 * BLOCK))
    y = nn(yhi, gh[...]) + nn(ylo, gh[...])
    un[...] = y.astype(bf16).reshape(TREE_BLK, cs, BLOCK)
    for k, o in enumerate((y0, y1, y2, y3)):
        o[...] = un[pl.ds((c ^ k) * 5, 5)]


def gate_kernel(sc, y0, y1, y2, y3, g0, u, cols, yo, p0, p1, p2, p3, ys, gs, pk):
    c, t = sc[1], sc[2]
    cs = y0.shape[1]
    for k, r in enumerate((y0, y1, y2, y3)):
        for b in range(5):
            ys[b, pl.ds(pl.multiple_of((c ^ k) * cs, 16), cs), :] = r[b]
    skip = cols[:, 5:6][: u.shape[1]]
    for b in range(5):
        y = ys[b]
        yo[b] = y
        gs[b] = g0[b] * (y.astype(f32) + skip * u[b].astype(f32))
    pack_all(t, u.shape[1], lambda j: gs[j // 2, :, (j % 2) * 128 : (j % 2) * 128 + 128], pk, (p0, p1, p2, p3))


def pack_all(t, ch, tiles, pk, outs):
    for s in range(WAYS):

        def store(row, v, s=s):
            pk[s, row : row + v.shape[0]] = v.astype(bf16)

        pack_share(tiles, s, ch, store)
    for k, o in enumerate(outs):
        if o is not None:
            o[...] = pk[t ^ k]


def unpack_all(t, ch, ins, pk, put):
    for k, r in enumerate(ins):
        pk[t ^ k] = r[...]
    for s in range(WAYS):
        (a, b), _ = share_tiles(s)
        put(a, pk[s, 0:ch].astype(f32))
        put(b, pk[s, ch : 2 * ch].astype(f32))
    low = lax.broadcasted_iota(jnp.int32, (ch // 2, 128), 1) < 64
    for j, (s0, s1) in ((2, (0, 1)), (7, (2, 3))):
        x0 = pk[s0, 2 * ch :].astype(f32)
        x1 = pk[s1, 2 * ch :].astype(f32)
        top = jnp.where(low, x0, pltpu.roll(x1, 64, 1))
        bot = jnp.where(low, pltpu.roll(x0, 64, 1), x1)
        put(j, jnp.concatenate([top, bot], axis=0))


def sides(sc, half):
    h = sc[0]
    return pl.ds(pl.multiple_of(h * half, 128), half), pl.ds(pl.multiple_of((1 - h) * half, 128), half)


def mix_kernel(sc, p0, p1, p2, p3, owm, owo, tok, ob, g2, b2, r1o, a2o, acc):
    t = sc[2]
    ch, half = p0.shape[0] * 2 // 5, owm.shape[2]
    mine, other = sides(sc, half)
    offs = share_offsets(t)
    parts = [None, None, None]
    for k, r in enumerate((p0, p1, p2, p3)):
        wm, wo = owm[k, :ch], owo[k, :ch]
        piece = r[...]
        xs = (piece[:ch].astype(f32), piece[ch : 2 * ch].astype(f32), left_rows(piece, ch))
        for i, x in enumerate(xs):
            xt = x.T.astype(bf16)
            v = (nn(xt, wm), nn(xt, wo))
            parts[i] = v if parts[i] is None else (parts[i][0] + v[0], parts[i][1] + v[1])
    for i, n in ((0, 128), (1, 128), (2, 64)):
        at = pl.ds(pl.multiple_of(offs[i], 64), n)
        acc[at, mine] = parts[i][0][:n]
        acc[at, other] = parts[i][1][:n]
    r1 = tok[...].astype(f32) + (acc[...] + row(ob))
    r1o[...] = r1
    nh, _ = norm_parts(r1)
    a2o[...] = (nh * row(g2) + row(b2)).astype(bf16)


def stacked(ref, at, n):
    return jnp.concatenate([ref[k, at : at + n] for k in range(WAYS)], axis=0)


def mlp_kernel(ch, sc, xa, xb, ca, cb, um, uo, dm, do, upb, dpo, aco, pa, pb):
    mine, other = sides(sc, um.shape[2])
    bias = upb[...]
    ffs = dm.shape[1]
    u_m, u_o = stacked(um, ch, ffs), stacked(uo, ch, ffs)
    d_m, d_o = stacked(dm, 0, ffs), stacked(do, 0, ffs)
    n = pa.shape[0]
    for i, (x, ct, po) in enumerate(((xa, ca, pa), (xb, cb, pb))):
        at = slice(i * n, (i + 1) * n)
        p = nt(x[:, mine], u_m) + nt(x[:, other], u_o) + bias
        d = nt(ct[:, mine], d_m) + nt(ct[:, other], d_o)
        p2 = p * p
        th = jnp.tanh(GELU_A * p * (1.0 + GELU_B * p2))
        half = 0.5 * (1.0 + th)
        aco[at] = (p * half).astype(bf16)
        slope = half + 0.5 * p * (1.0 - th * th) * (GELU_A * (1.0 + 3.0 * GELU_B * p2))
        dp = (d * slope).astype(bf16)
        dpo[at] = dp
        po[:, mine] = nn(dp, u_m).astype(bf16)
        po[:, other] = nn(dp, u_o).astype(bf16)


def ffn_part(sc, ac, dm, do, f0, f1):
    mine, other = sides(sc, dm.shape[2])
    n = dm.shape[1]
    d_m, d_o = stacked(dm, 0, n), stacked(do, 0, n)
    m = f0.shape[0]
    for i, out in enumerate((f0, f1)):
        a = ac[i * m : (i + 1) * m]
        out[:, mine] = nn(a, d_m).astype(bf16)
        out[:, other] = nn(a, d_o).astype(bf16)


def put_grad(sc, outs, v, mat):
    n = v.shape[0] // WAYS
    if len(outs) == 1:
        for q in range(WAYS):
            outs[0][q, mat] = v[q * n : (q + 1) * n].astype(bf16)
        return
    m = v.shape[1] // 2
    first = sc[0] == 0
    for q in range(WAYS):
        a, b = v[q * n : (q + 1) * n, :m], v[q * n : (q + 1) * n, m:]
        outs[0][q, mat] = jnp.where(first, a, b).astype(bf16)
        outs[1][q, mat] = jnp.where(first, b, a).astype(bf16)


def tn_pair(a, b0, b1):
    m = b0.shape[0]
    return tn(a[:m], b0[...]) + tn(a[m:], b1[...])


def mlp_grad_one_kernel(sc, x0, x1, dp, ac, c0, c1, dm, do, out, ub, f0, f1):
    out[0] = tn_pair(dp, x0, x1).astype(bf16)
    out[1] = tn_pair(ac, c0, c1).astype(bf16)
    ub[...] = jnp.sum(dp[...].astype(f32), axis=0, keepdims=True)
    ffn_part(sc, ac, dm, do, f0, f1)


def mlp_grad_two_kernel(sc, x0, x1, dp, ac, c0, c1, one, ubone, dm, do, *outs):
    *grads, ub, f0, f1 = outs
    put_grad(sc, grads, one[0].astype(f32) + tn_pair(dp, x0, x1), 0)
    put_grad(sc, grads, one[1].astype(f32) + tn_pair(ac, c0, c1), 1)
    ub[...] = ubone[...] + jnp.sum(dp[...].astype(f32), axis=0, keepdims=True)
    ffn_part(sc, ac, dm, do, f0, f1)


def norm2_kernel(sc, own, core, far, r1, cot, g2, owm, owo, dro, dmo, sums, p0, p1, p2, p3):
    t = sc[2]
    sums[...] = jnp.zeros_like(sums)
    dn2 = own[...].astype(f32) + core[...].astype(f32) + far[...].astype(f32)
    nh, rs = norm_parts(r1[...])
    ct = cot[...].astype(f32)
    sums[0:1] = jnp.sum(dn2 * nh, axis=0, keepdims=True)
    sums[1:2] = jnp.sum(dn2, axis=0, keepdims=True)
    dr = ct + norm_back(nh, rs, dn2 * row(g2))
    dro[...] = dr
    dm = dr.astype(bf16)
    dmo[...] = dm
    sums[2:3] = jnp.sum(dm.astype(f32), axis=0, keepdims=True)
    sums[3:4] = jnp.sum(ct, axis=0, keepdims=True)
    offs = share_offsets(t)
    ch, half = p0.shape[0] * 2 // 5, owm.shape[2]
    mine, other = sides(sc, half)
    low = lax.broadcasted_iota(jnp.int32, (ch // 2, 128), 1) < 64
    at = [pl.ds(pl.multiple_of(offs[i], 64), n) for i, n in ((0, 128), (1, 128), (2, 64))]
    dms = [(dmo[a, mine], dmo[a, other]) for a in at]
    dms[2] = tuple(jnp.concatenate([v, v], axis=0) for v in dms[2])
    for k, o in enumerate((p0, p1, p2, p3)):
        wm, wo = owm[k, :ch], owo[k, :ch]
        vs = [nt(wm, a) + nt(wo, b) for a, b in dms]
        o[0:ch] = vs[0].astype(bf16)
        o[ch : 2 * ch] = vs[1].astype(bf16)
        o[2 * ch :] = jnp.where(low, vs[2][: ch // 2], vs[2][ch // 2 :]).astype(bf16)


def out_grad_kernel(sc, p0, p1, p2, p3, dm, *outs):
    t = sc[2]
    offs = share_offsets(t)
    ch = p0.shape[0] * 2 // 5
    da = dm[pl.ds(pl.multiple_of(offs[0], 64), 128), :]
    db = dm[pl.ds(pl.multiple_of(offs[1], 64), 128), :]
    dc = dm[pl.ds(pl.multiple_of(offs[2], 64), 64), :]
    vs = []
    for r in (p0, p1, p2, p3):
        piece = r[...]
        left = left_rows(piece, ch)[:, :64].astype(bf16)
        vs.append(nn(piece[:ch], da) + nn(piece[ch : 2 * ch], db) + nn(left, dc))
    put_grad(sc, outs, jnp.concatenate(vs, axis=0), 0)


def ungate_kernel(sc, p0, p1, p2, p3, g0, ys, u, cols, dyo, dgo, so, d0, d1, d2, d3, pk, dg):
    c, t = sc[1], sc[2]
    ch = u.shape[1]
    cs = ch // WAYS

    def put(j, v):
        dg[j // 2, :, (j % 2) * 128 : (j % 2) * 128 + 128] = v

    unpack_all(t, ch, (p0, p1, p2, p3), pk, put)
    skip = cols[:, 5:6][:ch]
    tot = None
    for b in range(5):
        g = dg[b]
        uu = u[b].astype(f32)
        dgo[b] = g * (ys[b].astype(f32) + skip * uu)
        dy = g * g0[b]
        v = jnp.sum(dy * uu, axis=1, keepdims=True)
        tot = v if tot is None else tot + v
        dyo[b] = dy.astype(bf16)
    so[...] = tot
    for k, o in enumerate((d0, d1, d2, d3)):
        for b in range(5):
            o[b] = dyo[b, pl.ds(pl.multiple_of((c ^ k) * cs, 16), cs), :]


def conv_back_kernel(sc, d0, d1, d2, d3, ws, hs, fh, gh, dho, o0, o1, o2, o3, un, dy, dw, dh):
    c = sc[1]
    cs = d0.shape[1]
    for k, r in enumerate((d0, d1, d2, d3)):
        un[pl.ds((c ^ k) * 5, 5)] = r[...]
    da = un[...].reshape(TREE_BLK * cs, BLOCK)
    dy[0:TREE_BLK] = nt(da, gh[...]).reshape(TREE_BLK, cs, 2 * BLOCK)
    zero = jnp.zeros((cs, BLOCK), f32)
    zz = jnp.zeros((cs, 2 * BLOCK), f32)
    first_leaf = TRUNK + BRANCHES
    sum_b = lax.fori_loop(TRUNK, first_leaf, lambda k, a: a + dy[k], zz)
    sum_l = lax.fori_loop(first_leaf, TREE_BLK, lambda k, a: a + dy[k], zz)
    dy[TREE_BLK] = sum_b
    dy[TREE_BLK + 1] = sum_l
    for i in range(BRANCHES):
        dy[TREE_BLK + 2 + i] = zz

    @pl.loop(0, LEAVES)
    def _(i):
        k = TREE_BLK + 2 + leaf_parent(sc, i) - TRUNK
        dy[k] = dy[k] + dy[first_leaf + i]


    def put(ref, k, acc):
        ref[k, :, :BLOCK] = acc[0]
        ref[k, :, BLOCK:] = acc[1]

    @pl.loop(0, TRUNK)
    def _(j):
        acc = lax.fori_loop(j, TRUNK, lambda q, a: mul_conj(a, hs[q - j], dy[q]), (zero, zero))
        acc = mul_conj(acc, hs[8 - j], dy[TREE_BLK])
        put(dw, j, mul_conj(acc, hs[9 - j], dy[TREE_BLK + 1]))

    @pl.loop(0, BRANCHES)
    def _(i):
        k = TRUNK + i
        acc = mul_conj((zero, zero), hs[0], dy[k])
        put(dw, k, mul_conj(acc, hs[1], dy[TREE_BLK + 2 + i]))

    @pl.loop(first_leaf, TREE_BLK)
    def _(k):
        put(dw, k, mul_conj((zero, zero), hs[0], dy[k]))


    @pl.loop(0, TRUNK)
    def _(d):
        put(dh, d, lax.fori_loop(d, TRUNK, lambda q, a: mul_conj(a, ws[q - d], dy[q]), (zero, zero)))

    put(dh, 8, (zero, zero))
    put(dh, 9, (zero, zero))

    def more(d, k, q):
        acc = (dh[d, :, :BLOCK], dh[d, :, BLOCK:])
        put(dh, d, mul_conj(acc, ws[k], dy[q]))

    @pl.loop(1, 9)
    def _(d):
        more(d, 8 - d, TREE_BLK)

    @pl.loop(2, 10)
    def _(d):
        more(d, 9 - d, TREE_BLK + 1)

    @pl.loop(TRUNK, TREE_BLK)
    def _(k):
        more(0, k, k)

    @pl.loop(0, BRANCHES)
    def _(i):
        more(1, TRUNK + i, TREE_BLK + 2 + i)

    for d in range(NPATH):
        thi, tlo = two(dh[d])
        dho[:, d * BLOCK : (d + 1) * BLOCK] = nt(thi, fh[...]) + nt(tlo, fh[...])

    sg = signs()

    def own(k):
        w = dw[k]
        return jnp.concatenate([-(sg * w[:, BLOCK:]), sg * w[:, :BLOCK]], axis=1)

    @pl.loop(0, TRUNK - 1)
    def _(k):
        dy[k] = own(k) + dw[k + 1]

    dy[TRUNK - 1] = lax.fori_loop(TRUNK, first_leaf, lambda k, a: a + dw[k], own(TRUNK - 1))

    @pl.loop(TRUNK, TREE_BLK)
    def _(k):
        dy[k] = own(k)

    @pl.loop(0, LEAVES)
    def _(i):
        k = leaf_parent(sc, i)
        dy[k] = dy[k] + dw[first_leaf + i]

    shi, slo = two(dy[0:TREE_BLK].reshape(TREE_BLK * cs, 2 * BLOCK))
    du = nt(shi, fh[...]) + nt(slo, fh[...])
    un[...] = du.astype(bf16).reshape(TREE_BLK, cs, BLOCK)
    for k, o in enumerate((o0, o1, o2, o3)):
        o[...] = un[pl.ds((c ^ k) * 5, 5)]


def unconv_kernel(sc, u0, u1, u2, u3, dyv, dg0, gv, z, zr, cols, dzo, rims, cg, dus, rs, acc, zc, zs):
    c = sc[1]
    ch = dyv.shape[1]
    cs = ch // WAYS
    cv = cols[...]
    w0, w1, w2 = (cv[:, i : i + 1] for i in range(3))
    skip = cv[:ch, 5:6]
    lane = lax.broadcasted_iota(jnp.int32, (3 * ch, 128), 1)
    rs[...] = jnp.zeros_like(rs)
    acc[...] = jnp.zeros_like(acc)

    def fold(i, v):
        acc[i] = acc[i] + (v[:, :128] + v[:, 128:])

    zc[...] = jnp.zeros_like(zc)
    zc[0:16] = zr[...]
    zcol = zc[...].T
    for b in range(5):
        zs[b] = zcol[:, 2 * b : 2 * b + 2]

    @pl.loop(0, 5)
    def _(b):
        for k, r in enumerate((u0, u1, u2, u3)):
            dus[pl.ds(pl.multiple_of((c ^ k) * cs, 16), cs), :] = r[b]
        du = dus[...].astype(f32) + skip * dyv[b].astype(f32)
        sv = gv[b]
        ds = jnp.concatenate([dg0[b], du * sv[ch:], du * sv[:ch]], axis=0)
        zv = z[b].astype(f32)
        far, near = zs[b, :, 0:1], zs[b, :, 1:2]
        r1, r2 = pltpu.roll(ds, BLOCK - 1, 1), pltpu.roll(ds, BLOCK - 2, 1)
        n1 = jnp.concatenate([r1[:, :128], jnp.where(lane == 127, 0.0, r1[:, 128:])], axis=1)
        n2 = jnp.concatenate([r2[:, :128], jnp.where(lane >= 126, 0.0, r2[:, 128:])], axis=1)
        dzo[b] = w0 * ds + w1 * n1 + w2 * n2
        d0, d1 = ds[:, 0:1], ds[:, 1:2]
        fold(0, ds)
        fold(1, ds * zv)
        fold(2, n1 * zv)
        fold(3, n2 * zv)
        acc[2] = acc[2] + jnp.where(lane == 0, d0 * near, 0.0)
        acc[3] = acc[3] + jnp.where(lane == 0, d0 * far + d1 * near, 0.0)
        rs[...] = rs[...] + jnp.where(lane == 2 * b, w2 * d0, jnp.where(lane == 2 * b + 1, w1 * d0 + w2 * d1, 0.0))

    rims[...] = rs[...].T[:16]
    out = jnp.zeros(lane.shape, f32)
    for i in range(4):
        out = jnp.where(lane == i, jnp.sum(acc[i], axis=1, keepdims=True), out)
    cg[...] = out


def dz_kernel(sc, dzo, r0, r1, r2, r3, pick, dz, p0, p1, p2, p3, ib, rall, rt, pk):
    c, t = sc[1], sc[2]
    rows = dzo.shape[1]
    for k, r in enumerate((r0, r1, r2, r3)):
        rall[pl.ds(pl.multiple_of((c ^ k) * 16, 16), 16), :] = r[...]
    got = lax.dot_general(
        pick[...], rall[...], (((1,), (0,)), ((), ())), precision=exact_mode, preferred_element_type=f32
    )
    rt[...] = got.T
    lane = lax.broadcasted_iota(jnp.int32, (rows, 128), 1)
    tot = None
    for b in range(5):
        add = jnp.where(lane >= 126, pltpu.roll(rt[...], 126 - 2 * b, 1), 0.0)
        lo = dzo[b, :, :128].astype(bf16)
        hi = (dzo[b, :, 128:] + add).astype(bf16)
        dz[b, :, :128] = lo
        dz[b, :, 128:] = hi
        v = jnp.sum(lo.astype(f32) + hi.astype(f32), axis=1, keepdims=True)
        tot = v if tot is None else tot + v
    ib[...] = tot
    pack_all(t, rows, lambda j: dz[j // 2, :, (j % 2) * 128 : (j % 2) * 128 + 128].astype(f32), pk, (p0, p1, p2, p3))


def in_grad_kernel(sc, dz, a1, wt, ib, g, b1, *outs):
    acc = None
    for b in range(5):
        v = nn(dz[b], a1[b * BLOCK : (b + 1) * BLOCK, :])
        acc = v if acc is None else acc + v
    sums = outs[-1]
    if len(outs) == 2:
        outs[0][...] = acc
    else:
        n = acc.shape[1] // 2
        first = sc[0] == 0
        outs[0][...] = jnp.where(first, acc[:, :n], acc[:, n:])
        outs[1][...] = jnp.where(first, acc[:, n:], acc[:, :n]).astype(bf16)
    w = wt[...].astype(f32)
    gsum = jnp.sum(w * acc, axis=0, keepdims=True)
    bsum = jnp.sum(w * ib[...], axis=0, keepdims=True)
    sums[...] = jnp.zeros_like(sums)
    sums[0:1] = (gsum - row(b1) * bsum) / row(g)
    sums[1:2] = bsum


FILT_ROWS = 112


def put_row(out, at, row):
    n = row.shape[1]
    k = -(-n // 128)
    for j in range(k):
        w = min(128, n - 128 * j)
        out[pl.ds(at + j, 1), :w] = row[:, 128 * j : 128 * j + w]
    return k


def pack_kernel(sc, sums1, sums2, ub, filt, fo, cg, ib, skip, out, colt):
    c, t = sc[1], sc[2]
    out[...] = jnp.zeros_like(out)
    for i in range(4):
        put_row(out, 8 * i, sums2[i : i + 1])
    n = ub.shape[1] // WAYS
    for q in range(WAYS):
        put_row(out, 32 + 2 * (WAYS * c + (t ^ q)), ub[0:1, q * n : (q + 1) * n])
    out[64 : 64 + FILT_ROWS, : filt.shape[1]] = filt[...]
    at = 64 + FILT_ROWS
    put_row(out, at, sums1[0:1])
    put_row(out, at + 8, sums1[1:2])
    at += 16
    lane = lax.broadcasted_iota(jnp.int32, cg.shape, 1)
    colt[...] = jnp.where(lane == 4, ib[...], cg[...]).T
    m = cg.shape[0]
    for j in range(-(-m // 128)):
        w = min(128, m - 128 * j)
        out[at : at + 8, :w] = colt[0:8, 128 * j : 128 * j + w]
        at += 8
    ch = skip.shape[0]
    put_row(out, at, jnp.broadcast_to(skip[...], (ch, 128)).T[0:1])
    at += 8
    cs = fo.shape[0]
    out[pl.ds(at + c * cs, cs), : fo.shape[1]] = fo[...]


def filter_back_kernel(bands, sc, dt, fit, fmt, fc, fo, fm, out, fog, emb):
    def three(dot, a, b):
        (ah, al), (bh, bl) = two(a), two(b)
        return dot(ah, bh) + dot(ah, bl) + dot(al, bh)

    n, ne, cs = fm.shape[0], emb.shape[0], fo.shape[0]
    fov, fmv, frv = fo[...], fm[...], fc[:, 0:1]

    def step(d, acc):
        a_fo, a_fm, a_fi, a_b1, a_b2, a_fr = acc
        e, q1, one, c1, q2, mid, c2, lag, rate = filter_chunk(d, emb, fit, fmt, fc, bands)
        sl = pl.ds(pl.multiple_of(d * STEP, STEP), STEP)
        draw = dt[:, sl] * (jnp.exp(-lag * rate[:cs]) + 0.05)
        a_fo = a_fo + three(nt, draw, mid)
        da2 = three(tn, fov, draw) * c2
        dp2 = da2 * frv
        a_fm = a_fm + three(nt, one, dp2)
        da1 = three(nn, fmv, dp2) * c1
        dp1 = da1 * frv
        a_fi = a_fi + three(nt, e, dp1)
        sums = [jnp.sum(v, axis=1, keepdims=True) for v in (dp1, dp2, da2 * q2 + da1 * q1)]
        return a_fo, a_fm, a_fi, a_b1 + sums[0], a_b2 + sums[1], a_fr + sums[2]

    zero = jnp.zeros((n, 1), f32)
    init = (jnp.zeros(fog.shape, f32), jnp.zeros((n, n), f32), jnp.zeros((ne, n), f32), zero, zero, zero)
    a_fo, a_fm, a_fi, *cols = lax.fori_loop(0, PATH // STEP, step, init)
    fog[...] = a_fo
    out[...] = jnp.zeros_like(out)
    out[0:n] = a_fm
    out[n : n + ne] = a_fi
    lane = lax.broadcasted_iota(jnp.int32, (n, 128), 1)
    m = jnp.where(lane == 0, cols[0], jnp.where(lane == 1, cols[1], jnp.where(lane == 2, cols[2], 0.0)))
    out[n + ne : n + ne + 8] = m.T[0:8]


def norm1_kernel(sc, p0, p1, p2, p3, w0, wa, wb, wc, wd, tok, dr, g, out, acc, wr):
    t = sc[2]
    rows, n = w0.shape[0], wa.shape[1]
    mine, other = sides(sc, wa.shape[2])
    h = sc[1] & 1
    near, far = pl.ds(pl.multiple_of(h * n, 16), n), pl.ds(pl.multiple_of((1 - h) * n, 16), n)
    for i in range(WAYS - 1):
        wr[i, near, mine], wr[i, near, other] = wa[i], wb[i]
        wr[i, far, mine], wr[i, far, other] = wc[i], wd[i]
    offs = share_offsets(t)
    parts = [None, None, None]
    for k, r in enumerate((p0, p1, p2, p3)):
        w = w0[...] if k == 0 else wr[k - 1]
        piece = r[...]
        xs = (piece[:rows].astype(f32), piece[rows : 2 * rows].astype(f32), left_rows(piece, rows))
        for i, x in enumerate(xs):
            v = nn(x.T.astype(bf16), w)
            parts[i] = v if parts[i] is None else parts[i] + v
    acc[pl.ds(pl.multiple_of(offs[0], 64), 128), :] = parts[0]
    acc[pl.ds(pl.multiple_of(offs[1], 64), 128), :] = parts[1]
    acc[pl.ds(pl.multiple_of(offs[2], 64), 64), :] = parts[2][:64]
    nh, rs = norm_parts(tok[...].astype(f32))
    out[...] = (dr[...] + norm_back(nh, rs, acc[...] * row(g))).astype(bf16)


def matrices_kernel(sc, m0, m1, m2, m3, upo, downo, rows):
    c = sc[1]
    n = m0.shape[1]
    for k, m in enumerate((m0, m1, m2, m3)):
        at = pl.ds(pl.multiple_of((c ^ k) * n, 64), n)
        rows[at, :] = m[0].astype(f32)
        downo[at, :] = m[1].astype(f32)
    upo[...] = rows[...].T


def layer_out_kernel(sc, r1, own, core, far, db, out):
    ffn = own[...].astype(f32) + core[...].astype(f32) + far[...].astype(f32)
    out[...] = (r1[...] + ffn + row(db)).astype(bf16)


def body(
    shard_count,
    tokens,
    parents,
    norm1_gain,
    norm1_bias,
    in_weight,
    in_bias,
    conv_weight,
    conv_bias,
    filt_in,
    filt_bias1,
    filt_mid,
    filt_bias2,
    sine_freq,
    filt_out,
    skip_gain,
    out_weight,
    out_bias,
    norm2_gain,
    norm2_bias,
    up_weight,
    up_bias,
    down_weight,
    down_bias,
    cotangent,
):
    rows, width = tokens.shape
    ch = skip_gain.shape[0]
    cs = ch // WAYS
    ch3 = 3 * ch
    ffq = up_bias.shape[0]
    ffs = ffq // WAYS
    share = rows // WAYS
    d_part = in_weight.shape[0]
    s_id = lax.axis_index("shards")
    c_id = lax.axis_index("context")
    t_id = lax.axis_index("tensor")
    pair = shard_count == 2

    def gather_shards(x, axis, *deps):
        if not pair:
            return lax.all_gather(x, "shards", axis=axis, tiled=True)
        o = lax.ppermute(x, "shards", [(0, 1), (1, 0)])
        o = after(o, *deps) if deps else o
        lo = jnp.where(s_id == 0, x, o)
        hi = jnp.where(s_id == 0, o, x)
        return jnp.concatenate([lo, hi], axis=axis)

    par = parents[0]
    all_par = jnp.concatenate(
        [jnp.arange(-1, TRUNK - 1, dtype=jnp.int32), jnp.full((BRANCHES,), TRUNK - 1, jnp.int32), TRUNK - 1 + par[1 + BRANCHES :]]
    )
    own_par = lax.dynamic_slice_in_dim(all_par, c_id * 5, 5, 0)
    side = s_id if pair else jnp.zeros_like(s_id)
    sc = jnp.concatenate([jnp.stack([side, c_id, t_id]).astype(jnp.int32), own_par, par]).astype(jnp.int32)

    def swap_y(x):
        return lax.ppermute(x, "shards", [(0, 1), (1, 0)])

    n_in, fw = filt_in.shape
    bands = (n_in - 1) // 2
    ne = -(-n_in // 8) * 8
    fit = jnp.concatenate([filt_in[1:], filt_in[:1], jnp.zeros((ne - n_in, fw), f32)]).T
    fmt = filt_mid.T
    channel = (t_id * ch + c_id * cs).astype(f32) + jnp.arange(fw, dtype=f32)
    slow, fast = math.log(0.01) / 1.5, math.log(0.01) / 0.3
    rates = jnp.abs(slow + (fast - slow) * channel / (ch * WAYS - 1))
    fc = jnp.stack([sine_freq, filt_bias1, filt_bias2, rates] + [rates] * 4, axis=1)
    (hidden,) = call(functools.partial(hidden_kernel, bands), [((fw, PATH), f32)], 3, [pltpu.VMEM((ne, STEP), f32)])(
        sc, fit, fmt, fc
    )

    wt_part = jnp.transpose(in_weight, (1, 2, 0)).reshape(ch3, d_part)
    wt = gather_shards(wt_part, 1, hidden)
    rim_tok = tokens.reshape(5, BLOCK, width)[:, BLOCK - 2 :, :]
    rims_in = [rim_tok] + [swap(rim_tok, "context", k) for k in (1, 2, 3)]
    up_t = lax.dynamic_slice_in_dim(up_weight, c_id * ffs, ffs, 1).T
    down_c = lax.dynamic_slice_in_dim(down_weight, c_id * ffs, ffs, 0)
    bias_c = lax.dynamic_slice_in_dim(up_bias, c_id * ffs, ffs, 0)
    b_hi, b_mid = two(bias_c)
    b_lo = (bias_c - b_hi.astype(f32) - b_mid.astype(f32)).astype(bf16)
    wide = d_part >= ffs
    if wide:
        b_rows = jnp.stack([b_hi, b_mid, b_lo] + [jnp.zeros_like(b_hi)] * 13)
        b_rows = jnp.concatenate([b_rows, jnp.zeros((16, d_part - ffs), bf16)], axis=1)
        two_mats = jnp.concatenate([out_weight, up_t, b_rows])
    else:
        two_mats = jnp.concatenate([out_weight, up_t])
    def columns(parts):
        m = jnp.stack(parts)
        if pair:
            return m, swap_y(m)
        m = lax.all_gather(m, "shards", axis=2, tiled=True)
        return m[:, :, : width // 2], m[:, :, width // 2 :]

    parts_b = [down_c] + [swap(down_c, "tensor", k) for k in (1, 2, 3)]
    down = columns(after(tuple(parts_b), hidden))
    two_mats = after(two_mats, parts_b[1], parts_b[2], parts_b[3])
    parts_a = [two_mats] + [swap(two_mats, "tensor", k) for k in (1, 2, 3)]
    if pair:
        fo_other = swap_y(filt_out)
        fo = jnp.concatenate([jnp.where(s_id == 0, filt_out, fo_other), jnp.where(s_id == 0, fo_other, filt_out)], axis=0)
    else:
        fo = fo_other = lax.all_gather(filt_out, "shards", axis=0, tiled=True)
    fo_t = lax.dynamic_slice_in_dim(fo, c_id * cs, cs, 1).astype(f32).T

    fh, gh = (jnp.asarray(a) for a in dft_tables())

    nb, B = 5, BLOCK
    piece = ((nb, cs, B), bf16)
    a1, cols = call(norm1_fwd_kernel, [((rows, width), bf16), ((ch3, 128), f32)], 7, [pltpu.VMEM((128, ch3), f32)])(
        after(sc, wt, down[0], fo_other), tokens, conv_weight, conv_bias, in_bias, skip_gain, norm1_gain, norm1_bias
    )
    z, zr, g0, gv, u, u0, u1, u2, u3 = call(
        proj_kernel,
        [((nb, ch3, B), bf16), ((16, ch3), f32), ((nb, ch, B), f32), ((nb, 2 * ch, B), f32), ((nb, ch, B), bf16)]
        + [piece] * 4,
        9,
        [pltpu.VMEM((TREE_BLK, 2, width), bf16), pltpu.VMEM((nb, ch3, 2), f32)],
    )(sc, a1, *rims_in, wt, cols, norm1_gain, norm1_bias)

    def ctx(p):
        return (p[0], swap(p[1], "context", 1), swap(p[2], "context", 2), swap(p[3], "context", 3))

    def ten(p):
        return (p[0], swap(p[1], "tensor", 1), swap(p[2], "tensor", 2), swap(p[3], "tensor", 3))

    un = ctx((u0, u1, u2, u3))
    (taps,) = call(taps_kernel, [((cs, PATH), f32)], 3)(after(sc, u0), hidden, fc, fo_t)
    mats = columns(after(tuple(parts_a), un))
    if wide:
        up_b = jnp.concatenate([p[ch + ffs : ch + ffs + 3, :ffs].astype(f32).sum(0) for p in parts_a]).reshape(1, ffq)
    else:
        up_b = jnp.concatenate([bias_c] + [swap(bias_c, "tensor", k) for k in (1, 2, 3)]).reshape(1, ffq)
    up_b = after(up_b, u0)
    spec = ((TREE_BLK, cs, 2 * B), f32)
    ws, hs, y0, y1, y2, y3 = call(
        conv_kernel,
        [spec, ((NPATH, cs, 2 * B), f32)] + [piece] * 4,
        7,
        [pltpu.VMEM((TREE_BLK, cs, B), bf16), pltpu.VMEM((TREE_BLK, cs, 2 * B), f32)],
    )(sc, *un, taps, fh, gh)
    yn = ctx((y0, y1, y2, y3))
    tok_share = lax.dynamic_slice_in_dim(tokens, t_id * share, share, 0)
    cot_share = lax.dynamic_slice_in_dim(cotangent, t_id * share, share, 0)
    tok_share, cot_share = after((tok_share, cot_share), u0)

    packs = (5 * ch // 2, 128)
    packed_out = [(packs, bf16)] * 4
    ys, *gp = call(
        gate_kernel,
        [((nb, ch, B), bf16)] + packed_out,
        7,
        [pltpu.VMEM((nb, ch, B), bf16), pltpu.VMEM((nb, ch, B), f32), pltpu.VMEM((WAYS,) + packs, bf16)],
    )(sc, *yn, g0, after(u, mats[0]), cols)
    gn = ten(gp)
    cot_share = after(cot_share, ys)
    cot1 = swap(cot_share, "context", 1)
    cot2 = swap(cot_share, "context", 2)

    sh = (share, width)
    r1, a2 = call(mix_kernel, [(sh, f32), (sh, bf16)], 10, [pltpu.VMEM(sh, f32)])(
        sc, *gn, *mats, after(tok_share, up_b), out_bias, norm2_gain, norm2_bias
    )

    x1 = swap(a2, "context", 1)
    x2 = swap(a2, "context", 2)
    cot3 = swap(after(cot2, a2), "context", 1)
    odd = c_id & 1
    w_half = lax.dynamic_slice_in_dim(wt, odd * (ch3 // 2), ch3 // 2, 0)
    w_quarter = after(lax.dynamic_slice_in_dim(w_half, side * (width // 2), width // 2, 1), a2)
    w_got = [swap(w_quarter, "tensor", k) for k in (1, 2, 3)]
    mlp = call(functools.partial(mlp_kernel, ch), [((2 * share, ffq), bf16)] * 2 + [(sh, bf16)] * 2, 9)
    dpa, aca, n0, n1 = mlp(sc, a2, x1, cot_share, cot1, *mats, *down, up_b)
    one, ub_one, f0, f1 = call(mlp_grad_one_kernel, [((2, ffq, width), bf16), ((1, ffq), f32), (sh, bf16), (sh, bf16)], 8)(
        after(sc, n0), a2, x1, dpa, aca, cot_share, cot1, *down
    )
    x2 = after(x2, one, w_got[0], w_got[2])
    x3 = swap(x2, "context", 1)
    dpb, acb, n2, n3 = mlp(sc, x2, x3, cot2, cot3, *mats, *down, up_b)
    one, ub_one, f0, f1 = after((one, ub_one, f0, f1), n2)

    def sum_context(q0, q1, q2, q3, *deps):
        a = swap(q1, "context", 1)
        b = swap(q3, "context", 1)
        b = after(b, *deps) if deps else b
        mid = (q2.astype(f32) + b.astype(f32)).astype(bf16)
        return q0, a, swap(mid, "context", 2)

    dn = sum_context(n0, n1, n2, n3)
    n_grad = 2 if pair else 1
    gcol = width // n_grad
    *mg, ub, f2, f3 = call(
        mlp_grad_two_kernel, [((WAYS, 2, ffs, gcol), bf16)] * n_grad + [((1, ffq), f32), (sh, bf16), (sh, bf16)], 10
    )(after(sc, n2), x2, x3, dpb, acb, cot2, cot3, one, ub_one, *down)
    dn = dn[:2] + (after(dn[2], w_got[1], mg),)
    dr1, dm, sums2, *dgp = call(norm2_kernel, [(sh, f32), (sh, bf16), ((8, width), f32)] + packed_out, 8)(
        sc, *dn, r1, cot_share, norm2_gain, *mats
    )
    f1, w_got = after((f1, w_got), dm)
    wa = jnp.stack(w_got)
    if pair:
        wb = swap_y(wa)
    else:
        other = lax.dynamic_slice_in_dim(w_half, width // 2, width // 2, 1)
        wb = jnp.stack([swap(after(other, dm), "tensor", k) for k in (1, 2, 3)])
    dgn = ten(dgp)

    og = call(out_grad_kernel, [((WAYS, 1, ch, gcol), bf16)] * n_grad, 5)(sc, *gn, dm)

    def over_shards(x):
        if pair:
            return x[0], swap_y(x[1])
        return lax.psum_scatter(x[0].astype(f32), "shards", scatter_dimension=3, tiled=True), jnp.zeros((), f32)

    def added(x):
        a, b = x
        return (a if b is None else a.astype(f32) + b.astype(f32)).astype(bf16)

    dy, dg0, skip_g, d0, d1, d2, d3 = call(
        ungate_kernel,
        [((nb, ch, B), bf16), ((nb, ch, B), f32), ((ch, 1), f32)] + [piece] * 4,
        8,
        [pltpu.VMEM((WAYS,) + packs, bf16), pltpu.VMEM((nb, ch, B), f32)],
    )(sc, dgn[0], dgn[1], after(dgn[2], og), dgn[3], g0, ys, u, cols)
    f3 = after(f3, dy)
    mg_y, og_y = over_shards(after(mg, dm)), over_shards(og)
    dn_ = ctx((d0, d1, d2, d3))
    mg_y = after(mg_y, dn_[1], dn_[2], dn_[3])
    dtaps, e0, e1, e2, e3 = call(
        conv_back_kernel,
        [((cs, PATH), f32)] + [piece] * 4,
        8,
        [
            pltpu.VMEM((TREE_BLK, cs, B), bf16),
            pltpu.VMEM((TREE_BLK + 6, cs, 2 * B), f32),
            pltpu.VMEM((TREE_BLK, cs, 2 * B), f32),
            pltpu.VMEM((NPATH, cs, 2 * B), f32),
        ],
    )(sc, dn_[0], dn_[1], after(dn_[2], mg_y), dn_[3], ws, hs, fh, gh)
    en = ctx((e0, e1, e2, e3))
    mg_sum = added(mg_y)
    mg_got = [swap(mg_sum[k], "tensor", k) for k in (1, 2, 3)]
    dzo, rims, cg = call(
        unconv_kernel,
        [((nb, ch3, B), f32), ((16, ch3), f32), ((ch3, 128), f32)],
        10,
        [pltpu.VMEM((ch, B), bf16), pltpu.VMEM((ch3, 128), f32), pltpu.VMEM((4, ch3, 128), f32), pltpu.VMEM((128, ch3), f32), pltpu.VMEM((5, ch3, 2), f32)],
    )(sc, en[0], en[1], after(en[2], mg_got[0], mg_got[2]), en[3], dy, dg0, gv, z, zr, cols)
    wa, wb = after((wa, wb), rims)
    wc, wd = swap(wa, "context", 1), swap(wb, "context", 1)
    rn = ctx((rims, rims, rims, rims))
    col = jnp.arange(WAYS * 16, dtype=jnp.int32)
    col_blk = (col // 16) * 5 + (col % 16) // 2
    col_ok = (col % 16) < 10
    col_par = jnp.where(col_ok, all_par[jnp.minimum(col_blk, TREE_BLK - 1)], -2)
    row = jnp.arange(128, dtype=jnp.int32)
    pick = (
        (row[:, None] < 10)
        & (col_par[None, :] == c_id * 5 + row[:, None] // 2)
        & (col[None, :] % 2 == row[:, None] % 2)
    ).astype(f32)
    dpacks = (5 * ch3 // 2, 128)
    dz, q0, q1, q2, q3, ib = call(
        dz_kernel,
        [((nb, ch3, B), bf16)] + [(dpacks, bf16)] * 4 + [((ch3, 1), f32)],
        6,
        [pltpu.VMEM((WAYS * 16, ch3), f32), pltpu.VMEM((ch3, 128), f32), pltpu.VMEM((WAYS,) + dpacks, bf16)],
    )(sc, dzo, *rn, pick)
    qn = ten((q0, q1, q2, q3))
    if pair:
        mine, theirs, sums1 = call(
            in_grad_kernel,
            [((ch3, d_part), f32), ((ch3, d_part), bf16), ((8, width), f32)],
            6,
        )(sc, dz, a1, wt, ib, norm1_gain, norm1_bias)
        ih = mine + swap_y(theirs).astype(f32)
    else:
        ig, sums1 = call(in_grad_kernel, [((ch3, width), f32), ((8, width), f32)], 6)(sc, dz, a1, wt, ib, norm1_gain, norm1_bias)
        ih = lax.psum_scatter(ig, "shards", scatter_dimension=1, tiled=True)

    fs = sum_context(f0, f1, f2, f3, dz)
    filt, fo_g = call(functools.partial(filter_back_kernel, bands), [((FILT_ROWS, fw), f32), ((cs, fw), f32)], 6, [pltpu.VMEM((ne, STEP), f32)])(
        after(sc, dz), dtaps, fit, fmt, fc, fo_t, filt_mid
    )
    n_col = 8 * (-(-ch3 // 128))
    n_all = 64 + FILT_ROWS + 16
    (small,) = call(pack_kernel, [((n_all + n_col + 8 + ch, 128), f32)], 8, [pltpu.VMEM((128, ch3), f32)])(
        sc, sums1, sums2, ub, filt, fo_g, cg, ib, skip_g
    )
    ctx_small = tuple(swap(small, "context", k) for k in (1, 2, 3))

    def total(own, got):
        return ((own.astype(f32) + got[0].astype(f32)) + (got[1].astype(f32) + got[2].astype(f32))).astype(bf16)

    og_sum = added(after(og_y, qn[1]))
    og_got = tuple(swap(og_sum[k], "tensor", k) for k in (1, 2, 3))
    m0 = total(mg_sum[0], after(tuple(mg_got), qn[1]))
    m1, m2 = swap(m0, "context", 1), swap(m0, "context", 2)
    ih_core = swap(ih.astype(bf16), "context", 1)

    (tokens_grad,) = call(norm1_kernel, [(sh, bf16)], 12, [pltpu.VMEM(sh, f32), pltpu.VMEM((WAYS - 1, ch3, width), bf16)])(
        sc, *qn, wt, wa, wb, wc, wd, tok_share, dr1, norm1_gain
    )

    done = tokens_grad
    fs, ctx_small, m1, m2, ih_core, og_got = after((fs, ctx_small, m1, m2, ih_core, og_got), done)
    ih = ih + ih_core.astype(f32)
    far = swap(ih.astype(bf16), "context", 2)
    small = (small + ctx_small[0]) + (ctx_small[1] + ctx_small[2])
    small = small + swap_y(small) if pair else lax.psum(small, "shards")
    late = small[n_all:]
    early = small[:n_all]
    early = (early + swap(early, "tensor", 1)) + (swap(early, "tensor", 2) + swap(early, "tensor", 3))
    oh = total(og_sum[0], og_got)[0].astype(f32)
    oh = oh + swap(oh.astype(bf16), "context", 1).astype(f32)
    out_grad = oh + swap(oh.astype(bf16), "context", 2).astype(f32)
    m3 = swap(m2, "context", 1)
    up_grad, down_grad = call(
        matrices_kernel, [((d_part, ffq), f32), ((ffq, d_part), f32)], 4, [pltpu.VMEM((ffq, d_part), f32)]
    )(sc, m0, m1, m2, m3)
    in_grad = jnp.transpose((ih + far.astype(f32)).reshape(3, ch, d_part), (2, 0, 1))
    (layer_out,) = call(layer_out_kernel, [(sh, bf16)], 5)(sc, r1, *fs, down_bias)

    first = early[64 + FILT_ROWS :]

    def row_at(x, at):
        return x[at : at + 8].reshape(-1)[:width]

    hid = early[32:64].reshape(WAYS, WAYS, 256)[:, :, :ffs]
    up_bias_grad = lax.dynamic_index_in_dim(hid, t_id, 1, keepdims=False).reshape(ffq)
    fil = early[64 : 64 + FILT_ROWS, :fw]
    fo_own = lax.dynamic_slice_in_dim(late[8 + n_col :, :fw].T, s_id * filt_out.shape[0], filt_out.shape[0], 0)
    colsum = late[:n_col].reshape(n_col // 8, 8, 128).transpose(1, 0, 2).reshape(8, -1)[:, :ch3]
    skip_sum = late[n_col : 8 + n_col].reshape(-1)[:ch]
    conv_all = colsum.reshape(8, 3, ch)
    return (
        layer_out,
        tokens_grad,
        row_at(first, 0),
        row_at(first, 8),
        in_grad,
        conv_all[4],
        conv_all[1:4],
        conv_all[0],
        jnp.concatenate([fil[fw + n_in - 1 : fw + n_in], fil[fw : fw + n_in - 1]]),
        fil[fw + ne],
        fil[:fw],
        fil[fw + ne + 1],
        fil[fw + ne + 2],
        fo_own,
        skip_sum,
        out_grad,
        row_at(early, 16),
        row_at(early, 0),
        row_at(early, 8),
        up_grad,
        up_bias_grad,
        down_grad,
        row_at(early, 24),
    )


def solution(mesh):
    return jax.shard_map(
        functools.partial(body, mesh.shape["shards"]),
        mesh=mesh,
        in_specs=(
            P(("shards", "context"), None),
            P("shards", None),
            P(),
            P(),
            P("shards", None, "tensor"),
            P(None, "tensor"),
            P(None, None, "tensor"),
            P(None, "tensor"),
            P(),
            P(),
            P(),
            P(),
            P(),
            P("shards", "tensor"),
            P("tensor"),
            P("tensor", "shards"),
            P(),
            P(),
            P(),
            P("shards", "tensor"),
            P("tensor"),
            P("tensor", "shards"),
            P(),
            P(("shards", "context"), None),
        ),
        out_specs=(
            P(("shards", "context", "tensor"), None),
            P(("shards", "context", "tensor"), None),
            P(),
            P(),
            P("shards", None, "tensor"),
            P(None, "tensor"),
            P(None, None, "tensor"),
            P(None, "tensor"),
            P(),
            P(),
            P(),
            P(),
            P(),
            P("shards", "tensor"),
            P("tensor"),
            P("tensor", "shards"),
            P(),
            P(),
            P(),
            P("shards", "tensor"),
            P("tensor"),
            P("tensor", "shards"),
            P(),
        ),
        check_vma=False,
    )
```

```python
import functools
import math

import jax
import jax.numpy as jnp
import ml_dtypes
import numpy as np
from jax import lax
from jax.experimental import pallas as pl
from jax.experimental.pallas import tpu as pltpu
from jax.sharding import PartitionSpec as P

BLOCK = 256
TRUNK = 8
NPATH = 10
PATH = 2560
BRANCHES = 4
LEAVES = 8
TREE_BLK = 20
WAYS = 4

f32 = jnp.float32
bf16 = jnp.bfloat16
exact_mode = lax.Precision.HIGHEST
GELU_A = math.sqrt(2.0 / math.pi)
GELU_B = 0.044715


def dft_tables():
    k = np.arange(BLOCK)[None, :]
    n = np.arange(BLOCK)[:, None]
    ang = np.pi * ((2 * k + 1) * n % 1024) / 512.0
    fwd = np.concatenate([np.cos(ang), -np.sin(ang)], axis=1)
    m = BLOCK + np.arange(BLOCK)[None, :]
    kk = np.arange(BLOCK)[:, None]
    ang2 = np.pi * ((2 * kk + 1) * m % 1024) / 512.0
    inv = np.concatenate([np.cos(ang2), -np.sin(ang2)], axis=0) / 256.0
    return fwd.astype(ml_dtypes.bfloat16), inv.astype(ml_dtypes.bfloat16)


def swap(x, axis, k):
    return lax.ppermute(x, axis, [(i, i ^ k) for i in range(WAYS)])


def smem_spec():
    return pl.BlockSpec(memory_space=pltpu.SMEM)


def call(kernel, outs, n_in, scratch=(), limit=24):
    def run(sc, *args):
        assert len(args) == n_in
        vm = pl.BlockSpec(memory_space=pltpu.VMEM)
        return pl.pallas_call(
            kernel,
            out_shape=[jax.ShapeDtypeStruct(s, d) for s, d in outs],
            in_specs=[smem_spec()] + [vm] * n_in,
            out_specs=[vm] * len(outs),
            scratch_shapes=list(scratch),
            compiler_params=pltpu.CompilerParams(vmem_limit_bytes=limit << 20),
        )(sc, *args)

    return run


def after(x, *deps):
    return lax.optimization_barrier((x, deps))[0]


def nt(a, b):
    return lax.dot_general(a, b, (((1,), (1,)), ((), ())), preferred_element_type=f32)


def nn(a, b):
    return lax.dot_general(a, b, (((1,), (0,)), ((), ())), preferred_element_type=f32)


def tn(a, b):
    return lax.dot_general(a, b, (((0,), (0,)), ((), ())), preferred_element_type=f32)


def two(a):
    hi = a.astype(bf16)
    return hi, (a - hi.astype(f32)).astype(bf16)


def row(ref):
    return ref[...].reshape(1, ref.shape[0])


def norm_parts(x):
    mu = jnp.mean(x, axis=-1, keepdims=True)
    xc = x - mu
    rs = lax.rsqrt(jnp.mean(xc * xc, axis=-1, keepdims=True) + 1e-05)
    return xc * rs, rs


def norm_back(nh, rs, dnh):
    m1 = jnp.mean(dnh, axis=-1, keepdims=True)
    m2 = jnp.mean(dnh * nh, axis=-1, keepdims=True)
    return rs * (dnh - m1 - nh * m2)


def share_tiles(t):
    return [((0, 1), 2), ((3, 4), 2), ((5, 6), 7), ((8, 9), 7)][t]


def pack_share(tiles, t, ch, store):
    (a, b), c = share_tiles(t)
    store(0, tiles(a))
    store(ch, tiles(b))
    x = tiles(c)
    low = lax.broadcasted_iota(jnp.int32, (ch // 2, 128), 1) < 64
    top, bot = x[: ch // 2], x[ch // 2 :]
    if t % 2 == 0:
        y = jnp.where(low, top, pltpu.roll(bot, 64, 1))
    else:
        y = jnp.where(low, pltpu.roll(top, 64, 1), bot)
    store(2 * ch, y)


def left_rows(piece, ch):
    x = piece[2 * ch :].astype(f32)
    return jnp.concatenate([x, pltpu.roll(x, 64, 1)], axis=0)


def share_offsets(t):
    odd = t % 2
    return (64 * odd, 64 * odd + 128, 256 * (1 - odd))


def norm1_fwd_kernel(sc, tok, cw, cb, ib, sk, g, b, a1o, colo, rt):
    gain, shift = row(g), row(b)
    ch = sk.shape[0]
    rt[...] = jnp.zeros_like(rt)
    for p in range(3):
        at = slice(p * ch, (p + 1) * ch)
        for k in range(3):
            rt[k : k + 1, at] = cw[k, p : p + 1, :]
        rt[3:4, at] = cb[p : p + 1, :]
        rt[4:5, at] = ib[p : p + 1, :]
        rt[5:6, at] = row(sk)
    colo[...] = rt[...].T

    @pl.loop(0, 5)
    def _(i):
        rows = pl.ds(pl.multiple_of(i * BLOCK, BLOCK), BLOCK)
        nh, _ = norm_parts(tok[rows, :].astype(f32))
        a1o[rows, :] = (nh * gain + shift).astype(bf16)


def proj_kernel(sc, a1, m0, m1, m2, m3, wt, cols, g, bb, zo, zro, go, gvo, uo, u0, u1, u2, u3, rim, zs):
    c = sc[1]
    gain, shift = row(g), row(bb)
    cv = cols[...]
    w0, w1, w2, cb, ib = (cv[:, i : i + 1] for i in range(5))
    ch = go.shape[1]
    cs = ch // WAYS
    lane = lax.broadcasted_iota(jnp.int32, (3 * ch, 128), 1)
    for k, r in enumerate((m0, m1, m2, m3)):
        rim[pl.ds((c ^ k) * 5, 5)] = r[...]
    rows = [rim[jnp.maximum(sc[3 + b], 0)] for b in range(5)]
    nhr, _ = norm_parts(jnp.concatenate(rows, axis=0).astype(f32))
    a1r = (nhr * gain + shift).astype(bf16)
    a1r = jnp.concatenate([a1r, jnp.zeros((6, a1r.shape[1]), bf16)], axis=0)
    zr = (nt(wt[...], a1r) + ib).astype(bf16).astype(f32)
    lane16 = lax.broadcasted_iota(jnp.int32, zr.shape, 1)
    keep = jnp.zeros(zr.shape, f32)
    for b in range(5):
        keep = jnp.where(lane16 // 2 == b, jnp.where(sc[3 + b] >= 0, 1.0, 0.0), keep)
    zr = zr * keep
    zro[...] = jnp.concatenate([zr, jnp.zeros((zr.shape[0], 112), f32)], axis=1).T[:16]
    for b in range(5):
        zs[b] = zr[:, 2 * b : 2 * b + 2]

    for b in range(5):
        zb = (nt(wt[...], a1[b * BLOCK : (b + 1) * BLOCK, :]) + ib).astype(bf16)
        zo[b] = zb
        z = zb.astype(f32)
        far, near = zs[b, :, 0:1], zs[b, :, 1:2]
        r1, r2 = pltpu.roll(z, 1, 1), pltpu.roll(z, 2, 1)
        z1 = jnp.concatenate([jnp.where(lane == 0, near, r1[:, :128]), r1[:, 128:]], axis=1)
        z2 = jnp.concatenate(
            [jnp.where(lane == 0, far, jnp.where(lane == 1, near, r2[:, :128])), r2[:, 128:]], axis=1
        )
        sv = cb + w0 * z + w1 * z1 + w2 * z2
        go[b] = sv[:ch]
        gvo[b] = sv[ch:]
        uo[b] = (sv[2 * ch :] * sv[ch : 2 * ch]).astype(bf16)
        for k, o in enumerate((u0, u1, u2, u3)):
            o[b] = uo[b, pl.ds(pl.multiple_of((c ^ k) * cs, 16), cs), :]


def sincos(x):
    n = jnp.floor(x * (2.0 / math.pi) + 0.5)
    r = ((x - n * 1.5703125) - n * 4.837512969970703125e-4) - n * 7.54978995489188216e-8
    r2 = r * r
    sn = r + r * r2 * (-1.6666654611e-1 + r2 * (8.3321608736e-3 - r2 * 1.9515295891e-4))
    cn = 1.0 - 0.5 * r2 + r2 * r2 * (4.166664568298827e-2 + r2 * (-1.388731625493765e-3 + r2 * 2.443315711809948e-5))
    q = n.astype(jnp.int32)
    odd = (q & 1) == 1
    s1, c1 = jnp.where(odd, cn, sn), jnp.where(odd, sn, cn)
    return jnp.where((q & 2) == 2, -s1, s1), jnp.where(((q + 1) & 2) == 2, -c1, c1)


def exact_nn(a, b):
    return lax.dot_general(a, b, (((1,), (0,)), ((), ())), precision=exact_mode, preferred_element_type=f32)


STEP = 5 * BLOCK


def exact_tn(a, b):
    return lax.dot_general(a, b, (((0,), (0,)), ((), ())), precision=exact_mode, preferred_element_type=f32)


def filter_chunk(d, emb, fin, fmid, fc, bands):
    frv, b1, b2, rate = (fc[:, i : i + 1] for i in range(4))
    pos = (lax.broadcasted_iota(jnp.int32, (1, STEP), 1) + d * STEP).astype(f32)
    k = lax.broadcasted_iota(jnp.int32, (bands, 1), 0).astype(f32)
    freq = 0.0001 + (bands - 1 - 0.0001) * k / max(bands - 1, 1)
    sn, cn = sincos(freq * (2.0 * math.pi * pos / PATH))
    emb[...] = jnp.zeros_like(emb)
    emb[0:bands] = cn
    emb[bands : 2 * bands] = -sn
    lag = pos / (PATH - 1)
    emb[2 * bands : 2 * bands + 1] = lag
    e = emb[...]
    p1 = exact_tn(fin[...], e) + b1
    s1, c1 = sincos(frv * p1)
    p2 = exact_tn(fmid[...], s1) + b2
    s2, c2 = sincos(frv * p2)
    return e, p1, s1, c1, p2, s2, c2, lag, rate


def hidden_kernel(bands, ch, sc, filt_in, fmid, b1, b2, freq, mid, fin, fc, emb, rt):
    n_in, fw = filt_in.shape
    fin[...] = jnp.zeros_like(fin)
    fin[0 : n_in - 1] = filt_in[1:n_in]
    fin[n_in - 1 : n_in] = filt_in[0:1]
    first = (sc[2] * ch + sc[1] * (ch // WAYS)).astype(f32)
    channel = lax.broadcasted_iota(jnp.int32, (1, fw), 1).astype(f32) + first
    slow, fast = math.log(0.01) / 1.5, math.log(0.01) / 0.3
    rt[...] = jnp.zeros_like(rt)
    rt[0:1], rt[1:2], rt[2:3] = row(freq), row(b1), row(b2)
    rt[3:4] = jnp.abs(slow + (fast - slow) * channel / (ch * WAYS - 1))
    fc[...] = rt[...].T

    @pl.loop(0, PATH // STEP)
    def _(d):
        sl = pl.ds(pl.multiple_of(d * STEP, STEP), STEP)
        mid[:, sl] = filter_chunk(d, emb, fin, fmid, fc, bands)[5]


def taps_kernel(sc, mid, fc, fo, taps):
    cs = fo.shape[0]
    lag = lax.broadcasted_iota(jnp.int32, (1, PATH), 1).astype(f32) / (PATH - 1)
    taps[...] = exact_nn(fo[...], mid[...]) * (jnp.exp(-lag * fc[:cs, 3:4]) + 0.05)


def leaf_parent(sc, i):
    return TRUNK - 1 + sc[8 + 1 + BRANCHES + i]


def signs():
    lane = lax.broadcasted_iota(jnp.int32, (1, BLOCK), 1)
    return (1 - 2 * (lane % 2)).astype(f32)


def mul(acc, h, w):
    hr, hi = h[:, :BLOCK], h[:, BLOCK:]
    wr, wi = w[:, :BLOCK], w[:, BLOCK:]
    return acc[0] + (hr * wr - hi * wi), acc[1] + (hr * wi + hi * wr)


def mul_conj(acc, h, w):
    hr, hi = h[:, :BLOCK], h[:, BLOCK:]
    wr, wi = w[:, :BLOCK], w[:, BLOCK:]
    return acc[0] + (hr * wr + hi * wi), acc[1] + (hr * wi - hi * wr)


def conv_kernel(sc, u0, u1, u2, u3, taps, fh, gh, wo, ho, y0, y1, y2, y3, un, sp):
    c = sc[1]
    cs = u0.shape[1]
    for k, r in enumerate((u0, u1, u2, u3)):
        un[pl.ds((c ^ k) * 5, 5)] = r[...]
    for d in range(NPATH):
        thi, tlo = two(taps[:, d * BLOCK : (d + 1) * BLOCK])
        ho[d] = nn(thi, fh[...]) + nn(tlo, fh[...])
    ua = un[...].reshape(TREE_BLK * cs, BLOCK)
    sp[...] = nn(ua, fh[...]).reshape(TREE_BLK, cs, 2 * BLOCK)
    sg = signs()

    def window(k, par):
        a = sp[k]
        wr = sg * a[:, BLOCK:]
        wi = -(sg * a[:, :BLOCK])
        if par is not None:
            q = sp[par]
            wr = wr + q[:, :BLOCK]
            wi = wi + q[:, BLOCK:]
        wo[k, :, :BLOCK] = wr
        wo[k, :, BLOCK:] = wi

    window(0, None)

    @pl.loop(1, TRUNK)
    def _(k):
        window(k, k - 1)

    @pl.loop(0, BRANCHES)
    def _(i):
        window(TRUNK + i, TRUNK - 1)

    @pl.loop(0, LEAVES)
    def _(i):
        window(TRUNK + BRANCHES + i, leaf_parent(sc, i))

    zero = jnp.zeros((cs, BLOCK), f32)

    def put(k, acc):
        sp[k, :, :BLOCK] = acc[0]
        sp[k, :, BLOCK:] = acc[1]

    @pl.loop(0, TRUNK)
    def _(q):
        acc = lax.fori_loop(0, q + 1, lambda d, a: mul(a, ho[d], wo[q - d]), (zero, zero))
        put(q, acc)

    common_b = lax.fori_loop(1, 9, lambda d, a: mul(a, ho[d], wo[8 - d]), (zero, zero))

    @pl.loop(TRUNK, TRUNK + BRANCHES)
    def _(k):
        put(k, mul(common_b, ho[0], wo[k]))

    common_l = lax.fori_loop(2, 10, lambda d, a: mul(a, ho[d], wo[9 - d]), (zero, zero))

    @pl.loop(0, LEAVES)
    def _(i):
        k = TRUNK + BRANCHES + i
        put(k, mul(mul(common_l, ho[0], wo[k]), ho[1], wo[leaf_parent(sc, i)]))

    yhi, ylo = two(sp[...].reshape(TREE_BLK * cs, 2 * BLOCK))
    y = nn(yhi, gh[...]) + nn(ylo, gh[...])
    un[...] = y.astype(bf16).reshape(TREE_BLK, cs, BLOCK)
    for k, o in enumerate((y0, y1, y2, y3)):
        o[...] = un[pl.ds((c ^ k) * 5, 5)]


def gate_kernel(sc, y0, y1, y2, y3, g0, u, cols, yo, p0, p1, p2, p3, ys, gs, pk):
    c, t = sc[1], sc[2]
    cs = y0.shape[1]
    for k, r in enumerate((y0, y1, y2, y3)):
        for b in range(5):
            ys[b, pl.ds(pl.multiple_of((c ^ k) * cs, 16), cs), :] = r[b]
    skip = cols[:, 5:6][: u.shape[1]]
    for b in range(5):
        y = ys[b]
        yo[b] = y
        gs[b] = g0[b] * (y.astype(f32) + skip * u[b].astype(f32))
    pack_all(t, u.shape[1], lambda j: gs[j // 2, :, (j % 2) * 128 : (j % 2) * 128 + 128], pk, (p0, p1, p2, p3))


def pack_all(t, ch, tiles, pk, outs):
    for s in range(WAYS):

        def store(row, v, s=s):
            pk[s, row : row + v.shape[0]] = v.astype(bf16)

        pack_share(tiles, s, ch, store)
    for k, o in enumerate(outs):
        if o is not None:
            o[...] = pk[t ^ k]


def unpack_all(t, ch, ins, pk, put):
    for k, r in enumerate(ins):
        pk[t ^ k] = r[...]
    for s in range(WAYS):
        (a, b), _ = share_tiles(s)
        put(a, pk[s, 0:ch].astype(f32))
        put(b, pk[s, ch : 2 * ch].astype(f32))
    low = lax.broadcasted_iota(jnp.int32, (ch // 2, 128), 1) < 64
    for j, (s0, s1) in ((2, (0, 1)), (7, (2, 3))):
        x0 = pk[s0, 2 * ch :].astype(f32)
        x1 = pk[s1, 2 * ch :].astype(f32)
        top = jnp.where(low, x0, pltpu.roll(x1, 64, 1))
        bot = jnp.where(low, pltpu.roll(x0, 64, 1), x1)
        put(j, jnp.concatenate([top, bot], axis=0))


def sides(sc, half):
    h = sc[0]
    return pl.ds(pl.multiple_of(h * half, 128), half), pl.ds(pl.multiple_of((1 - h) * half, 128), half)


def mix_kernel(sc, p0, p1, p2, p3, owm, owo, tok, ob, g2, b2, r1o, a2o, acc):
    t = sc[2]
    ch, half = p0.shape[0] * 2 // 5, owm.shape[2]
    mine, other = sides(sc, half)
    offs = share_offsets(t)
    parts = [None, None, None]
    for k, r in enumerate((p0, p1, p2, p3)):
        wm, wo = owm[k, :ch], owo[k, :ch]
        piece = r[...]
        xs = (piece[:ch].astype(f32), piece[ch : 2 * ch].astype(f32), left_rows(piece, ch))
        for i, x in enumerate(xs):
            xt = x.T.astype(bf16)
            v = (nn(xt, wm), nn(xt, wo))
            parts[i] = v if parts[i] is None else (parts[i][0] + v[0], parts[i][1] + v[1])
    for i, n in ((0, 128), (1, 128), (2, 64)):
        at = pl.ds(pl.multiple_of(offs[i], 64), n)
        acc[at, mine] = parts[i][0][:n]
        acc[at, other] = parts[i][1][:n]
    r1 = tok[...].astype(f32) + (acc[...] + row(ob))
    r1o[...] = r1
    nh, _ = norm_parts(r1)
    a2o[...] = (nh * row(g2) + row(b2)).astype(bf16)


def stacked(ref, at, n):
    return jnp.concatenate([ref[k, at : at + n] for k in range(WAYS)], axis=0)


def mlp_kernel(ch, sc, xa, xb, ca, cb, um, uo, dm, do, upb, dpo, aco, pa, pb):
    mine, other = sides(sc, um.shape[2])
    bias = upb[...]
    ffs = dm.shape[1]
    u_m, u_o = stacked(um, ch, ffs), stacked(uo, ch, ffs)
    d_m, d_o = stacked(dm, 0, ffs), stacked(do, 0, ffs)
    n = pa.shape[0]
    for i, (x, ct, po) in enumerate(((xa, ca, pa), (xb, cb, pb))):
        at = slice(i * n, (i + 1) * n)
        p = nt(x[:, mine], u_m) + nt(x[:, other], u_o) + bias
        d = nt(ct[:, mine], d_m) + nt(ct[:, other], d_o)
        p2 = p * p
        th = jnp.tanh(GELU_A * p * (1.0 + GELU_B * p2))
        half = 0.5 * (1.0 + th)
        aco[at] = (p * half).astype(bf16)
        slope = half + 0.5 * p * (1.0 - th * th) * (GELU_A * (1.0 + 3.0 * GELU_B * p2))
        dp = (d * slope).astype(bf16)
        dpo[at] = dp
        po[:, mine] = nn(dp, u_m).astype(bf16)
        po[:, other] = nn(dp, u_o).astype(bf16)


def ffn_part(sc, ac, dm, do, f0, f1):
    mine, other = sides(sc, dm.shape[2])
    n = dm.shape[1]
    d_m, d_o = stacked(dm, 0, n), stacked(do, 0, n)
    m = f0.shape[0]
    for i, out in enumerate((f0, f1)):
        a = ac[i * m : (i + 1) * m]
        out[:, mine] = nn(a, d_m).astype(bf16)
        out[:, other] = nn(a, d_o).astype(bf16)


def put_grad(sc, outs, v, mat):
    n = v.shape[0] // WAYS
    if len(outs) == 1:
        for q in range(WAYS):
            outs[0][q, mat] = v[q * n : (q + 1) * n].astype(bf16)
        return
    m = v.shape[1] // 2
    first = sc[0] == 0
    for q in range(WAYS):
        a, b = v[q * n : (q + 1) * n, :m], v[q * n : (q + 1) * n, m:]
        outs[0][q, mat] = jnp.where(first, a, b).astype(bf16)
        outs[1][q, mat] = jnp.where(first, b, a).astype(bf16)


def tn_pair(a, b0, b1):
    m = b0.shape[0]
    return tn(a[:m], b0[...]) + tn(a[m:], b1[...])


def mlp_grad_one_kernel(sc, x0, x1, dp, ac, c0, c1, dm, do, out, ub, f0, f1):
    out[0] = tn_pair(dp, x0, x1).astype(bf16)
    out[1] = tn_pair(ac, c0, c1).astype(bf16)
    ub[...] = jnp.sum(dp[...].astype(f32), axis=0, keepdims=True)
    ffn_part(sc, ac, dm, do, f0, f1)


def mlp_grad_two_kernel(sc, x0, x1, dp, ac, c0, c1, one, ubone, dm, do, *outs):
    *grads, ub, f0, f1 = outs
    put_grad(sc, grads, one[0].astype(f32) + tn_pair(dp, x0, x1), 0)
    put_grad(sc, grads, one[1].astype(f32) + tn_pair(ac, c0, c1), 1)
    ub[...] = ubone[...] + jnp.sum(dp[...].astype(f32), axis=0, keepdims=True)
    ffn_part(sc, ac, dm, do, f0, f1)


def norm2_kernel(sc, own, core, far, r1, cot, g2, owm, owo, dro, dmo, sums, p0, p1, p2, p3):
    t = sc[2]
    sums[...] = jnp.zeros_like(sums)
    dn2 = own[...].astype(f32) + core[...].astype(f32) + far[...].astype(f32)
    nh, rs = norm_parts(r1[...])
    ct = cot[...].astype(f32)
    sums[0:1] = jnp.sum(dn2 * nh, axis=0, keepdims=True)
    sums[1:2] = jnp.sum(dn2, axis=0, keepdims=True)
    dr = ct + norm_back(nh, rs, dn2 * row(g2))
    dro[...] = dr
    dm = dr.astype(bf16)
    dmo[...] = dm
    sums[2:3] = jnp.sum(dm.astype(f32), axis=0, keepdims=True)
    sums[3:4] = jnp.sum(ct, axis=0, keepdims=True)
    offs = share_offsets(t)
    ch, half = p0.shape[0] * 2 // 5, owm.shape[2]
    mine, other = sides(sc, half)
    low = lax.broadcasted_iota(jnp.int32, (ch // 2, 128), 1) < 64
    at = [pl.ds(pl.multiple_of(offs[i], 64), n) for i, n in ((0, 128), (1, 128), (2, 64))]
    dms = [(dmo[a, mine], dmo[a, other]) for a in at]
    dms[2] = tuple(jnp.concatenate([v, v], axis=0) for v in dms[2])
    for k, o in enumerate((p0, p1, p2, p3)):
        wm, wo = owm[k, :ch], owo[k, :ch]
        vs = [nt(wm, a) + nt(wo, b) for a, b in dms]
        o[0:ch] = vs[0].astype(bf16)
        o[ch : 2 * ch] = vs[1].astype(bf16)
        o[2 * ch :] = jnp.where(low, vs[2][: ch // 2], vs[2][ch // 2 :]).astype(bf16)


def out_grad_kernel(sc, p0, p1, p2, p3, dm, *outs):
    t = sc[2]
    offs = share_offsets(t)
    ch = p0.shape[0] * 2 // 5
    da = dm[pl.ds(pl.multiple_of(offs[0], 64), 128), :]
    db = dm[pl.ds(pl.multiple_of(offs[1], 64), 128), :]
    dc = dm[pl.ds(pl.multiple_of(offs[2], 64), 64), :]
    vs = []
    for r in (p0, p1, p2, p3):
        piece = r[...]
        left = left_rows(piece, ch)[:, :64].astype(bf16)
        vs.append(nn(piece[:ch], da) + nn(piece[ch : 2 * ch], db) + nn(left, dc))
    put_grad(sc, outs, jnp.concatenate(vs, axis=0), 0)


def ungate_kernel(sc, p0, p1, p2, p3, g0, ys, u, cols, dyo, dgo, so, d0, d1, d2, d3, pk, dg):
    c, t = sc[1], sc[2]
    ch = u.shape[1]
    cs = ch // WAYS

    def put(j, v):
        dg[j // 2, :, (j % 2) * 128 : (j % 2) * 128 + 128] = v

    unpack_all(t, ch, (p0, p1, p2, p3), pk, put)
    skip = cols[:, 5:6][:ch]
    tot = None
    for b in range(5):
        g = dg[b]
        uu = u[b].astype(f32)
        dgo[b] = g * (ys[b].astype(f32) + skip * uu)
        dy = g * g0[b]
        v = jnp.sum(dy * uu, axis=1, keepdims=True)
        tot = v if tot is None else tot + v
        dyo[b] = dy.astype(bf16)
    so[...] = tot
    for k, o in enumerate((d0, d1, d2, d3)):
        for b in range(5):
            o[b] = dyo[b, pl.ds(pl.multiple_of((c ^ k) * cs, 16), cs), :]


def conv_back_kernel(sc, d0, d1, d2, d3, ws, hs, fh, gh, dho, o0, o1, o2, o3, un, dy, dw, dh):
    c = sc[1]
    cs = d0.shape[1]
    for k, r in enumerate((d0, d1, d2, d3)):
        un[pl.ds((c ^ k) * 5, 5)] = r[...]
    da = un[...].reshape(TREE_BLK * cs, BLOCK)
    dy[0:TREE_BLK] = nt(da, gh[...]).reshape(TREE_BLK, cs, 2 * BLOCK)
    zero = jnp.zeros((cs, BLOCK), f32)
    zz = jnp.zeros((cs, 2 * BLOCK), f32)
    first_leaf = TRUNK + BRANCHES
    sum_b = lax.fori_loop(TRUNK, first_leaf, lambda k, a: a + dy[k], zz)
    sum_l = lax.fori_loop(first_leaf, TREE_BLK, lambda k, a: a + dy[k], zz)
    dy[TREE_BLK] = sum_b
    dy[TREE_BLK + 1] = sum_l
    for i in range(BRANCHES):
        dy[TREE_BLK + 2 + i] = zz

    @pl.loop(0, LEAVES)
    def _(i):
        k = TREE_BLK + 2 + leaf_parent(sc, i) - TRUNK
        dy[k] = dy[k] + dy[first_leaf + i]


    def put(ref, k, acc):
        ref[k, :, :BLOCK] = acc[0]
        ref[k, :, BLOCK:] = acc[1]

    @pl.loop(0, TRUNK)
    def _(j):
        acc = lax.fori_loop(j, TRUNK, lambda q, a: mul_conj(a, hs[q - j], dy[q]), (zero, zero))
        acc = mul_conj(acc, hs[8 - j], dy[TREE_BLK])
        put(dw, j, mul_conj(acc, hs[9 - j], dy[TREE_BLK + 1]))

    @pl.loop(0, BRANCHES)
    def _(i):
        k = TRUNK + i
        acc = mul_conj((zero, zero), hs[0], dy[k])
        put(dw, k, mul_conj(acc, hs[1], dy[TREE_BLK + 2 + i]))

    @pl.loop(first_leaf, TREE_BLK)
    def _(k):
        put(dw, k, mul_conj((zero, zero), hs[0], dy[k]))


    @pl.loop(0, TRUNK)
    def _(d):
        put(dh, d, lax.fori_loop(d, TRUNK, lambda q, a: mul_conj(a, ws[q - d], dy[q]), (zero, zero)))

    put(dh, 8, (zero, zero))
    put(dh, 9, (zero, zero))

    def more(d, k, q):
        acc = (dh[d, :, :BLOCK], dh[d, :, BLOCK:])
        put(dh, d, mul_conj(acc, ws[k], dy[q]))

    @pl.loop(1, 9)
    def _(d):
        more(d, 8 - d, TREE_BLK)

    @pl.loop(2, 10)
    def _(d):
        more(d, 9 - d, TREE_BLK + 1)

    @pl.loop(TRUNK, TREE_BLK)
    def _(k):
        more(0, k, k)

    @pl.loop(0, BRANCHES)
    def _(i):
        more(1, TRUNK + i, TREE_BLK + 2 + i)

    for d in range(NPATH):
        thi, tlo = two(dh[d])
        dho[:, d * BLOCK : (d + 1) * BLOCK] = nt(thi, fh[...]) + nt(tlo, fh[...])

    sg = signs()

    def own(k):
        w = dw[k]
        return jnp.concatenate([-(sg * w[:, BLOCK:]), sg * w[:, :BLOCK]], axis=1)

    @pl.loop(0, TRUNK - 1)
    def _(k):
        dy[k] = own(k) + dw[k + 1]

    dy[TRUNK - 1] = lax.fori_loop(TRUNK, first_leaf, lambda k, a: a + dw[k], own(TRUNK - 1))

    @pl.loop(TRUNK, TREE_BLK)
    def _(k):
        dy[k] = own(k)

    @pl.loop(0, LEAVES)
    def _(i):
        k = leaf_parent(sc, i)
        dy[k] = dy[k] + dw[first_leaf + i]

    shi, slo = two(dy[0:TREE_BLK].reshape(TREE_BLK * cs, 2 * BLOCK))
    du = nt(shi, fh[...]) + nt(slo, fh[...])
    un[...] = du.astype(bf16).reshape(TREE_BLK, cs, BLOCK)
    for k, o in enumerate((o0, o1, o2, o3)):
        o[...] = un[pl.ds((c ^ k) * 5, 5)]


def unconv_kernel(sc, u0, u1, u2, u3, dyv, dg0, gv, z, zr, cols, dzo, rims, cg, dus, rs, acc, zc, zs):
    c = sc[1]
    ch = dyv.shape[1]
    cs = ch // WAYS
    cv = cols[...]
    w0, w1, w2 = (cv[:, i : i + 1] for i in range(3))
    skip = cv[:ch, 5:6]
    lane = lax.broadcasted_iota(jnp.int32, (3 * ch, 128), 1)
    rs[...] = jnp.zeros_like(rs)
    acc[...] = jnp.zeros_like(acc)

    def fold(i, v):
        acc[i] = acc[i] + (v[:, :128] + v[:, 128:])

    zc[...] = jnp.zeros_like(zc)
    zc[0:16] = zr[...]
    zcol = zc[...].T
    for b in range(5):
        zs[b] = zcol[:, 2 * b : 2 * b + 2]

    @pl.loop(0, 5)
    def _(b):
        for k, r in enumerate((u0, u1, u2, u3)):
            dus[pl.ds(pl.multiple_of((c ^ k) * cs, 16), cs), :] = r[b]
        du = dus[...].astype(f32) + skip * dyv[b].astype(f32)
        sv = gv[b]
        ds = jnp.concatenate([dg0[b], du * sv[ch:], du * sv[:ch]], axis=0)
        zv = z[b].astype(f32)
        far, near = zs[b, :, 0:1], zs[b, :, 1:2]
        r1, r2 = pltpu.roll(ds, BLOCK - 1, 1), pltpu.roll(ds, BLOCK - 2, 1)
        n1 = jnp.concatenate([r1[:, :128], jnp.where(lane == 127, 0.0, r1[:, 128:])], axis=1)
        n2 = jnp.concatenate([r2[:, :128], jnp.where(lane >= 126, 0.0, r2[:, 128:])], axis=1)
        dzo[b] = w0 * ds + w1 * n1 + w2 * n2
        d0, d1 = ds[:, 0:1], ds[:, 1:2]
        fold(0, ds)
        fold(1, ds * zv)
        fold(2, n1 * zv)
        fold(3, n2 * zv)
        acc[2] = acc[2] + jnp.where(lane == 0, d0 * near, 0.0)
        acc[3] = acc[3] + jnp.where(lane == 0, d0 * far + d1 * near, 0.0)
        rs[...] = rs[...] + jnp.where(lane == 2 * b, w2 * d0, jnp.where(lane == 2 * b + 1, w1 * d0 + w2 * d1, 0.0))

    rims[...] = rs[...].T[:16]
    out = jnp.zeros(lane.shape, f32)
    for i in range(4):
        out = jnp.where(lane == i, jnp.sum(acc[i], axis=1, keepdims=True), out)
    cg[...] = out


def dz_kernel(sc, dzo, r0, r1, r2, r3, pick, dz, p0, p1, p2, p3, ib, rall, rt, pk):
    c, t = sc[1], sc[2]
    rows = dzo.shape[1]
    for k, r in enumerate((r0, r1, r2, r3)):
        rall[pl.ds(pl.multiple_of((c ^ k) * 16, 16), 16), :] = r[...]
    got = lax.dot_general(
        pick[...], rall[...], (((1,), (0,)), ((), ())), precision=exact_mode, preferred_element_type=f32
    )
    rt[...] = got.T
    lane = lax.broadcasted_iota(jnp.int32, (rows, 128), 1)
    tot = None
    for b in range(5):
        add = jnp.where(lane >= 126, pltpu.roll(rt[...], 126 - 2 * b, 1), 0.0)
        lo = dzo[b, :, :128].astype(bf16)
        hi = (dzo[b, :, 128:] + add).astype(bf16)
        dz[b, :, :128] = lo
        dz[b, :, 128:] = hi
        v = jnp.sum(lo.astype(f32) + hi.astype(f32), axis=1, keepdims=True)
        tot = v if tot is None else tot + v
    ib[...] = tot
    pack_all(t, rows, lambda j: dz[j // 2, :, (j % 2) * 128 : (j % 2) * 128 + 128].astype(f32), pk, (p0, p1, p2, p3))


def in_grad_kernel(sc, dz, a1, wt, ib, g, b1, *outs):
    acc = None
    for b in range(5):
        v = nn(dz[b], a1[b * BLOCK : (b + 1) * BLOCK, :])
        acc = v if acc is None else acc + v
    sums = outs[-1]
    if len(outs) == 2:
        outs[0][...] = acc
    else:
        n = acc.shape[1] // 2
        first = sc[0] == 0
        outs[0][...] = jnp.where(first, acc[:, :n], acc[:, n:])
        outs[1][...] = jnp.where(first, acc[:, n:], acc[:, :n]).astype(bf16)
    w = wt[...].astype(f32)
    gsum = jnp.sum(w * acc, axis=0, keepdims=True)
    bsum = jnp.sum(w * ib[...], axis=0, keepdims=True)
    sums[...] = jnp.zeros_like(sums)
    sums[0:1] = (gsum - row(b1) * bsum) / row(g)
    sums[1:2] = bsum


FILT_ROWS = 112


def put_row(out, at, row):
    n = row.shape[1]
    k = -(-n // 128)
    for j in range(k):
        w = min(128, n - 128 * j)
        out[pl.ds(at + j, 1), :w] = row[:, 128 * j : 128 * j + w]
    return k


def pack_kernel(sc, sums1, sums2, ub, filt, fo, cg, ib, skip, out, colt):
    c, t = sc[1], sc[2]
    out[...] = jnp.zeros_like(out)
    for i in range(4):
        put_row(out, 8 * i, sums2[i : i + 1])
    n = ub.shape[1] // WAYS
    for q in range(WAYS):
        put_row(out, 32 + 2 * (WAYS * c + (t ^ q)), ub[0:1, q * n : (q + 1) * n])
    out[64 : 64 + FILT_ROWS, : filt.shape[1]] = filt[...]
    at = 64 + FILT_ROWS
    put_row(out, at, sums1[0:1])
    put_row(out, at + 8, sums1[1:2])
    at += 16
    lane = lax.broadcasted_iota(jnp.int32, cg.shape, 1)
    colt[...] = jnp.where(lane == 4, ib[...], cg[...]).T
    m = cg.shape[0]
    for j in range(-(-m // 128)):
        w = min(128, m - 128 * j)
        out[at : at + 8, :w] = colt[0:8, 128 * j : 128 * j + w]
        at += 8
    ch = skip.shape[0]
    put_row(out, at, jnp.broadcast_to(skip[...], (ch, 128)).T[0:1])
    at += 8
    cs = fo.shape[0]
    out[pl.ds(at + c * cs, cs), : fo.shape[1]] = fo[...]


def filter_back_kernel(bands, sc, dt, fin, fc, fo, fm, out, fog, emb):
    def three(dot, a, b):
        (ah, al), (bh, bl) = two(a), two(b)
        return dot(ah, bh) + dot(ah, bl) + dot(al, bh)

    n, ne, cs = fm.shape[0], emb.shape[0], fo.shape[0]
    fov, fmv, frv = fo[...], fm[...], fc[:, 0:1]

    def step(d, acc):
        a_fo, a_fm, a_fi, a_b1, a_b2, a_fr = acc
        e, q1, one, c1, q2, mid, c2, lag, rate = filter_chunk(d, emb, fin, fm, fc, bands)
        sl = pl.ds(pl.multiple_of(d * STEP, STEP), STEP)
        draw = dt[:, sl] * (jnp.exp(-lag * rate[:cs]) + 0.05)
        a_fo = a_fo + three(nt, draw, mid)
        da2 = three(tn, fov, draw) * c2
        dp2 = da2 * frv
        a_fm = a_fm + three(nt, one, dp2)
        da1 = three(nn, fmv, dp2) * c1
        dp1 = da1 * frv
        a_fi = a_fi + three(nt, e, dp1)
        sums = [jnp.sum(v, axis=1, keepdims=True) for v in (dp1, dp2, da2 * q2 + da1 * q1)]
        return a_fo, a_fm, a_fi, a_b1 + sums[0], a_b2 + sums[1], a_fr + sums[2]

    zero = jnp.zeros((n, 1), f32)
    init = (jnp.zeros(fog.shape, f32), jnp.zeros((n, n), f32), jnp.zeros((ne, n), f32), zero, zero, zero)
    a_fo, a_fm, a_fi, *cols = lax.fori_loop(0, PATH // STEP, step, init)
    fog[...] = a_fo
    out[...] = jnp.zeros_like(out)
    out[0:n] = a_fm
    out[n : n + ne] = a_fi
    lane = lax.broadcasted_iota(jnp.int32, (n, 128), 1)
    m = jnp.where(lane == 0, cols[0], jnp.where(lane == 1, cols[1], jnp.where(lane == 2, cols[2], 0.0)))
    out[n + ne : n + ne + 8] = m.T[0:8]


def piece_product(r, w, parts):
    rows = w.shape[0]
    piece = r[...]
    xs = (piece[:rows].astype(f32), piece[rows : 2 * rows].astype(f32), left_rows(piece, rows))
    for i, x in enumerate(xs):
        v = nn(x.T.astype(bf16), w)
        parts[i] = v if parts[i] is None else parts[i] + v


def put_parts(sc, parts, acc, old=None):
    offs = share_offsets(sc[2])
    for i, n in ((0, 128), (1, 128), (2, 64)):
        at = pl.ds(pl.multiple_of(offs[i], 64), n)
        acc[at, :] = parts[i][:n] if old is None else parts[i][:n] + old[at, :]


def norm1_part_kernel(sc, p0, p1, p3, w0, wa, wb, wc, wd, acc, w2, wr):
    n = wa.shape[1]
    mine, other = sides(sc, wa.shape[2])
    h = sc[1] & 1
    near, far = pl.ds(pl.multiple_of(h * n, 16), n), pl.ds(pl.multiple_of((1 - h) * n, 16), n)
    for i, w in ((0, wr.at[0]), (1, w2), (2, wr.at[1])):
        w[near, mine], w[near, other] = wa[i], wb[i]
        w[far, mine], w[far, other] = wc[i], wd[i]
    parts = [None, None, None]
    for r, w in ((p0, w0), (p1, wr.at[0]), (p3, wr.at[1])):
        piece_product(r, w[...], parts)
    put_parts(sc, parts, acc)


def norm1_kernel(sc, part, p2, w2, tok, dr, g, out, acc):
    parts = [None, None, None]
    piece_product(p2, w2[...], parts)
    put_parts(sc, parts, acc, part)
    nh, rs = norm_parts(tok[...].astype(f32))
    out[...] = (dr[...] + norm_back(nh, rs, acc[...] * row(g))).astype(bf16)


def matrices_kernel(sc, m0, m1, m2, m3, upo, downo, rows):
    c = sc[1]
    n = m0.shape[1]
    for k, m in enumerate((m0, m1, m2, m3)):
        at = pl.ds(pl.multiple_of((c ^ k) * n, 64), n)
        rows[at, :] = m[0].astype(f32)
        downo[at, :] = m[1].astype(f32)
    upo[...] = rows[...].T


def layer_out_kernel(sc, r1, own, core, far, db, out):
    ffn = own[...].astype(f32) + core[...].astype(f32) + far[...].astype(f32)
    out[...] = (r1[...] + ffn + row(db)).astype(bf16)


def body(
    shard_count,
    tokens,
    parents,
    norm1_gain,
    norm1_bias,
    in_weight,
    in_bias,
    conv_weight,
    conv_bias,
    filt_in,
    filt_bias1,
    filt_mid,
    filt_bias2,
    sine_freq,
    filt_out,
    skip_gain,
    out_weight,
    out_bias,
    norm2_gain,
    norm2_bias,
    up_weight,
    up_bias,
    down_weight,
    down_bias,
    cotangent,
):
    rows, width = tokens.shape
    ch = skip_gain.shape[0]
    cs = ch // WAYS
    ch3 = 3 * ch
    ffq = up_bias.shape[0]
    ffs = ffq // WAYS
    share = rows // WAYS
    d_part = in_weight.shape[0]
    s_id = lax.axis_index("shards")
    c_id = lax.axis_index("context")
    t_id = lax.axis_index("tensor")
    pair = shard_count == 2

    def gather_shards(x, axis, *deps):
        if not pair:
            return lax.all_gather(x, "shards", axis=axis, tiled=True)
        o = lax.ppermute(x, "shards", [(0, 1), (1, 0)])
        o = after(o, *deps) if deps else o
        lo = jnp.where(s_id == 0, x, o)
        hi = jnp.where(s_id == 0, o, x)
        return jnp.concatenate([lo, hi], axis=axis)

    par = parents[0]
    all_par = jnp.concatenate(
        [jnp.arange(-1, TRUNK - 1, dtype=jnp.int32), jnp.full((BRANCHES,), TRUNK - 1, jnp.int32), TRUNK - 1 + par[1 + BRANCHES :]]
    )
    own_par = lax.dynamic_slice_in_dim(all_par, c_id * 5, 5, 0)
    side = s_id if pair else jnp.zeros_like(s_id)
    sc = jnp.concatenate([jnp.stack([side, c_id, t_id]).astype(jnp.int32), own_par, par]).astype(jnp.int32)

    def swap_y(x):
        return lax.ppermute(x, "shards", [(0, 1), (1, 0)])

    n_in, fw = filt_in.shape
    bands = (n_in - 1) // 2
    ne = -(-n_in // 8) * 8
    hidden, fin, fc = call(
        functools.partial(hidden_kernel, bands, ch),
        [((fw, PATH), f32), ((ne, fw), f32), ((fw, 128), f32)],
        5,
        [pltpu.VMEM((ne, STEP), f32), pltpu.VMEM((128, fw), f32)],
    )(sc, filt_in, filt_mid, filt_bias1, filt_bias2, sine_freq)

    wt_part = jnp.transpose(in_weight, (1, 2, 0)).reshape(ch3, d_part)
    wt = gather_shards(wt_part, 1, hidden)
    rim_tok = tokens.reshape(5, BLOCK, width)[:, BLOCK - 2 :, :]
    rims_in = [rim_tok] + [swap(rim_tok, "context", k) for k in (1, 2, 3)]
    up_t = lax.dynamic_slice_in_dim(up_weight, c_id * ffs, ffs, 1).T
    down_c = lax.dynamic_slice_in_dim(down_weight, c_id * ffs, ffs, 0)
    bias_c = lax.dynamic_slice_in_dim(up_bias, c_id * ffs, ffs, 0)
    b_hi, b_mid = two(bias_c)
    b_lo = (bias_c - b_hi.astype(f32) - b_mid.astype(f32)).astype(bf16)
    wide = d_part >= ffs
    if wide:
        b_rows = jnp.stack([b_hi, b_mid, b_lo] + [jnp.zeros_like(b_hi)] * 13)
        b_rows = jnp.concatenate([b_rows, jnp.zeros((16, d_part - ffs), bf16)], axis=1)
        two_mats = jnp.concatenate([out_weight, up_t, b_rows])
    else:
        two_mats = jnp.concatenate([out_weight, up_t])
    def columns(parts):
        m = jnp.stack(parts)
        if pair:
            return m, swap_y(m)
        m = lax.all_gather(m, "shards", axis=2, tiled=True)
        return m[:, :, : width // 2], m[:, :, width // 2 :]

    parts_b = [down_c] + [swap(down_c, "tensor", k) for k in (1, 2, 3)]
    down = columns(after(tuple(parts_b), hidden))
    parts_a = [two_mats] + [swap(two_mats, "tensor", k) for k in (1, 2, 3)]
    if pair:
        fo_other = swap_y(filt_out)
        fo = jnp.concatenate([jnp.where(s_id == 0, filt_out, fo_other), jnp.where(s_id == 0, fo_other, filt_out)], axis=0)
    else:
        fo = fo_other = lax.all_gather(filt_out, "shards", axis=0, tiled=True)
    fo_t = lax.dynamic_slice_in_dim(fo, c_id * cs, cs, 1).astype(f32).T

    fh, gh = (jnp.asarray(a) for a in dft_tables())

    nb, B = 5, BLOCK
    piece = ((nb, cs, B), bf16)
    a1, cols = call(norm1_fwd_kernel, [((rows, width), bf16), ((ch3, 128), f32)], 7, [pltpu.VMEM((128, ch3), f32)])(
        after(sc, wt, down[0], fo_other), tokens, conv_weight, conv_bias, in_bias, skip_gain, norm1_gain, norm1_bias
    )
    z, zr, g0, gv, u, u0, u1, u2, u3 = call(
        proj_kernel,
        [((nb, ch3, B), bf16), ((16, ch3), f32), ((nb, ch, B), f32), ((nb, 2 * ch, B), f32), ((nb, ch, B), bf16)]
        + [piece] * 4,
        9,
        [pltpu.VMEM((TREE_BLK, 2, width), bf16), pltpu.VMEM((nb, ch3, 2), f32)],
    )(sc, a1, *rims_in, wt, cols, norm1_gain, norm1_bias)

    def ctx(p):
        return (p[0], swap(p[1], "context", 1), swap(p[2], "context", 2), swap(p[3], "context", 3))

    def ten(p):
        return (p[0], swap(p[1], "tensor", 1), swap(p[2], "tensor", 2), swap(p[3], "tensor", 3))

    un = ctx((u0, u1, u2, u3))
    (taps,) = call(taps_kernel, [((cs, PATH), f32)], 3)(after(sc, u0), hidden, fc, fo_t)
    mats = columns(after(tuple(parts_a), un))
    if wide:
        up_b = jnp.concatenate([p[ch + ffs : ch + ffs + 3, :ffs].astype(f32).sum(0) for p in parts_a]).reshape(1, ffq)
    else:
        up_b = jnp.concatenate([bias_c] + [swap(bias_c, "tensor", k) for k in (1, 2, 3)]).reshape(1, ffq)
    up_b = after(up_b, u0)
    spec = ((TREE_BLK, cs, 2 * B), f32)
    ws, hs, y0, y1, y2, y3 = call(
        conv_kernel,
        [spec, ((NPATH, cs, 2 * B), f32)] + [piece] * 4,
        7,
        [pltpu.VMEM((TREE_BLK, cs, B), bf16), pltpu.VMEM((TREE_BLK, cs, 2 * B), f32)],
    )(sc, *un, taps, fh, gh)
    yn = ctx((y0, y1, y2, y3))
    tok_share = lax.dynamic_slice_in_dim(tokens, t_id * share, share, 0)
    cot_share = lax.dynamic_slice_in_dim(cotangent, t_id * share, share, 0)
    tok_share, cot_share = after((tok_share, cot_share), u0)

    packs = (5 * ch // 2, 128)
    packed_out = [(packs, bf16)] * 4
    ys, *gp = call(
        gate_kernel,
        [((nb, ch, B), bf16)] + packed_out,
        7,
        [pltpu.VMEM((nb, ch, B), bf16), pltpu.VMEM((nb, ch, B), f32), pltpu.VMEM((WAYS,) + packs, bf16)],
    )(sc, *yn, g0, after(u, mats[0]), cols)
    gn = ten(gp)
    cot_share = after(cot_share, ys)
    cot1 = swap(cot_share, "context", 1)
    cot2 = swap(cot_share, "context", 2)

    sh = (share, width)
    r1, a2 = call(mix_kernel, [(sh, f32), (sh, bf16)], 10, [pltpu.VMEM(sh, f32)])(
        sc, *gn, *mats, after(tok_share, up_b), out_bias, norm2_gain, norm2_bias
    )

    x1 = swap(a2, "context", 1)
    x2 = swap(a2, "context", 2)
    cot3 = swap(after(cot2, a2), "context", 1)
    odd = c_id & 1
    w_half = lax.dynamic_slice_in_dim(wt, odd * (ch3 // 2), ch3 // 2, 0)
    w_quarter = after(lax.dynamic_slice_in_dim(w_half, side * (width // 2), width // 2, 1), a2)
    w_got = [swap(w_quarter, "tensor", k) for k in (1, 2, 3)]
    mlp = call(functools.partial(mlp_kernel, ch), [((2 * share, ffq), bf16)] * 2 + [(sh, bf16)] * 2, 9)
    dpa, aca, n0, n1 = mlp(sc, a2, x1, cot_share, cot1, *mats, *down, up_b)
    one, ub_one, f0, f1 = call(mlp_grad_one_kernel, [((2, ffq, width), bf16), ((1, ffq), f32), (sh, bf16), (sh, bf16)], 8)(
        after(sc, n0), a2, x1, dpa, aca, cot_share, cot1, *down
    )
    x2 = after(x2, one, w_got[0], w_got[2])
    x3 = swap(x2, "context", 1)
    dpb, acb, n2, n3 = mlp(sc, x2, x3, cot2, cot3, *mats, *down, up_b)
    one, ub_one, f0, f1 = after((one, ub_one, f0, f1), n2)

    def sum_context(q0, q1, q2, q3, *deps):
        a = swap(q1, "context", 1)
        b = swap(q3, "context", 1)
        b = after(b, *deps) if deps else b
        mid = (q2.astype(f32) + b.astype(f32)).astype(bf16)
        return q0, a, swap(mid, "context", 2)

    dn = sum_context(n0, n1, n2, n3)
    n_grad = 2 if pair else 1
    gcol = width // n_grad
    *mg, ub, f2, f3 = call(
        mlp_grad_two_kernel, [((WAYS, 2, ffs, gcol), bf16)] * n_grad + [((1, ffq), f32), (sh, bf16), (sh, bf16)], 10
    )(after(sc, n2), x2, x3, dpb, acb, cot2, cot3, one, ub_one, *down)
    dn = dn[:2] + (after(dn[2], mg),)
    dr1, dm, sums2, *dgp = call(norm2_kernel, [(sh, f32), (sh, bf16), ((8, width), f32)] + packed_out, 8)(
        sc, *dn, r1, cot_share, norm2_gain, *mats
    )
    f1, w_got = after((f1, w_got), dm)
    wa = jnp.stack(w_got)
    if pair:
        wb = swap_y(wa)
    else:
        other = lax.dynamic_slice_in_dim(w_half, width // 2, width // 2, 1)
        wb = jnp.stack([swap(after(other, dm), "tensor", k) for k in (1, 2, 3)])
    dgn = ten(dgp)

    og = call(out_grad_kernel, [((WAYS, 1, ch, gcol), bf16)] * n_grad, 5)(sc, *gn, dm)

    def over_shards(x):
        if pair:
            return x[0], swap_y(x[1])
        return lax.psum_scatter(x[0].astype(f32), "shards", scatter_dimension=3, tiled=True), jnp.zeros((), f32)

    def added(x):
        a, b = x
        return (a if b is None else a.astype(f32) + b.astype(f32)).astype(bf16)

    dy, dg0, skip_g, d0, d1, d2, d3 = call(
        ungate_kernel,
        [((nb, ch, B), bf16), ((nb, ch, B), f32), ((ch, 1), f32)] + [piece] * 4,
        8,
        [pltpu.VMEM((WAYS,) + packs, bf16), pltpu.VMEM((nb, ch, B), f32)],
    )(sc, dgn[0], dgn[1], after(dgn[2], og), dgn[3], g0, ys, u, cols)
    f3 = after(f3, dy)
    mg_y, og_y = over_shards(after(mg, dm)), over_shards(og)
    dn_ = ctx((d0, d1, d2, d3))
    mg_y = after(mg_y, dn_[1], dn_[2], dn_[3])
    dtaps, e0, e1, e2, e3 = call(
        conv_back_kernel,
        [((cs, PATH), f32)] + [piece] * 4,
        8,
        [
            pltpu.VMEM((TREE_BLK, cs, B), bf16),
            pltpu.VMEM((TREE_BLK + 6, cs, 2 * B), f32),
            pltpu.VMEM((TREE_BLK, cs, 2 * B), f32),
            pltpu.VMEM((NPATH, cs, 2 * B), f32),
        ],
    )(sc, dn_[0], dn_[1], after(dn_[2], mg_y), dn_[3], ws, hs, fh, gh)
    en = ctx((e0, e1, e2, e3))
    mg_sum = added(mg_y)
    mg_got = [swap(mg_sum[k], "tensor", k) for k in (1, 2, 3)]
    dzo, rims, cg = call(
        unconv_kernel,
        [((nb, ch3, B), f32), ((16, ch3), f32), ((ch3, 128), f32)],
        10,
        [pltpu.VMEM((ch, B), bf16), pltpu.VMEM((ch3, 128), f32), pltpu.VMEM((4, ch3, 128), f32), pltpu.VMEM((128, ch3), f32), pltpu.VMEM((5, ch3, 2), f32)],
    )(sc, en[0], en[1], after(en[2], mg_got[0], mg_got[2]), en[3], dy, dg0, gv, z, zr, cols)
    wa, wb = after((wa, wb), rims)
    wc, wd = swap(wa, "context", 1), swap(wb, "context", 1)
    rn = ctx((rims, rims, rims, rims))
    og_y = after(og_y, rims)
    og_sum = added(og_y)
    og_got = tuple(swap(og_sum[k], "tensor", k) for k in (1, 2, 3))
    rn = (rn[0], rn[1], rn[2], after(rn[3], og_y))
    col = jnp.arange(WAYS * 16, dtype=jnp.int32)
    col_blk = (col // 16) * 5 + (col % 16) // 2
    col_ok = (col % 16) < 10
    col_par = jnp.where(col_ok, all_par[jnp.minimum(col_blk, TREE_BLK - 1)], -2)
    row = jnp.arange(128, dtype=jnp.int32)
    pick = (
        (row[:, None] < 10)
        & (col_par[None, :] == c_id * 5 + row[:, None] // 2)
        & (col[None, :] % 2 == row[:, None] % 2)
    ).astype(f32)
    dpacks = (5 * ch3 // 2, 128)
    dz, q0, q1, q2, q3, ib = call(
        dz_kernel,
        [((nb, ch3, B), bf16)] + [(dpacks, bf16)] * 4 + [((ch3, 1), f32)],
        6,
        [pltpu.VMEM((WAYS * 16, ch3), f32), pltpu.VMEM((ch3, 128), f32), pltpu.VMEM((WAYS,) + dpacks, bf16)],
    )(sc, dzo, *rn, pick)
    qn = ten((q0, q1, q2, q3))
    if pair:
        mine, theirs, sums1 = call(
            in_grad_kernel,
            [((ch3, d_part), f32), ((ch3, d_part), bf16), ((8, width), f32)],
            6,
        )(after(sc, mg_got[1], og_got[0]), dz, a1, wt, ib, norm1_gain, norm1_bias)
        ih = mine + swap_y(theirs).astype(f32)
    else:
        ig, sums1 = call(in_grad_kernel, [((ch3, width), f32), ((8, width), f32)], 6)(sc, dz, a1, wt, ib, norm1_gain, norm1_bias)
        ih = lax.psum_scatter(ig, "shards", scatter_dimension=1, tiled=True)

    fs = sum_context(f0, f1, f2, f3, dy)
    filt, fo_g = call(functools.partial(filter_back_kernel, bands), [((FILT_ROWS, fw), f32), ((cs, fw), f32)], 5, [pltpu.VMEM((ne, STEP), f32)])(
        after(sc, dz), dtaps, fin, fc, fo_t, filt_mid
    )
    n_col = 8 * (-(-ch3 // 128))
    n_all = 64 + FILT_ROWS + 16
    (small,) = call(pack_kernel, [((n_all + n_col + 8 + ch, 128), f32)], 8, [pltpu.VMEM((128, ch3), f32)])(
        sc, sums1, sums2, ub, filt, fo_g, cg, ib, skip_g
    )
    ctx_small = tuple(swap(small, "context", k) for k in (1, 2, 3))

    def total(own, got):
        return ((own.astype(f32) + got[0].astype(f32)) + (got[1].astype(f32) + got[2].astype(f32))).astype(bf16)

    m0 = total(mg_sum[0], after(tuple(mg_got), qn[2]))
    m1, m2 = swap(m0, "context", 1), swap(m0, "context", 2)
    ih_core = swap(ih.astype(bf16), "context", 1)

    ih = ih + ih_core.astype(f32)
    far = swap(ih.astype(bf16), "context", 2)
    small = (small + ctx_small[0]) + (ctx_small[1] + ctx_small[2])
    small_y = swap_y(small) if pair else lax.psum(small, "shards")
    oh = total(og_sum[0], after(og_got, qn[2]))[0].astype(f32)
    oh = oh + swap(oh.astype(bf16), "context", 1).astype(f32)
    oh_far = swap(oh.astype(bf16), "context", 2)
    part, w2 = call(
        norm1_part_kernel, [(sh, f32), ((ch3, width), bf16)], 8, [pltpu.VMEM((2, ch3, width), bf16)]
    )(sc, qn[0], qn[1], qn[3], wt, wa, wb, wc, wd)
    (tokens_grad,) = call(norm1_kernel, [(sh, bf16)], 6, [pltpu.VMEM(sh, f32)])(
        sc, part, qn[2], w2, tok_share, dr1, norm1_gain
    )

    done = tokens_grad
    fs, m1, m2, far, oh_far, small_y = after((fs, m1, m2, far, oh_far, small_y), done)
    small = small + small_y if pair else small_y
    late = small[n_all:]
    early = small[:n_all]
    early = (early + swap(early, "tensor", 1)) + (swap(early, "tensor", 2) + swap(early, "tensor", 3))
    out_grad = oh + oh_far.astype(f32)
    m3 = swap(m2, "context", 1)
    up_grad, down_grad = call(
        matrices_kernel, [((d_part, ffq), f32), ((ffq, d_part), f32)], 4, [pltpu.VMEM((ffq, d_part), f32)]
    )(sc, m0, m1, m2, m3)
    in_grad = jnp.transpose((ih + far.astype(f32)).reshape(3, ch, d_part), (2, 0, 1))
    (layer_out,) = call(layer_out_kernel, [(sh, bf16)], 5)(sc, r1, *fs, down_bias)

    first = early[64 + FILT_ROWS :]

    def row_at(x, at):
        return x[at : at + 8].reshape(-1)[:width]

    hid = early[32:64].reshape(WAYS, WAYS, 256)[:, :, :ffs]
    up_bias_grad = lax.dynamic_index_in_dim(hid, t_id, 1, keepdims=False).reshape(ffq)
    fil = early[64 : 64 + FILT_ROWS, :fw]
    fo_own = lax.dynamic_slice_in_dim(late[8 + n_col :, :fw].T, s_id * filt_out.shape[0], filt_out.shape[0], 0)
    colsum = late[:n_col].reshape(n_col // 8, 8, 128).transpose(1, 0, 2).reshape(8, -1)[:, :ch3]
    skip_sum = late[n_col : 8 + n_col].reshape(-1)[:ch]
    conv_all = colsum.reshape(8, 3, ch)
    return (
        layer_out,
        tokens_grad,
        row_at(first, 0),
        row_at(first, 8),
        in_grad,
        conv_all[4],
        conv_all[1:4],
        conv_all[0],
        jnp.concatenate([fil[fw + n_in - 1 : fw + n_in], fil[fw : fw + n_in - 1]]),
        fil[fw + ne],
        fil[:fw],
        fil[fw + ne + 1],
        fil[fw + ne + 2],
        fo_own,
        skip_sum,
        out_grad,
        row_at(early, 16),
        row_at(early, 0),
        row_at(early, 8),
        up_grad,
        up_bias_grad,
        down_grad,
        row_at(early, 24),
    )


def solution(mesh):
    return jax.shard_map(
        functools.partial(body, mesh.shape["shards"]),
        mesh=mesh,
        in_specs=(
            P(("shards", "context"), None),
            P("shards", None),
            P(),
            P(),
            P("shards", None, "tensor"),
            P(None, "tensor"),
            P(None, None, "tensor"),
            P(None, "tensor"),
            P(),
            P(),
            P(),
            P(),
            P(),
            P("shards", "tensor"),
            P("tensor"),
            P("tensor", "shards"),
            P(),
            P(),
            P(),
            P("shards", "tensor"),
            P("tensor"),
            P("tensor", "shards"),
            P(),
            P(("shards", "context"), None),
        ),
        out_specs=(
            P(("shards", "context", "tensor"), None),
            P(("shards", "context", "tensor"), None),
            P(),
            P(),
            P("shards", None, "tensor"),
            P(None, "tensor"),
            P(None, None, "tensor"),
            P(None, "tensor"),
            P(),
            P(),
            P(),
            P(),
            P(),
            P("shards", "tensor"),
            P("tensor"),
            P("tensor", "shards"),
            P(),
            P(),
            P(),
            P("shards", "tensor"),
            P("tensor"),
            P("tensor", "shards"),
            P(),
        ),
        check_vma=False,
    )
```

```python
import functools
import math

import jax
import jax.numpy as jnp
import ml_dtypes
import numpy as np
from jax import lax
from jax.experimental import pallas as pl
from jax.experimental.pallas import tpu as pltpu
from jax.sharding import PartitionSpec as P

BLOCK = 256
TRUNK = 8
NPATH = 10
PATH = 2560
BRANCHES = 4
LEAVES = 8
TREE_BLK = 20
WAYS = 4

f32 = jnp.float32
bf16 = jnp.bfloat16
exact_mode = lax.Precision.HIGHEST
GELU_A = math.sqrt(2.0 / math.pi)
GELU_B = 0.044715


def dft_tables():
    k = np.arange(BLOCK)[None, :]
    n = np.arange(BLOCK)[:, None]
    ang = np.pi * ((2 * k + 1) * n % 1024) / 512.0
    fwd = np.concatenate([np.cos(ang), -np.sin(ang)], axis=1)
    m = BLOCK + np.arange(BLOCK)[None, :]
    kk = np.arange(BLOCK)[:, None]
    ang2 = np.pi * ((2 * kk + 1) * m % 1024) / 512.0
    inv = np.concatenate([np.cos(ang2), -np.sin(ang2)], axis=0) / 256.0
    return fwd.astype(ml_dtypes.bfloat16), inv.astype(ml_dtypes.bfloat16)


def swap(x, axis, k):
    return lax.ppermute(x, axis, [(i, i ^ k) for i in range(WAYS)])


def smem_spec():
    return pl.BlockSpec(memory_space=pltpu.SMEM)


def call(kernel, outs, n_in, scratch=(), limit=24):
    def run(sc, *args):
        assert len(args) == n_in
        vm = pl.BlockSpec(memory_space=pltpu.VMEM)
        return pl.pallas_call(
            kernel,
            out_shape=[jax.ShapeDtypeStruct(s, d) for s, d in outs],
            in_specs=[smem_spec()] + [vm] * n_in,
            out_specs=[vm] * len(outs),
            scratch_shapes=list(scratch),
            compiler_params=pltpu.CompilerParams(vmem_limit_bytes=limit << 20),
        )(sc, *args)

    return run


def after(x, *deps):
    return lax.optimization_barrier((x, deps))[0]


def nt(a, b):
    return lax.dot_general(a, b, (((1,), (1,)), ((), ())), preferred_element_type=f32)


def nn(a, b):
    return lax.dot_general(a, b, (((1,), (0,)), ((), ())), preferred_element_type=f32)


def tn(a, b):
    return lax.dot_general(a, b, (((0,), (0,)), ((), ())), preferred_element_type=f32)


def two(a):
    hi = a.astype(bf16)
    return hi, (a - hi.astype(f32)).astype(bf16)


def row(ref):
    return ref[...].reshape(1, ref.shape[0])


def norm_parts(x):
    mu = jnp.mean(x, axis=-1, keepdims=True)
    xc = x - mu
    rs = lax.rsqrt(jnp.mean(xc * xc, axis=-1, keepdims=True) + 1e-05)
    return xc * rs, rs


def norm_back(nh, rs, dnh):
    m1 = jnp.mean(dnh, axis=-1, keepdims=True)
    m2 = jnp.mean(dnh * nh, axis=-1, keepdims=True)
    return rs * (dnh - m1 - nh * m2)


def share_tiles(t):
    return [((0, 1), 2), ((3, 4), 2), ((5, 6), 7), ((8, 9), 7)][t]


def pack_share(tiles, t, ch, store):
    (a, b), c = share_tiles(t)
    store(0, tiles(a))
    store(ch, tiles(b))
    x = tiles(c)
    low = lax.broadcasted_iota(jnp.int32, (ch // 2, 128), 1) < 64
    top, bot = x[: ch // 2], x[ch // 2 :]
    if t % 2 == 0:
        y = jnp.where(low, top, pltpu.roll(bot, 64, 1))
    else:
        y = jnp.where(low, pltpu.roll(top, 64, 1), bot)
    store(2 * ch, y)


def left_rows(piece, ch):
    x = piece[2 * ch :].astype(f32)
    return jnp.concatenate([x, pltpu.roll(x, 64, 1)], axis=0)


def share_offsets(t):
    odd = t % 2
    return (64 * odd, 64 * odd + 128, 256 * (1 - odd))


def norm1_fwd_kernel(sc, tok, cw, cb, ib, sk, g, b, a1o, colo, rt):
    gain, shift = row(g), row(b)
    ch = sk.shape[0]
    rt[...] = jnp.zeros_like(rt)
    for p in range(3):
        at = slice(p * ch, (p + 1) * ch)
        for k in range(3):
            rt[k : k + 1, at] = cw[k, p : p + 1, :]
        rt[3:4, at] = cb[p : p + 1, :]
        rt[4:5, at] = ib[p : p + 1, :]
        rt[5:6, at] = row(sk)
    colo[...] = rt[...].T

    @pl.loop(0, 5)
    def _(i):
        rows = pl.ds(pl.multiple_of(i * BLOCK, BLOCK), BLOCK)
        nh, _ = norm_parts(tok[rows, :].astype(f32))
        a1o[rows, :] = (nh * gain + shift).astype(bf16)


def proj_kernel(sc, a1, m0, m1, m2, m3, wt, cols, g, bb, zo, zro, go, gvo, uo, u0, u1, u2, u3, rim, zs):
    c = sc[1]
    gain, shift = row(g), row(bb)
    cv = cols[...]
    w0, w1, w2, cb, ib = (cv[:, i : i + 1] for i in range(5))
    ch = go.shape[1]
    cs = ch // WAYS
    lane = lax.broadcasted_iota(jnp.int32, (3 * ch, 128), 1)
    for k, r in enumerate((m0, m1, m2, m3)):
        rim[pl.ds((c ^ k) * 5, 5)] = r[...]
    rows = [rim[jnp.maximum(sc[3 + b], 0)] for b in range(5)]
    nhr, _ = norm_parts(jnp.concatenate(rows, axis=0).astype(f32))
    a1r = (nhr * gain + shift).astype(bf16)
    a1r = jnp.concatenate([a1r, jnp.zeros((6, a1r.shape[1]), bf16)], axis=0)
    zr = (nt(wt[...], a1r) + ib).astype(bf16).astype(f32)
    lane16 = lax.broadcasted_iota(jnp.int32, zr.shape, 1)
    keep = jnp.zeros(zr.shape, f32)
    for b in range(5):
        keep = jnp.where(lane16 // 2 == b, jnp.where(sc[3 + b] >= 0, 1.0, 0.0), keep)
    zr = zr * keep
    zro[...] = jnp.concatenate([zr, jnp.zeros((zr.shape[0], 112), f32)], axis=1).T[:16]
    for b in range(5):
        zs[b] = zr[:, 2 * b : 2 * b + 2]

    for b in range(5):
        zb = (nt(wt[...], a1[b * BLOCK : (b + 1) * BLOCK, :]) + ib).astype(bf16)
        zo[b] = zb
        z = zb.astype(f32)
        far, near = zs[b, :, 0:1], zs[b, :, 1:2]
        r1, r2 = pltpu.roll(z, 1, 1), pltpu.roll(z, 2, 1)
        z1 = jnp.concatenate([jnp.where(lane == 0, near, r1[:, :128]), r1[:, 128:]], axis=1)
        z2 = jnp.concatenate(
            [jnp.where(lane == 0, far, jnp.where(lane == 1, near, r2[:, :128])), r2[:, 128:]], axis=1
        )
        sv = cb + w0 * z + w1 * z1 + w2 * z2
        go[b] = sv[:ch]
        gvo[b] = sv[ch:]
        uo[b] = (sv[2 * ch :] * sv[ch : 2 * ch]).astype(bf16)
        for k, o in enumerate((u0, u1, u2, u3)):
            o[b] = uo[b, pl.ds(pl.multiple_of((c ^ k) * cs, 16), cs), :]


def sincos(x):
    n = jnp.floor(x * (2.0 / math.pi) + 0.5)
    r = ((x - n * 1.5703125) - n * 4.837512969970703125e-4) - n * 7.54978995489188216e-8
    r2 = r * r
    sn = r + r * r2 * (-1.6666654611e-1 + r2 * (8.3321608736e-3 - r2 * 1.9515295891e-4))
    cn = 1.0 - 0.5 * r2 + r2 * r2 * (4.166664568298827e-2 + r2 * (-1.388731625493765e-3 + r2 * 2.443315711809948e-5))
    q = n.astype(jnp.int32)
    odd = (q & 1) == 1
    s1, c1 = jnp.where(odd, cn, sn), jnp.where(odd, sn, cn)
    return jnp.where((q & 2) == 2, -s1, s1), jnp.where(((q + 1) & 2) == 2, -c1, c1)


def exact_nn(a, b):
    return lax.dot_general(a, b, (((1,), (0,)), ((), ())), precision=exact_mode, preferred_element_type=f32)


STEP = 5 * BLOCK


def exact_tn(a, b):
    return lax.dot_general(a, b, (((0,), (0,)), ((), ())), precision=exact_mode, preferred_element_type=f32)


def filter_chunk(d, emb, fin, fmid, fc, bands):
    frv, b1, b2, rate = (fc[:, i : i + 1] for i in range(4))
    pos = (lax.broadcasted_iota(jnp.int32, (1, STEP), 1) + d * STEP).astype(f32)
    k = lax.broadcasted_iota(jnp.int32, (bands, 1), 0).astype(f32)
    freq = 0.0001 + (bands - 1 - 0.0001) * k / max(bands - 1, 1)
    sn, cn = sincos(freq * (2.0 * math.pi * pos / PATH))
    emb[...] = jnp.zeros_like(emb)
    emb[0:bands] = cn
    emb[bands : 2 * bands] = -sn
    lag = pos / (PATH - 1)
    emb[2 * bands : 2 * bands + 1] = lag
    e = emb[...]
    p1 = exact_tn(fin[...], e) + b1
    s1, c1 = sincos(frv * p1)
    p2 = exact_tn(fmid[...], s1) + b2
    s2, c2 = sincos(frv * p2)
    return e, p1, s1, c1, p2, s2, c2, lag, rate


def hidden_kernel(bands, ch, sc, filt_in, fmid, b1, b2, freq, mid, fin, fc, emb, rt):
    n_in, fw = filt_in.shape
    fin[...] = jnp.zeros_like(fin)
    fin[0 : n_in - 1] = filt_in[1:n_in]
    fin[n_in - 1 : n_in] = filt_in[0:1]
    first = (sc[2] * ch + sc[1] * (ch // WAYS)).astype(f32)
    channel = lax.broadcasted_iota(jnp.int32, (1, fw), 1).astype(f32) + first
    slow, fast = math.log(0.01) / 1.5, math.log(0.01) / 0.3
    rt[...] = jnp.zeros_like(rt)
    rt[0:1], rt[1:2], rt[2:3] = row(freq), row(b1), row(b2)
    rt[3:4] = jnp.abs(slow + (fast - slow) * channel / (ch * WAYS - 1))
    fc[...] = rt[...].T

    @pl.loop(0, PATH // STEP)
    def _(d):
        sl = pl.ds(pl.multiple_of(d * STEP, STEP), STEP)
        mid[:, sl] = filter_chunk(d, emb, fin, fmid, fc, bands)[5]


def taps_kernel(sc, mid, fc, fo, taps):
    cs = fo.shape[0]
    lag = lax.broadcasted_iota(jnp.int32, (1, PATH), 1).astype(f32) / (PATH - 1)
    taps[...] = exact_nn(fo[...], mid[...]) * (jnp.exp(-lag * fc[:cs, 3:4]) + 0.05)


def leaf_parent(sc, i):
    return TRUNK - 1 + sc[8 + 1 + BRANCHES + i]


def signs():
    lane = lax.broadcasted_iota(jnp.int32, (1, BLOCK), 1)
    return (1 - 2 * (lane % 2)).astype(f32)


def mul(acc, h, w):
    hr, hi = h[:, :BLOCK], h[:, BLOCK:]
    wr, wi = w[:, :BLOCK], w[:, BLOCK:]
    return acc[0] + (hr * wr - hi * wi), acc[1] + (hr * wi + hi * wr)


def mul_conj(acc, h, w):
    hr, hi = h[:, :BLOCK], h[:, BLOCK:]
    wr, wi = w[:, :BLOCK], w[:, BLOCK:]
    return acc[0] + (hr * wr + hi * wi), acc[1] + (hr * wi - hi * wr)


def conv_kernel(sc, u0, u1, u2, u3, taps, fh, gh, wo, ho, y0, y1, y2, y3, un, sp):
    c = sc[1]
    cs = u0.shape[1]
    for k, r in enumerate((u0, u1, u2, u3)):
        un[pl.ds((c ^ k) * 5, 5)] = r[...]
    for d in range(NPATH):
        thi, tlo = two(taps[:, d * BLOCK : (d + 1) * BLOCK])
        ho[d] = nn(thi, fh[...]) + nn(tlo, fh[...])
    ua = un[...].reshape(TREE_BLK * cs, BLOCK)
    sp[...] = nn(ua, fh[...]).reshape(TREE_BLK, cs, 2 * BLOCK)
    sg = signs()

    def window(k, par):
        a = sp[k]
        wr = sg * a[:, BLOCK:]
        wi = -(sg * a[:, :BLOCK])
        if par is not None:
            q = sp[par]
            wr = wr + q[:, :BLOCK]
            wi = wi + q[:, BLOCK:]
        wo[k, :, :BLOCK] = wr
        wo[k, :, BLOCK:] = wi

    window(0, None)

    @pl.loop(1, TRUNK)
    def _(k):
        window(k, k - 1)

    @pl.loop(0, BRANCHES)
    def _(i):
        window(TRUNK + i, TRUNK - 1)

    @pl.loop(0, LEAVES)
    def _(i):
        window(TRUNK + BRANCHES + i, leaf_parent(sc, i))

    zero = jnp.zeros((cs, BLOCK), f32)

    def put(k, acc):
        sp[k, :, :BLOCK] = acc[0]
        sp[k, :, BLOCK:] = acc[1]

    @pl.loop(0, TRUNK)
    def _(q):
        acc = lax.fori_loop(0, q + 1, lambda d, a: mul(a, ho[d], wo[q - d]), (zero, zero))
        put(q, acc)

    common_b = lax.fori_loop(1, 9, lambda d, a: mul(a, ho[d], wo[8 - d]), (zero, zero))

    @pl.loop(TRUNK, TRUNK + BRANCHES)
    def _(k):
        put(k, mul(common_b, ho[0], wo[k]))

    common_l = lax.fori_loop(2, 10, lambda d, a: mul(a, ho[d], wo[9 - d]), (zero, zero))

    @pl.loop(0, LEAVES)
    def _(i):
        k = TRUNK + BRANCHES + i
        put(k, mul(mul(common_l, ho[0], wo[k]), ho[1], wo[leaf_parent(sc, i)]))

    yhi, ylo = two(sp[...].reshape(TREE_BLK * cs, 2 * BLOCK))
    y = nn(yhi, gh[...]) + nn(ylo, gh[...])
    un[...] = y.astype(bf16).reshape(TREE_BLK, cs, BLOCK)
    for k, o in enumerate((y0, y1, y2, y3)):
        o[...] = un[pl.ds((c ^ k) * 5, 5)]


def gate_kernel(sc, y0, y1, y2, y3, g0, u, cols, yo, p0, p1, p2, p3, ys, gs, pk):
    c, t = sc[1], sc[2]
    cs = y0.shape[1]
    for k, r in enumerate((y0, y1, y2, y3)):
        for b in range(5):
            ys[b, pl.ds(pl.multiple_of((c ^ k) * cs, 16), cs), :] = r[b]
    skip = cols[:, 5:6][: u.shape[1]]
    for b in range(5):
        y = ys[b]
        yo[b] = y
        gs[b] = g0[b] * (y.astype(f32) + skip * u[b].astype(f32))
    pack_all(t, u.shape[1], lambda j: gs[j // 2, :, (j % 2) * 128 : (j % 2) * 128 + 128], pk, (p0, p1, p2, p3))


def pack_all(t, ch, tiles, pk, outs):
    for s in range(WAYS):

        def store(row, v, s=s):
            pk[s, row : row + v.shape[0]] = v.astype(bf16)

        pack_share(tiles, s, ch, store)
    for k, o in enumerate(outs):
        if o is not None:
            o[...] = pk[t ^ k]


def unpack_all(t, ch, ins, pk, put):
    for k, r in enumerate(ins):
        pk[t ^ k] = r[...]
    for s in range(WAYS):
        (a, b), _ = share_tiles(s)
        put(a, pk[s, 0:ch].astype(f32))
        put(b, pk[s, ch : 2 * ch].astype(f32))
    low = lax.broadcasted_iota(jnp.int32, (ch // 2, 128), 1) < 64
    for j, (s0, s1) in ((2, (0, 1)), (7, (2, 3))):
        x0 = pk[s0, 2 * ch :].astype(f32)
        x1 = pk[s1, 2 * ch :].astype(f32)
        top = jnp.where(low, x0, pltpu.roll(x1, 64, 1))
        bot = jnp.where(low, pltpu.roll(x0, 64, 1), x1)
        put(j, jnp.concatenate([top, bot], axis=0))


def sides(sc, half):
    h = sc[0]
    return pl.ds(pl.multiple_of(h * half, 128), half), pl.ds(pl.multiple_of((1 - h) * half, 128), half)


def mix_kernel(sc, p0, p1, p2, p3, owm, owo, tok, ob, g2, b2, r1o, a2o, acc):
    t = sc[2]
    ch, half = p0.shape[0] * 2 // 5, owm.shape[2]
    mine, other = sides(sc, half)
    offs = share_offsets(t)
    parts = [None, None, None]
    for k, r in enumerate((p0, p1, p2, p3)):
        wm, wo = owm[k, :ch], owo[k, :ch]
        piece = r[...]
        xs = (piece[:ch].astype(f32), piece[ch : 2 * ch].astype(f32), left_rows(piece, ch))
        for i, x in enumerate(xs):
            xt = x.T.astype(bf16)
            v = (nn(xt, wm), nn(xt, wo))
            parts[i] = v if parts[i] is None else (parts[i][0] + v[0], parts[i][1] + v[1])
    for i, n in ((0, 128), (1, 128), (2, 64)):
        at = pl.ds(pl.multiple_of(offs[i], 64), n)
        acc[at, mine] = parts[i][0][:n]
        acc[at, other] = parts[i][1][:n]
    r1 = tok[...].astype(f32) + (acc[...] + row(ob))
    r1o[...] = r1
    nh, _ = norm_parts(r1)
    a2o[...] = (nh * row(g2) + row(b2)).astype(bf16)


def stacked(ref, at, n):
    return jnp.concatenate([ref[k, at : at + n] for k in range(WAYS)], axis=0)


def mlp_kernel(ch, sc, xa, xb, ca, cb, um, uo, dm, do, upb, dpo, aco, pa, pb):
    mine, other = sides(sc, um.shape[2])
    bias = upb[...]
    ffs = dm.shape[1]
    u_m, u_o = stacked(um, ch, ffs), stacked(uo, ch, ffs)
    d_m, d_o = stacked(dm, 0, ffs), stacked(do, 0, ffs)
    n = pa.shape[0]
    for i, (x, ct, po) in enumerate(((xa, ca, pa), (xb, cb, pb))):
        at = slice(i * n, (i + 1) * n)
        p = nt(x[:, mine], u_m) + nt(x[:, other], u_o) + bias
        d = nt(ct[:, mine], d_m) + nt(ct[:, other], d_o)
        p2 = p * p
        th = jnp.tanh(GELU_A * p * (1.0 + GELU_B * p2))
        half = 0.5 * (1.0 + th)
        aco[at] = (p * half).astype(bf16)
        slope = half + 0.5 * p * (1.0 - th * th) * (GELU_A * (1.0 + 3.0 * GELU_B * p2))
        dp = (d * slope).astype(bf16)
        dpo[at] = dp
        po[:, mine] = nn(dp, u_m).astype(bf16)
        po[:, other] = nn(dp, u_o).astype(bf16)


def ffn_part(sc, ac, dm, do, f0, f1):
    mine, other = sides(sc, dm.shape[2])
    n = dm.shape[1]
    d_m, d_o = stacked(dm, 0, n), stacked(do, 0, n)
    m = f0.shape[0]
    for i, out in enumerate((f0, f1)):
        a = ac[i * m : (i + 1) * m]
        out[:, mine] = nn(a, d_m).astype(bf16)
        out[:, other] = nn(a, d_o).astype(bf16)


def put_grad(sc, outs, v, mat):
    n = v.shape[0] // WAYS
    if len(outs) == 1:
        for q in range(WAYS):
            outs[0][q, mat] = v[q * n : (q + 1) * n].astype(bf16)
        return
    m = v.shape[1] // 2
    first = sc[0] == 0
    for q in range(WAYS):
        a, b = v[q * n : (q + 1) * n, :m], v[q * n : (q + 1) * n, m:]
        outs[0][q, mat] = jnp.where(first, a, b).astype(bf16)
        outs[1][q, mat] = jnp.where(first, b, a).astype(bf16)


def tn_pair(a, b0, b1):
    m = b0.shape[0]
    return tn(a[:m], b0[...]) + tn(a[m:], b1[...])


def mlp_grad_one_kernel(sc, x0, x1, dp, ac, c0, c1, dm, do, out, ub, f0, f1):
    out[0] = tn_pair(dp, x0, x1).astype(bf16)
    out[1] = tn_pair(ac, c0, c1).astype(bf16)
    ub[...] = jnp.sum(dp[...].astype(f32), axis=0, keepdims=True)
    ffn_part(sc, ac, dm, do, f0, f1)


def mlp_grad_two_kernel(sc, x0, x1, dp, ac, c0, c1, one, ubone, dm, do, *outs):
    *grads, ub, f0, f1 = outs
    put_grad(sc, grads, one[0].astype(f32) + tn_pair(dp, x0, x1), 0)
    put_grad(sc, grads, one[1].astype(f32) + tn_pair(ac, c0, c1), 1)
    ub[...] = ubone[...] + jnp.sum(dp[...].astype(f32), axis=0, keepdims=True)
    ffn_part(sc, ac, dm, do, f0, f1)


def norm2_kernel(sc, own, core, far, r1, cot, g2, owm, owo, dro, dmo, sums, p0, p1, p2, p3):
    t = sc[2]
    sums[...] = jnp.zeros_like(sums)
    dn2 = own[...].astype(f32) + core[...].astype(f32) + far[...].astype(f32)
    nh, rs = norm_parts(r1[...])
    ct = cot[...].astype(f32)
    sums[0:1] = jnp.sum(dn2 * nh, axis=0, keepdims=True)
    sums[1:2] = jnp.sum(dn2, axis=0, keepdims=True)
    dr = ct + norm_back(nh, rs, dn2 * row(g2))
    dro[...] = dr
    dm = dr.astype(bf16)
    dmo[...] = dm
    sums[2:3] = jnp.sum(dm.astype(f32), axis=0, keepdims=True)
    sums[3:4] = jnp.sum(ct, axis=0, keepdims=True)
    offs = share_offsets(t)
    ch, half = p0.shape[0] * 2 // 5, owm.shape[2]
    mine, other = sides(sc, half)
    low = lax.broadcasted_iota(jnp.int32, (ch // 2, 128), 1) < 64
    at = [pl.ds(pl.multiple_of(offs[i], 64), n) for i, n in ((0, 128), (1, 128), (2, 64))]
    dms = [(dmo[a, mine], dmo[a, other]) for a in at]
    dms[2] = tuple(jnp.concatenate([v, v], axis=0) for v in dms[2])
    for k, o in enumerate((p0, p1, p2, p3)):
        wm, wo = owm[k, :ch], owo[k, :ch]
        vs = [nt(wm, a) + nt(wo, b) for a, b in dms]
        o[0:ch] = vs[0].astype(bf16)
        o[ch : 2 * ch] = vs[1].astype(bf16)
        o[2 * ch :] = jnp.where(low, vs[2][: ch // 2], vs[2][ch // 2 :]).astype(bf16)


def out_grad_kernel(sc, p0, p1, p2, p3, dm, *outs):
    t = sc[2]
    offs = share_offsets(t)
    ch = p0.shape[0] * 2 // 5
    da = dm[pl.ds(pl.multiple_of(offs[0], 64), 128), :]
    db = dm[pl.ds(pl.multiple_of(offs[1], 64), 128), :]
    dc = dm[pl.ds(pl.multiple_of(offs[2], 64), 64), :]
    vs = []
    for r in (p0, p1, p2, p3):
        piece = r[...]
        left = left_rows(piece, ch)[:, :64].astype(bf16)
        vs.append(nn(piece[:ch], da) + nn(piece[ch : 2 * ch], db) + nn(left, dc))
    put_grad(sc, outs, jnp.concatenate(vs, axis=0), 0)


def ungate_kernel(sc, p0, p1, p2, p3, g0, ys, u, cols, dyo, dgo, so, d0, d1, d2, d3, pk, dg):
    c, t = sc[1], sc[2]
    ch = u.shape[1]
    cs = ch // WAYS

    def put(j, v):
        dg[j // 2, :, (j % 2) * 128 : (j % 2) * 128 + 128] = v

    unpack_all(t, ch, (p0, p1, p2, p3), pk, put)
    skip = cols[:, 5:6][:ch]
    tot = None
    for b in range(5):
        g = dg[b]
        uu = u[b].astype(f32)
        dgo[b] = g * (ys[b].astype(f32) + skip * uu)
        dy = g * g0[b]
        v = jnp.sum(dy * uu, axis=1, keepdims=True)
        tot = v if tot is None else tot + v
        dyo[b] = dy.astype(bf16)
    so[...] = tot
    for k, o in enumerate((d0, d1, d2, d3)):
        for b in range(5):
            o[b] = dyo[b, pl.ds(pl.multiple_of((c ^ k) * cs, 16), cs), :]


def conv_back_kernel(sc, d0, d1, d2, d3, ws, hs, fh, gh, dho, o0, o1, o2, o3, un, dy, dw, dh):
    c = sc[1]
    cs = d0.shape[1]
    for k, r in enumerate((d0, d1, d2, d3)):
        un[pl.ds((c ^ k) * 5, 5)] = r[...]
    da = un[...].reshape(TREE_BLK * cs, BLOCK)
    dy[0:TREE_BLK] = nt(da, gh[...]).reshape(TREE_BLK, cs, 2 * BLOCK)
    zero = jnp.zeros((cs, BLOCK), f32)
    zz = jnp.zeros((cs, 2 * BLOCK), f32)
    first_leaf = TRUNK + BRANCHES
    sum_b = lax.fori_loop(TRUNK, first_leaf, lambda k, a: a + dy[k], zz)
    sum_l = lax.fori_loop(first_leaf, TREE_BLK, lambda k, a: a + dy[k], zz)
    dy[TREE_BLK] = sum_b
    dy[TREE_BLK + 1] = sum_l
    for i in range(BRANCHES):
        dy[TREE_BLK + 2 + i] = zz

    @pl.loop(0, LEAVES)
    def _(i):
        k = TREE_BLK + 2 + leaf_parent(sc, i) - TRUNK
        dy[k] = dy[k] + dy[first_leaf + i]


    def put(ref, k, acc):
        ref[k, :, :BLOCK] = acc[0]
        ref[k, :, BLOCK:] = acc[1]

    @pl.loop(0, TRUNK)
    def _(j):
        acc = lax.fori_loop(j, TRUNK, lambda q, a: mul_conj(a, hs[q - j], dy[q]), (zero, zero))
        acc = mul_conj(acc, hs[8 - j], dy[TREE_BLK])
        put(dw, j, mul_conj(acc, hs[9 - j], dy[TREE_BLK + 1]))

    @pl.loop(0, BRANCHES)
    def _(i):
        k = TRUNK + i
        acc = mul_conj((zero, zero), hs[0], dy[k])
        put(dw, k, mul_conj(acc, hs[1], dy[TREE_BLK + 2 + i]))

    @pl.loop(first_leaf, TREE_BLK)
    def _(k):
        put(dw, k, mul_conj((zero, zero), hs[0], dy[k]))


    @pl.loop(0, TRUNK)
    def _(d):
        put(dh, d, lax.fori_loop(d, TRUNK, lambda q, a: mul_conj(a, ws[q - d], dy[q]), (zero, zero)))

    put(dh, 8, (zero, zero))
    put(dh, 9, (zero, zero))

    def more(d, k, q):
        acc = (dh[d, :, :BLOCK], dh[d, :, BLOCK:])
        put(dh, d, mul_conj(acc, ws[k], dy[q]))

    @pl.loop(1, 9)
    def _(d):
        more(d, 8 - d, TREE_BLK)

    @pl.loop(2, 10)
    def _(d):
        more(d, 9 - d, TREE_BLK + 1)

    @pl.loop(TRUNK, TREE_BLK)
    def _(k):
        more(0, k, k)

    @pl.loop(0, BRANCHES)
    def _(i):
        more(1, TRUNK + i, TREE_BLK + 2 + i)

    for d in range(NPATH):
        thi, tlo = two(dh[d])
        dho[:, d * BLOCK : (d + 1) * BLOCK] = nt(thi, fh[...]) + nt(tlo, fh[...])

    sg = signs()

    def own(k):
        w = dw[k]
        return jnp.concatenate([-(sg * w[:, BLOCK:]), sg * w[:, :BLOCK]], axis=1)

    @pl.loop(0, TRUNK - 1)
    def _(k):
        dy[k] = own(k) + dw[k + 1]

    dy[TRUNK - 1] = lax.fori_loop(TRUNK, first_leaf, lambda k, a: a + dw[k], own(TRUNK - 1))

    @pl.loop(TRUNK, TREE_BLK)
    def _(k):
        dy[k] = own(k)

    @pl.loop(0, LEAVES)
    def _(i):
        k = leaf_parent(sc, i)
        dy[k] = dy[k] + dw[first_leaf + i]

    shi, slo = two(dy[0:TREE_BLK].reshape(TREE_BLK * cs, 2 * BLOCK))
    du = nt(shi, fh[...]) + nt(slo, fh[...])
    un[...] = du.astype(bf16).reshape(TREE_BLK, cs, BLOCK)
    for k, o in enumerate((o0, o1, o2, o3)):
        o[...] = un[pl.ds((c ^ k) * 5, 5)]


def unconv_kernel(sc, u0, u1, u2, u3, dyv, dg0, gv, z, zr, cols, dzo, rims, cg, dus, rs, acc, zc, zs):
    c = sc[1]
    ch = dyv.shape[1]
    cs = ch // WAYS
    cv = cols[...]
    w0, w1, w2 = (cv[:, i : i + 1] for i in range(3))
    skip = cv[:ch, 5:6]
    lane = lax.broadcasted_iota(jnp.int32, (3 * ch, 128), 1)
    rs[...] = jnp.zeros_like(rs)
    acc[...] = jnp.zeros_like(acc)

    def fold(i, v):
        acc[i] = acc[i] + (v[:, :128] + v[:, 128:])

    zc[...] = jnp.zeros_like(zc)
    zc[0:16] = zr[...]
    zcol = zc[...].T
    for b in range(5):
        zs[b] = zcol[:, 2 * b : 2 * b + 2]

    @pl.loop(0, 5)
    def _(b):
        for k, r in enumerate((u0, u1, u2, u3)):
            dus[pl.ds(pl.multiple_of((c ^ k) * cs, 16), cs), :] = r[b]
        du = dus[...].astype(f32) + skip * dyv[b].astype(f32)
        sv = gv[b]
        ds = jnp.concatenate([dg0[b], du * sv[ch:], du * sv[:ch]], axis=0)
        zv = z[b].astype(f32)
        far, near = zs[b, :, 0:1], zs[b, :, 1:2]
        r1, r2 = pltpu.roll(ds, BLOCK - 1, 1), pltpu.roll(ds, BLOCK - 2, 1)
        n1 = jnp.concatenate([r1[:, :128], jnp.where(lane == 127, 0.0, r1[:, 128:])], axis=1)
        n2 = jnp.concatenate([r2[:, :128], jnp.where(lane >= 126, 0.0, r2[:, 128:])], axis=1)
        dzo[b] = w0 * ds + w1 * n1 + w2 * n2
        d0, d1 = ds[:, 0:1], ds[:, 1:2]
        fold(0, ds)
        fold(1, ds * zv)
        fold(2, n1 * zv)
        fold(3, n2 * zv)
        acc[2] = acc[2] + jnp.where(lane == 0, d0 * near, 0.0)
        acc[3] = acc[3] + jnp.where(lane == 0, d0 * far + d1 * near, 0.0)
        rs[...] = rs[...] + jnp.where(lane == 2 * b, w2 * d0, jnp.where(lane == 2 * b + 1, w1 * d0 + w2 * d1, 0.0))

    rims[...] = rs[...].T[:16]
    out = jnp.zeros(lane.shape, f32)
    for i in range(4):
        out = jnp.where(lane == i, jnp.sum(acc[i], axis=1, keepdims=True), out)
    cg[...] = out


def dz_kernel(sc, dzo, r0, r1, r2, r3, pick, dz, p0, p1, p2, p3, ib, rall, rt, pk):
    c, t = sc[1], sc[2]
    rows = dzo.shape[1]
    for k, r in enumerate((r0, r1, r2, r3)):
        rall[pl.ds(pl.multiple_of((c ^ k) * 16, 16), 16), :] = r[...]
    got = lax.dot_general(
        pick[...], rall[...], (((1,), (0,)), ((), ())), precision=exact_mode, preferred_element_type=f32
    )
    rt[...] = got.T
    lane = lax.broadcasted_iota(jnp.int32, (rows, 128), 1)
    tot = None
    for b in range(5):
        add = jnp.where(lane >= 126, pltpu.roll(rt[...], 126 - 2 * b, 1), 0.0)
        lo = dzo[b, :, :128].astype(bf16)
        hi = (dzo[b, :, 128:] + add).astype(bf16)
        dz[b, :, :128] = lo
        dz[b, :, 128:] = hi
        v = jnp.sum(lo.astype(f32) + hi.astype(f32), axis=1, keepdims=True)
        tot = v if tot is None else tot + v
    ib[...] = tot
    pack_all(t, rows, lambda j: dz[j // 2, :, (j % 2) * 128 : (j % 2) * 128 + 128].astype(f32), pk, (p0, p1, p2, p3))


def in_grad_kernel(sc, dz, a1, wt, ib, g, b1, *outs):
    acc = None
    for b in range(5):
        v = nn(dz[b], a1[b * BLOCK : (b + 1) * BLOCK, :])
        acc = v if acc is None else acc + v
    sums = outs[-1]
    if len(outs) == 2:
        outs[0][...] = acc
    else:
        n = acc.shape[1] // 2
        first = sc[0] == 0
        outs[0][...] = jnp.where(first, acc[:, :n], acc[:, n:])
        outs[1][...] = jnp.where(first, acc[:, n:], acc[:, :n]).astype(bf16)
    w = wt[...].astype(f32)
    gsum = jnp.sum(w * acc, axis=0, keepdims=True)
    bsum = jnp.sum(w * ib[...], axis=0, keepdims=True)
    sums[...] = jnp.zeros_like(sums)
    sums[0:1] = (gsum - row(b1) * bsum) / row(g)
    sums[1:2] = bsum


FILT_ROWS = 112


def put_row(out, at, row):
    n = row.shape[1]
    k = -(-n // 128)
    for j in range(k):
        w = min(128, n - 128 * j)
        out[pl.ds(at + j, 1), :w] = row[:, 128 * j : 128 * j + w]
    return k


def pack_kernel(sc, sums1, sums2, ub, filt, fo, cg, ib, skip, out, colt):
    c, t = sc[1], sc[2]
    out[...] = jnp.zeros_like(out)
    for i in range(4):
        put_row(out, 8 * i, sums2[i : i + 1])
    n = ub.shape[1] // WAYS
    for q in range(WAYS):
        put_row(out, 32 + 2 * (WAYS * c + (t ^ q)), ub[0:1, q * n : (q + 1) * n])
    out[64 : 64 + FILT_ROWS, : filt.shape[1]] = filt[...]
    at = 64 + FILT_ROWS
    put_row(out, at, sums1[0:1])
    put_row(out, at + 8, sums1[1:2])
    at += 16
    lane = lax.broadcasted_iota(jnp.int32, cg.shape, 1)
    colt[...] = jnp.where(lane == 4, ib[...], cg[...]).T
    m = cg.shape[0]
    for j in range(-(-m // 128)):
        w = min(128, m - 128 * j)
        out[at : at + 8, :w] = colt[0:8, 128 * j : 128 * j + w]
        at += 8
    ch = skip.shape[0]
    put_row(out, at, jnp.broadcast_to(skip[...], (ch, 128)).T[0:1])
    at += 8
    cs = fo.shape[0]
    out[pl.ds(at + c * cs, cs), : fo.shape[1]] = fo[...]


def filter_back_kernel(bands, sc, dt, fin, fc, fo, fm, out, fog, emb):
    def three(dot, a, b):
        (ah, al), (bh, bl) = two(a), two(b)
        return dot(ah, bh) + dot(ah, bl) + dot(al, bh)

    n, ne, cs = fm.shape[0], emb.shape[0], fo.shape[0]
    fov, fmv, frv = fo[...], fm[...], fc[:, 0:1]

    def step(d, acc):
        a_fo, a_fm, a_fi, a_b1, a_b2, a_fr = acc
        e, q1, one, c1, q2, mid, c2, lag, rate = filter_chunk(d, emb, fin, fm, fc, bands)
        sl = pl.ds(pl.multiple_of(d * STEP, STEP), STEP)
        draw = dt[:, sl] * (jnp.exp(-lag * rate[:cs]) + 0.05)
        a_fo = a_fo + three(nt, draw, mid)
        da2 = three(tn, fov, draw) * c2
        dp2 = da2 * frv
        a_fm = a_fm + three(nt, one, dp2)
        da1 = three(nn, fmv, dp2) * c1
        dp1 = da1 * frv
        a_fi = a_fi + three(nt, e, dp1)
        sums = [jnp.sum(v, axis=1, keepdims=True) for v in (dp1, dp2, da2 * q2 + da1 * q1)]
        return a_fo, a_fm, a_fi, a_b1 + sums[0], a_b2 + sums[1], a_fr + sums[2]

    zero = jnp.zeros((n, 1), f32)
    init = (jnp.zeros(fog.shape, f32), jnp.zeros((n, n), f32), jnp.zeros((ne, n), f32), zero, zero, zero)
    a_fo, a_fm, a_fi, *cols = lax.fori_loop(0, PATH // STEP, step, init)
    fog[...] = a_fo
    out[...] = jnp.zeros_like(out)
    out[0:n] = a_fm
    out[n : n + ne] = a_fi
    lane = lax.broadcasted_iota(jnp.int32, (n, 128), 1)
    m = jnp.where(lane == 0, cols[0], jnp.where(lane == 1, cols[1], jnp.where(lane == 2, cols[2], 0.0)))
    out[n + ne : n + ne + 8] = m.T[0:8]


def piece_product(r, w, parts):
    rows = w.shape[0]
    piece = r[...]
    xs = (piece[:rows].astype(f32), piece[rows : 2 * rows].astype(f32), left_rows(piece, rows))
    for i, x in enumerate(xs):
        v = nn(x.T.astype(bf16), w)
        parts[i] = v if parts[i] is None else parts[i] + v


def put_parts(sc, parts, acc, old=None):
    offs = share_offsets(sc[2])
    for i, n in ((0, 128), (1, 128), (2, 64)):
        at = pl.ds(pl.multiple_of(offs[i], 64), n)
        acc[at, :] = parts[i][:n] if old is None else parts[i][:n] + old[at, :]


def norm1_part_kernel(sc, p0, p1, p3, w0, wa, wb, wc, wd, acc, w2, wr):
    n = wa.shape[1]
    mine, other = sides(sc, wa.shape[2])
    h = sc[1] & 1
    near, far = pl.ds(pl.multiple_of(h * n, 16), n), pl.ds(pl.multiple_of((1 - h) * n, 16), n)
    for i, w in ((0, wr.at[0]), (1, w2), (2, wr.at[1])):
        w[near, mine], w[near, other] = wa[i], wb[i]
        w[far, mine], w[far, other] = wc[i], wd[i]
    parts = [None, None, None]
    for r, w in ((p0, w0), (p1, wr.at[0]), (p3, wr.at[1])):
        piece_product(r, w[...], parts)
    put_parts(sc, parts, acc)


def norm1_kernel(sc, part, p2, w2, tok, dr, g, out, acc):
    parts = [None, None, None]
    piece_product(p2, w2[...], parts)
    put_parts(sc, parts, acc, part)
    nh, rs = norm_parts(tok[...].astype(f32))
    out[...] = (dr[...] + norm_back(nh, rs, acc[...] * row(g))).astype(bf16)


def matrices_kernel(sc, m0, m1, m2, m3, upo, downo, rows):
    c = sc[1]
    n = m0.shape[1]
    for k, m in enumerate((m0, m1, m2, m3)):
        at = pl.ds(pl.multiple_of((c ^ k) * n, 64), n)
        rows[at, :] = m[0].astype(f32)
        downo[at, :] = m[1].astype(f32)
    upo[...] = rows[...].T


def layer_out_kernel(sc, r1, own, core, far, db, out):
    ffn = own[...].astype(f32) + core[...].astype(f32) + far[...].astype(f32)
    out[...] = (r1[...] + ffn + row(db)).astype(bf16)


def body(
    shard_count,
    tokens,
    parents,
    norm1_gain,
    norm1_bias,
    in_weight,
    in_bias,
    conv_weight,
    conv_bias,
    filt_in,
    filt_bias1,
    filt_mid,
    filt_bias2,
    sine_freq,
    filt_out,
    skip_gain,
    out_weight,
    out_bias,
    norm2_gain,
    norm2_bias,
    up_weight,
    up_bias,
    down_weight,
    down_bias,
    cotangent,
):
    rows, width = tokens.shape
    ch = skip_gain.shape[0]
    cs = ch // WAYS
    ch3 = 3 * ch
    ffq = up_bias.shape[0]
    ffs = ffq // WAYS
    share = rows // WAYS
    d_part = in_weight.shape[0]
    s_id = lax.axis_index("shards")
    c_id = lax.axis_index("context")
    t_id = lax.axis_index("tensor")
    pair = shard_count == 2

    def gather_shards(x, axis, *deps):
        if not pair:
            return lax.all_gather(x, "shards", axis=axis, tiled=True)
        o = lax.ppermute(x, "shards", [(0, 1), (1, 0)])
        o = after(o, *deps) if deps else o
        lo = jnp.where(s_id == 0, x, o)
        hi = jnp.where(s_id == 0, o, x)
        return jnp.concatenate([lo, hi], axis=axis)

    par = parents[0]
    all_par = jnp.concatenate(
        [jnp.arange(-1, TRUNK - 1, dtype=jnp.int32), jnp.full((BRANCHES,), TRUNK - 1, jnp.int32), TRUNK - 1 + par[1 + BRANCHES :]]
    )
    own_par = lax.dynamic_slice_in_dim(all_par, c_id * 5, 5, 0)
    side = s_id if pair else jnp.zeros_like(s_id)
    sc = jnp.concatenate([jnp.stack([side, c_id, t_id]).astype(jnp.int32), own_par, par]).astype(jnp.int32)

    def swap_y(x):
        return lax.ppermute(x, "shards", [(0, 1), (1, 0)])

    n_in, fw = filt_in.shape
    bands = (n_in - 1) // 2
    ne = -(-n_in // 8) * 8
    hidden, fin, fc = call(
        functools.partial(hidden_kernel, bands, ch),
        [((fw, PATH), f32), ((ne, fw), f32), ((fw, 128), f32)],
        5,
        [pltpu.VMEM((ne, STEP), f32), pltpu.VMEM((128, fw), f32)],
    )(sc, filt_in, filt_mid, filt_bias1, filt_bias2, sine_freq)

    wt_part = jnp.transpose(in_weight, (1, 2, 0)).reshape(ch3, d_part)
    wt = gather_shards(wt_part, 1, hidden)
    rim_tok = tokens.reshape(5, BLOCK, width)[:, BLOCK - 2 :, :]
    rims_in = [rim_tok] + [swap(rim_tok, "context", k) for k in (1, 2, 3)]
    up_t = lax.dynamic_slice_in_dim(up_weight, c_id * ffs, ffs, 1).T
    down_c = lax.dynamic_slice_in_dim(down_weight, c_id * ffs, ffs, 0)
    bias_c = lax.dynamic_slice_in_dim(up_bias, c_id * ffs, ffs, 0)
    b_hi, b_mid = two(bias_c)
    b_lo = (bias_c - b_hi.astype(f32) - b_mid.astype(f32)).astype(bf16)
    wide = d_part >= ffs
    if wide:
        b_rows = jnp.stack([b_hi, b_mid, b_lo] + [jnp.zeros_like(b_hi)] * 13)
        b_rows = jnp.concatenate([b_rows, jnp.zeros((16, d_part - ffs), bf16)], axis=1)
        two_mats = jnp.concatenate([out_weight, up_t, b_rows])
    else:
        two_mats = jnp.concatenate([out_weight, up_t])
    def columns(parts):
        m = jnp.stack(parts)
        if pair:
            return m, swap_y(m)
        m = lax.all_gather(m, "shards", axis=2, tiled=True)
        return m[:, :, : width // 2], m[:, :, width // 2 :]

    parts_b = [down_c] + [swap(down_c, "tensor", k) for k in (1, 2, 3)]
    down = columns(after(tuple(parts_b), hidden))
    parts_a = [two_mats] + [swap(two_mats, "tensor", k) for k in (1, 2, 3)]
    if pair:
        fo_other = swap_y(filt_out)
        fo = jnp.concatenate([jnp.where(s_id == 0, filt_out, fo_other), jnp.where(s_id == 0, fo_other, filt_out)], axis=0)
    else:
        fo = fo_other = lax.all_gather(filt_out, "shards", axis=0, tiled=True)
    fo_t = lax.dynamic_slice_in_dim(fo, c_id * cs, cs, 1).astype(f32).T

    fh, gh = (jnp.asarray(a) for a in dft_tables())

    nb, B = 5, BLOCK
    piece = ((nb, cs, B), bf16)
    a1, cols = call(norm1_fwd_kernel, [((rows, width), bf16), ((ch3, 128), f32)], 7, [pltpu.VMEM((128, ch3), f32)])(
        after(sc, wt, down[0], fo_other), tokens, conv_weight, conv_bias, in_bias, skip_gain, norm1_gain, norm1_bias
    )
    z, zr, g0, gv, u, u0, u1, u2, u3 = call(
        proj_kernel,
        [((nb, ch3, B), bf16), ((16, ch3), f32), ((nb, ch, B), f32), ((nb, 2 * ch, B), f32), ((nb, ch, B), bf16)]
        + [piece] * 4,
        9,
        [pltpu.VMEM((TREE_BLK, 2, width), bf16), pltpu.VMEM((nb, ch3, 2), f32)],
    )(sc, a1, *rims_in, wt, cols, norm1_gain, norm1_bias)

    def ctx(p):
        return (p[0], swap(p[1], "context", 1), swap(p[2], "context", 2), swap(p[3], "context", 3))

    def ten(p):
        return (p[0], swap(p[1], "tensor", 1), swap(p[2], "tensor", 2), swap(p[3], "tensor", 3))

    un = ctx((u0, u1, u2, u3))
    (taps,) = call(taps_kernel, [((cs, PATH), f32)], 3)(after(sc, u0), hidden, fc, fo_t)
    mats = columns(after(tuple(parts_a), un))
    if wide:
        up_b = jnp.concatenate([p[ch + ffs : ch + ffs + 3, :ffs].astype(f32).sum(0) for p in parts_a]).reshape(1, ffq)
    else:
        up_b = jnp.concatenate([bias_c] + [swap(bias_c, "tensor", k) for k in (1, 2, 3)]).reshape(1, ffq)
    up_b = after(up_b, u0)
    spec = ((TREE_BLK, cs, 2 * B), f32)
    ws, hs, y0, y1, y2, y3 = call(
        conv_kernel,
        [spec, ((NPATH, cs, 2 * B), f32)] + [piece] * 4,
        7,
        [pltpu.VMEM((TREE_BLK, cs, B), bf16), pltpu.VMEM((TREE_BLK, cs, 2 * B), f32)],
    )(sc, *un, taps, fh, gh)
    yn = ctx((y0, y1, y2, y3))
    tok_share = lax.dynamic_slice_in_dim(tokens, t_id * share, share, 0)
    cot_share = lax.dynamic_slice_in_dim(cotangent, t_id * share, share, 0)
    tok_share, cot_share = after((tok_share, cot_share), u0)

    packs = (5 * ch // 2, 128)
    packed_out = [(packs, bf16)] * 4
    ys, *gp = call(
        gate_kernel,
        [((nb, ch, B), bf16)] + packed_out,
        7,
        [pltpu.VMEM((nb, ch, B), bf16), pltpu.VMEM((nb, ch, B), f32), pltpu.VMEM((WAYS,) + packs, bf16)],
    )(sc, *yn, g0, after(u, mats[0]), cols)
    gn = ten(gp)
    cot_share = after(cot_share, ys)
    cot1 = swap(cot_share, "context", 1)
    cot2 = swap(cot_share, "context", 2)

    sh = (share, width)
    r1, a2 = call(mix_kernel, [(sh, f32), (sh, bf16)], 10, [pltpu.VMEM(sh, f32)])(
        sc, *gn, *mats, after(tok_share, up_b), out_bias, norm2_gain, norm2_bias
    )

    x1 = swap(a2, "context", 1)
    x2 = swap(a2, "context", 2)
    cot3 = swap(after(cot2, a2), "context", 1)
    odd = c_id & 1
    w_half = lax.dynamic_slice_in_dim(wt, odd * (ch3 // 2), ch3 // 2, 0)
    w_quarter = after(lax.dynamic_slice_in_dim(w_half, side * (width // 2), width // 2, 1), a2)
    w_got = [swap(w_quarter, "tensor", k) for k in (1, 2, 3)]
    mlp = call(functools.partial(mlp_kernel, ch), [((2 * share, ffq), bf16)] * 2 + [(sh, bf16)] * 2, 9)
    dpa, aca, n0, n1 = mlp(sc, a2, x1, cot_share, cot1, *mats, *down, up_b)
    one, ub_one, f0, f1 = call(mlp_grad_one_kernel, [((2, ffq, width), bf16), ((1, ffq), f32), (sh, bf16), (sh, bf16)], 8)(
        after(sc, n0), a2, x1, dpa, aca, cot_share, cot1, *down
    )
    x2 = after(x2, one, w_got[0], w_got[2])
    x3 = swap(x2, "context", 1)
    dpb, acb, n2, n3 = mlp(sc, x2, x3, cot2, cot3, *mats, *down, up_b)
    one, ub_one, f0, f1 = after((one, ub_one, f0, f1), n2)

    def sum_context(q0, q1, q2, q3, *deps):
        a = swap(q1, "context", 1)
        b = swap(q3, "context", 1)
        b = after(b, *deps) if deps else b
        mid = (q2.astype(f32) + b.astype(f32)).astype(bf16)
        return q0, a, swap(mid, "context", 2)

    dn = sum_context(n0, n1, n2, n3)
    n_grad = 2 if pair else 1
    gcol = width // n_grad
    *mg, ub, f2, f3 = call(
        mlp_grad_two_kernel, [((WAYS, 2, ffs, gcol), bf16)] * n_grad + [((1, ffq), f32), (sh, bf16), (sh, bf16)], 10
    )(after(sc, n2), x2, x3, dpb, acb, cot2, cot3, one, ub_one, *down)
    dn = dn[:2] + (after(dn[2], w_got[0], w_got[2], mg),)
    dr1, dm, sums2, *dgp = call(norm2_kernel, [(sh, f32), (sh, bf16), ((8, width), f32)] + packed_out, 8)(
        sc, *dn, r1, cot_share, norm2_gain, *mats
    )
    f1, w_got = after((f1, w_got), dm)
    wa = jnp.stack(w_got)
    if pair:
        wb = swap_y(wa)
    else:
        other = lax.dynamic_slice_in_dim(w_half, width // 2, width // 2, 1)
        wb = jnp.stack([swap(after(other, dm), "tensor", k) for k in (1, 2, 3)])
    dgn = ten(dgp)

    og = call(out_grad_kernel, [((WAYS, 1, ch, gcol), bf16)] * n_grad, 5)(sc, *gn, dm)

    def over_shards(x):
        if pair:
            return x[0], swap_y(x[1])
        return lax.psum_scatter(x[0].astype(f32), "shards", scatter_dimension=3, tiled=True), jnp.zeros((), f32)

    def added(x):
        a, b = x
        return (a if b is None else a.astype(f32) + b.astype(f32)).astype(bf16)

    dy, dg0, skip_g, d0, d1, d2, d3 = call(
        ungate_kernel,
        [((nb, ch, B), bf16), ((nb, ch, B), f32), ((ch, 1), f32)] + [piece] * 4,
        8,
        [pltpu.VMEM((WAYS,) + packs, bf16), pltpu.VMEM((nb, ch, B), f32)],
    )(sc, dgn[0], dgn[1], after(dgn[2], og), dgn[3], g0, ys, u, cols)
    f3 = after(f3, dy)
    mg_y, og_y = over_shards(after(mg, dm)), over_shards(og)
    dn_ = ctx((d0, d1, d2, d3))
    mg_y = after(mg_y, dn_[1], dn_[2], dn_[3])
    dtaps, e0, e1, e2, e3 = call(
        conv_back_kernel,
        [((cs, PATH), f32)] + [piece] * 4,
        8,
        [
            pltpu.VMEM((TREE_BLK, cs, B), bf16),
            pltpu.VMEM((TREE_BLK + 6, cs, 2 * B), f32),
            pltpu.VMEM((TREE_BLK, cs, 2 * B), f32),
            pltpu.VMEM((NPATH, cs, 2 * B), f32),
        ],
    )(sc, dn_[0], dn_[1], after(dn_[2], mg_y), dn_[3], ws, hs, fh, gh)
    en = ctx((e0, e1, e2, e3))
    mg_sum = added(mg_y)
    mg_got = [swap(mg_sum[k], "tensor", k) for k in (1, 2, 3)]
    dzo, rims, cg = call(
        unconv_kernel,
        [((nb, ch3, B), f32), ((16, ch3), f32), ((ch3, 128), f32)],
        10,
        [pltpu.VMEM((ch, B), bf16), pltpu.VMEM((ch3, 128), f32), pltpu.VMEM((4, ch3, 128), f32), pltpu.VMEM((128, ch3), f32), pltpu.VMEM((5, ch3, 2), f32)],
    )(sc, en[0], en[1], after(en[2], mg_got[0], mg_got[2]), en[3], dy, dg0, gv, z, zr, cols)
    wa, wb = after((wa, wb), rims)
    wc, wd = swap(wa, "context", 1), swap(wb, "context", 1)
    rn = ctx((rims, rims, rims, rims))
    og_y = after(og_y, rims)
    og_sum = added(og_y)
    og_got = tuple(swap(og_sum[k], "tensor", k) for k in (1, 2, 3))
    rn = (rn[0], rn[1], rn[2], after(rn[3], og_y))
    col = jnp.arange(WAYS * 16, dtype=jnp.int32)
    col_blk = (col // 16) * 5 + (col % 16) // 2
    col_ok = (col % 16) < 10
    col_par = jnp.where(col_ok, all_par[jnp.minimum(col_blk, TREE_BLK - 1)], -2)
    row = jnp.arange(128, dtype=jnp.int32)
    pick = (
        (row[:, None] < 10)
        & (col_par[None, :] == c_id * 5 + row[:, None] // 2)
        & (col[None, :] % 2 == row[:, None] % 2)
    ).astype(f32)
    dpacks = (5 * ch3 // 2, 128)
    dz, q0, q1, q2, q3, ib = call(
        dz_kernel,
        [((nb, ch3, B), bf16)] + [(dpacks, bf16)] * 4 + [((ch3, 1), f32)],
        6,
        [pltpu.VMEM((WAYS * 16, ch3), f32), pltpu.VMEM((ch3, 128), f32), pltpu.VMEM((WAYS,) + dpacks, bf16)],
    )(sc, dzo, *rn, pick)
    qn = ten((q0, q1, q2, q3))
    if pair:
        mine, theirs, sums1 = call(
            in_grad_kernel,
            [((ch3, d_part), f32), ((ch3, d_part), bf16), ((8, width), f32)],
            6,
        )(after(sc, mg_got[1], og_got[0]), dz, a1, wt, ib, norm1_gain, norm1_bias)
        ih = mine + swap_y(theirs).astype(f32)
    else:
        ig, sums1 = call(in_grad_kernel, [((ch3, width), f32), ((8, width), f32)], 6)(sc, dz, a1, wt, ib, norm1_gain, norm1_bias)
        ih = lax.psum_scatter(ig, "shards", scatter_dimension=1, tiled=True)

    fs = sum_context(f0, f1, f2, f3, dy)
    filt, fo_g = call(functools.partial(filter_back_kernel, bands), [((FILT_ROWS, fw), f32), ((cs, fw), f32)], 5, [pltpu.VMEM((ne, STEP), f32)])(
        after(sc, dz), dtaps, fin, fc, fo_t, filt_mid
    )
    n_col = 8 * (-(-ch3 // 128))
    n_all = 64 + FILT_ROWS + 16
    (small,) = call(pack_kernel, [((n_all + n_col + 8 + ch, 128), f32)], 8, [pltpu.VMEM((128, ch3), f32)])(
        sc, sums1, sums2, ub, filt, fo_g, cg, ib, skip_g
    )
    ctx_small = tuple(swap(small, "context", k) for k in (1, 2, 3))

    def total(own, got):
        return ((own.astype(f32) + got[0].astype(f32)) + (got[1].astype(f32) + got[2].astype(f32))).astype(bf16)

    m0 = total(mg_sum[0], after(tuple(mg_got), qn[2]))
    m1, m2 = swap(m0, "context", 1), swap(m0, "context", 2)
    ih_core = swap(ih.astype(bf16), "context", 1)

    ih = ih + ih_core.astype(f32)
    far = swap(ih.astype(bf16), "context", 2)
    small = (small + ctx_small[0]) + (ctx_small[1] + ctx_small[2])
    small_y = swap_y(small) if pair else lax.psum(small, "shards")
    oh = total(og_sum[0], after(og_got, qn[2]))[0].astype(f32)
    oh = oh + swap(oh.astype(bf16), "context", 1).astype(f32)
    oh_far = swap(oh.astype(bf16), "context", 2)
    part, w2 = call(
        norm1_part_kernel, [(sh, f32), ((ch3, width), bf16)], 8, [pltpu.VMEM((2, ch3, width), bf16)]
    )(sc, qn[0], qn[1], qn[3], wt, wa, wb, wc, wd)
    (tokens_grad,) = call(norm1_kernel, [(sh, bf16)], 6, [pltpu.VMEM(sh, f32)])(
        sc, part, qn[2], w2, tok_share, dr1, norm1_gain
    )

    done = tokens_grad
    fs, m1, m2, far, oh_far, small_y = after((fs, m1, m2, far, oh_far, small_y), done)
    small = small + small_y if pair else small_y
    late = small[n_all:]
    early = small[:n_all]
    early = (early + swap(early, "tensor", 1)) + (swap(early, "tensor", 2) + swap(early, "tensor", 3))
    out_grad = oh + oh_far.astype(f32)
    m3 = swap(m2, "context", 1)
    up_grad, down_grad = call(
        matrices_kernel, [((d_part, ffq), f32), ((ffq, d_part), f32)], 4, [pltpu.VMEM((ffq, d_part), f32)]
    )(sc, m0, m1, m2, m3)
    in_grad = jnp.transpose((ih + far.astype(f32)).reshape(3, ch, d_part), (2, 0, 1))
    (layer_out,) = call(layer_out_kernel, [(sh, bf16)], 5)(sc, r1, *fs, down_bias)

    first = early[64 + FILT_ROWS :]

    def row_at(x, at):
        return x[at : at + 8].reshape(-1)[:width]

    hid = early[32:64].reshape(WAYS, WAYS, 256)[:, :, :ffs]
    up_bias_grad = lax.dynamic_index_in_dim(hid, t_id, 1, keepdims=False).reshape(ffq)
    fil = early[64 : 64 + FILT_ROWS, :fw]
    fo_own = lax.dynamic_slice_in_dim(late[8 + n_col :, :fw].T, s_id * filt_out.shape[0], filt_out.shape[0], 0)
    colsum = late[:n_col].reshape(n_col // 8, 8, 128).transpose(1, 0, 2).reshape(8, -1)[:, :ch3]
    skip_sum = late[n_col : 8 + n_col].reshape(-1)[:ch]
    conv_all = colsum.reshape(8, 3, ch)
    return (
        layer_out,
        tokens_grad,
        row_at(first, 0),
        row_at(first, 8),
        in_grad,
        conv_all[4],
        conv_all[1:4],
        conv_all[0],
        jnp.concatenate([fil[fw + n_in - 1 : fw + n_in], fil[fw : fw + n_in - 1]]),
        fil[fw + ne],
        fil[:fw],
        fil[fw + ne + 1],
        fil[fw + ne + 2],
        fo_own,
        skip_sum,
        out_grad,
        row_at(early, 16),
        row_at(early, 0),
        row_at(early, 8),
        up_grad,
        up_bias_grad,
        down_grad,
        row_at(early, 24),
    )


def solution(mesh):
    return jax.shard_map(
        functools.partial(body, mesh.shape["shards"]),
        mesh=mesh,
        in_specs=(
            P(("shards", "context"), None),
            P("shards", None),
            P(),
            P(),
            P("shards", None, "tensor"),
            P(None, "tensor"),
            P(None, None, "tensor"),
            P(None, "tensor"),
            P(),
            P(),
            P(),
            P(),
            P(),
            P("shards", "tensor"),
            P("tensor"),
            P("tensor", "shards"),
            P(),
            P(),
            P(),
            P("shards", "tensor"),
            P("tensor"),
            P("tensor", "shards"),
            P(),
            P(("shards", "context"), None),
        ),
        out_specs=(
            P(("shards", "context", "tensor"), None),
            P(("shards", "context", "tensor"), None),
            P(),
            P(),
            P("shards", None, "tensor"),
            P(None, "tensor"),
            P(None, None, "tensor"),
            P(None, "tensor"),
            P(),
            P(),
            P(),
            P(),
            P(),
            P("shards", "tensor"),
            P("tensor"),
            P("tensor", "shards"),
            P(),
            P(),
            P(),
            P("shards", "tensor"),
            P("tensor"),
            P("tensor", "shards"),
            P(),
        ),
        check_vma=False,
    )
```
